32 devices in a mesh: group: 2 (over y), tile: 4 (over z), strip: 2 (over x), sub: 2 (over core).
Axes of the slice: x: 2, y: 2, z: 4, core: 2. Of those that a mesh axis runs over, the one named last changes fastest.
Arguments:
- right_side: float32 [32, 128, 1024], P('group', 'tile', ('strip', 'sub')), parts along dimension 0, may hold values from -24 to 24
- horiz_coef: float32 [256, 1024], P(('group', 'tile'), ('strip', 'sub')), parts along dimension 0, may hold values from 8 to 32
- vert_coef: float32 [256, 1024], P(('group', 'tile'), ('strip', 'sub')), parts along dimension 0, may hold values from 1 to 8
- panel_owner: int32 [16384, 1], P(('group', 'tile', 'strip', 'sub')), parts along dimension 0, may hold values from 0 to 3; in each aligned block of 512 rows (0 to 511, 512 to 1023, ...) at most 384 rows name the same one
- panel_cell: int32 [16384], P(('group', 'tile', 'strip', 'sub')), parts along dimension 0, may hold values from 0 to 8191
- panel_pressure: float32 [16384], P(('group', 'tile', 'strip', 'sub')), parts along dimension 0, may hold values from -48 to 48
Outputs:
- potential: float32 [32, 128, 1024], P('group', 'tile', ('strip', 'sub')), parts along dimension 0
- residual: float32 [32, 128, 1024], P('group', 'tile', ('strip', 'sub')), parts along dimension 0
The draws below stay inside these ranges and needn't reach their ends.
There are 2 independent parts, one for each index of `group`. The reference program is written for one: setup_inputs(seed, part) draws one part's arguments, and reference() takes and returns one part's arrays. A program takes and returns all parts, laid end to end along the dimension named above; each array names one. Nothing has to cross between parts.
Inputs may be any that keep to these rules, and one draw needn't show every extreme that they name: `panel_owner`: among the 512 panels of one device at most 384 name one owner; some device reaches 384 in every draw.
All inputs are finite; a program needn't handle non-finite values.
Results may differ from the reference program's by a relative error of at most 0.00015.
Values sent between devices are 32-bit elements; how exact they have to be, the bound alone decides.
No kernel may reach another device: no remote copies, remote signals or barrier semaphores. Data moves between devices by JAX's collectives and lax.ppermute only.
A program may use at most 128 MiB of HBM per device.

```python
import math
import jax
import jax.numpy as jnp
import numpy as np
from jax import lax

NZ = 16
CX = 32
CY = 256
LEVELS = 3
SWEEPS = 2
COARSE = 8
PAN_DEV = 512
TILES = 4
CAP = 384
NX = 128
NY = 1024
PANELS = 8192


def touch_ends(result, rng, least, top_value):
    longest = result.shape.index(max(result.shape))
    spots = []
    for shift in (0, 1):
        where = [jax.random.randint(jax.random.fold_in(rng, axis), (), 0, length) for axis, length in enumerate(result.shape)]
        where[longest] = (where[longest] + shift) % result.shape[longest]
        spots.append(tuple(where))
    return result.at[spots[0]].set(least).at[spots[1]].set(top_value)


def level_of(rng, extent, split, least, high):
    loudness, own = 1.0, jax.random.fold_in(rng, 6)
    for position, blocks in split:
        heights = jnp.exp(jax.random.uniform(jax.random.fold_in(own, position), (blocks,), jnp.float32, least / len(split), high / len(split)))
        loudness = loudness * jnp.repeat(heights, extent[position] // blocks).reshape([-1 if axis == position else 1 for axis in range(len(extent))])
    return loudness


def routed_block(key, own, number, rows, number_of, top, reach, lean):
    ranking = jax.random.permutation(key, number_of)
    packed, usual = load_shares(number_of, rows * top, reach, lean, True), load_shares(number_of, rows * top, reach, lean, False)
    places = jnp.arange(number_of)

    def named(sizes, offset_by):
        used = int((sizes > 0).sum())
        fixed = max(1, used // 4)
        passed = fixed + (places - fixed + offset_by * (used - fixed)) % max(1, number_of - fixed)
        return jnp.zeros((number_of,), jnp.int32).at[ranking[jnp.where(places < fixed, places, passed)]].set(jnp.asarray(sizes, jnp.int32))

    sizes = jnp.where(number % 4 == 0, named(packed, number // 4), named(usual, number - number // 4 - 1))
    mixed = jax.random.permutation(jax.random.fold_in(own, 3), number_of)
    source_of, receiver = mixed[0:number_of // 2 * 2:2], mixed[1:number_of // 2 * 2:2]
    slack = jnp.minimum(sizes[source_of] - 1, reach - sizes[receiver]) // 2
    slack = jnp.where((source_of == ranking[0]) | (receiver == ranking[0]) | (sizes[receiver] == 0), 0, jnp.maximum(slack, 0))
    passed = jax.random.randint(jax.random.fold_in(own, 4), (number_of // 2,), 0, 1 << 20) % (slack + 1)
    sizes = sizes.at[source_of].add(-passed).at[receiver].add(passed)
    items = jnp.searchsorted(jnp.cumsum(sizes), jnp.arange(rows * top), side="right").astype(jnp.int32)
    listing = items.reshape(top, rows).T
    listing = listing[jax.random.permutation(jax.random.fold_in(own, 1), rows)]
    offset_by = jax.random.randint(jax.random.fold_in(own, 2), (rows, 1), 0, top)
    return jnp.take_along_axis(listing, (jnp.arange(top)[None, :] + offset_by) % top, axis=1)


def load_shares(number_of, total, most, skew, full):
    loads = [(1 << 20) // math.isqrt(standing ** skew) + 1 for standing in range(1, number_of + 1)]
    largest = most if full else min(most, max(-(-total // number_of), total * loads[0] // sum(loads)))
    least = 1 if total - largest >= number_of - 1 else 0
    holding, surplus = [largest] + [least] * (number_of - 1), total - largest - least * (number_of - 1)
    while surplus > 0:
        free = [i for i in range(1, number_of) if holding[i] < largest] or [i for i in range(1, number_of) if holding[i] < most]
        whole, left = sum([loads[i] for i in free]), surplus
        for i in free:
            extra = min(most - holding[i], max(1, left * loads[i] // whole), surplus)
            holding[i] = holding[i] + extra
            surplus = surplus - extra
    return np.array(holding)


def noise(rng, shape, deviation, reach, pieces=(), kind=jnp.bfloat16):
    drawn = deviation * jax.random.normal(rng, shape, jnp.float32)
    if pieces:
        drawn = drawn * level_of(rng, shape, pieces, -0.22, 0.18)
    return jnp.clip(drawn, -reach, reach).astype(kind)


def setup_inputs(seed: int = 0, part: int = 0) -> dict:
    seeds = jax.random.split(jax.random.key(seed), 7)
    part_keys = jax.random.split(jax.random.fold_in(seeds[6], part), 7)
    right_side = noise(part_keys[0], (NZ, NX, NY), 4.0, 24.0, ((1, 4), (2, 4)), jnp.float32)
    horiz_coef = jnp.clip(jnp.exp(math.log(32.0) - 1.3862944 * jax.random.uniform(part_keys[1], (NX, NY), jnp.float32) ** level_of(part_keys[1], (NX, NY), ((0, 4), (1, 4)), -0.2, 0.2)), 8.0, 32.0)
    vert_coef = jnp.clip(jnp.exp(math.log(8.0) - 2.0794415 * jax.random.uniform(part_keys[2], (NX, NY), jnp.float32) ** level_of(part_keys[2], (NX, NY), ((0, 4), (1, 4)), -0.2, 0.2)), 1.0, 8.0)
    panel_owner_keys = jax.random.split(jax.random.fold_in(part_keys[3], 1), PANELS // PAN_DEV)
    panel_owner_turns = jax.random.permutation(jax.random.fold_in(part_keys[3], 3), PANELS // PAN_DEV)
    panel_owner = jax.vmap(lambda own, number: routed_block(jax.random.fold_in(part_keys[3], 2), own, number, PAN_DEV, TILES, 1, CAP, 2))(panel_owner_keys, panel_owner_turns).reshape((PANELS, 1))
    panel_cell = touch_ends(jax.random.randint(part_keys[4], (PANELS,), 0, CX * CY), jax.random.fold_in(part_keys[4], 1), 0, (CX * CY) - 1).astype(jnp.int32)
    panel_pressure = noise(part_keys[5], (PANELS,), 8.0, 48.0, ((0, 16),), jnp.float32)
    return {"right_side": right_side, "horiz_coef": horiz_coef, "vert_coef": vert_coef, "panel_owner": panel_owner, "panel_cell": panel_cell, "panel_pressure": panel_pressure}


OMEGA = 0.8


def diag_of(kh, kv, scale, depth):
    lower = (lax.iota(jnp.int32, depth) > 0).astype(kh.dtype)
    return 4.0 * scale * kh[None] + kv[None] * (1.0 + lower[:, None, None])


def apply_level(field, kh, kv, scale):
    padded = jnp.pad(field, ((0, 0), (1, 1), (1, 1)))
    hsum = padded[:, 2:, 1:-1] + padded[:, :-2, 1:-1] + padded[:, 1:-1, 2:] + padded[:, 1:-1, :-2]
    zeros = jnp.zeros_like(field[:1])
    above = jnp.concatenate([field[1:], zeros], 0)
    below = jnp.concatenate([zeros, field[:-1]], 0)
    diag = diag_of(kh, kv, scale, field.shape[0])
    return diag * field - scale * kh[None] * hsum - kv[None] * (above + below)


def relax_from(field, source, kh, kv, scale, count):
    diag = diag_of(kh, kv, scale, source.shape[0])
    for step in range(count):
        field = field + OMEGA * (source - apply_level(field, kh, kv, scale)) / diag
    return field


def coarsen(field):
    shape = field.shape
    return field.reshape(shape[:-2] + (shape[-2] // 2, 2, shape[-1] // 2, 2)).mean(axis=(-3, -1))


def cycle(source, kh, kv, level):
    scale = 0.25 ** level
    diag = diag_of(kh, kv, scale, source.shape[0])
    first = OMEGA * source / diag
    if level == LEVELS - 1:
        return relax_from(first, source, kh, kv, scale, COARSE - 1)
    field = relax_from(first, source, kh, kv, scale, SWEEPS - 1)
    remain = source - apply_level(field, kh, kv, scale)
    correction = cycle(coarsen(remain), coarsen(kh), coarsen(kv), level + 1)
    field = field + jnp.repeat(jnp.repeat(correction, 2, axis=1), 2, axis=2)
    return relax_from(field, source, kh, kv, scale, SWEEPS)


def reference(right_side, horiz_coef, vert_coef, panel_owner, panel_cell, panel_pressure):
    block = jnp.arange(PANELS, dtype=jnp.int32) // PAN_DEV
    column = block % (NY // CY)
    gx = panel_owner[:, 0] * CX + panel_cell // CY
    gy = column * CY + panel_cell % CY
    forcing = jnp.zeros((NX, NY), jnp.float32).at[gx, gy].add(panel_pressure)
    source = right_side.at[NZ - 1].add(forcing)
    potential = cycle(source, horiz_coef, vert_coef, 0)
    residual = source - apply_level(potential, horiz_coef, vert_coef, 1.0)
    return potential, residual
```

```python
import jax
import jax.numpy as jnp
import numpy as np
from jax import lax
from jax.experimental import pallas as pl
from jax.experimental.pallas import tpu as pltpu

COARSE = 8
OMEGA = 0.8

HX = 12
HX2 = 9
HY = 42
SLABS = 3


def edge_pairs(count, odd):
    out = []
    for i in range(1 if odd else 0, count - 1, 2):
        out += [(i, i + 1), (i + 1, i)]
    return out


def lane_maps(cols):
    one = -np.ones(cols + 128, np.int64)
    half = cols // 2
    one[:cols] = np.arange(cols) // 2
    one[cols : cols + HY] = half + np.arange(HY) // 2
    one[cols + 128 - HY :] = 2 * half - HY // 2 + np.arange(HY) // 2
    h1 = HY // 2
    two = -np.ones(2 * half, np.int64)
    quarter = half // 2
    two[:half] = np.arange(half) // 2
    two[half : half + h1 - 1] = quarter + np.arange(h1 - 1) // 2
    two[2 * half - h1 + 1 :] = 2 * quarter - (h1 - 1) // 2 + np.arange(h1 - 1) // 2
    return one, two


def selection(lanes, width):
    return (lanes[:, None] == np.arange(width)[None, :]).astype(np.float32)


def exact_dot(left, right):
    high = left.astype(jnp.bfloat16)
    rest = left - high.astype(jnp.float32)
    mid = rest.astype(jnp.bfloat16)
    low = (rest - mid.astype(jnp.float32)).astype(jnp.bfloat16)
    dot = lambda part: jnp.dot(part, right, preferred_element_type=jnp.float32)
    return dot(high) + dot(mid) + dot(low)


def neighbours(u):
    rows, lanes = u.shape
    return (
        pltpu.roll(u, 1, 0)
        + pltpu.roll(u, rows - 1, 0)
        + pltpu.roll(u, 1, 1)
        + pltpu.roll(u, lanes - 1, 1)
    )


def weights(kh, kv, scale, inside, w_ref, a_ref, b_ref):
    for i, layers in enumerate((1.0, 2.0)):
        diag = 4.0 * scale * kh + layers * kv
        w = jnp.where(inside, OMEGA / jnp.where(inside, diag, 1.0), 0.0)
        if w_ref is not None:
            w_ref[i] = w
        a_ref[i] = w * (scale * kh)
        b_ref[i] = w * kv


def sweep(src, dst, wb, a_ref, b_ref, depth):
    def layer(z, c):
        i = jnp.minimum(z, 1)
        u = src[z + 1]
        dst[z + 1] = (
            (1.0 - OMEGA) * u
            + wb[z]
            + a_ref[i] * neighbours(u)
            + b_ref[i] * (src[z] + src[z + 2])
        )
        return c

    lax.fori_loop(0, depth, layer, 0)


def residual_of(src, z, b, kh, kv, scale):
    layers = jnp.where(z == 0, 1.0, 2.0)
    u = src[z + 1]
    return b + (scale * kh) * (neighbours(u) - 4.0 * u) + kv * (src[z] + src[z + 2] - layers * u)


def blocks_out(ref, l, x):
    for j in range(ref.shape[1]):
        ref[l, j, 0 : x.shape[0], :] = x[:, 128 * j : 128 * (j + 1)]


def blocks_in(ref, l):
    return jnp.concatenate([ref[l, j] for j in range(ref.shape[1])], 1)


def rows_doubled(ref, l, part):
    n = part.shape[0]
    for j in range(ref.shape[1]):
        for s in (0, 1):
            ref[l, j, pl.ds(s, n, stride=2), :] = part[:, 128 * j : 128 * (j + 1)]


def pack_rows_kernel(rs, kh, kv, a_out, b_out):
    depth, rows, _ = rs.shape
    even = lax.axis_index("tile") % 2 == 0

    def layer(l):
        return rs[l] if l < depth else (kh[...] if l == depth else kv[...])

    count = depth + 2
    half = count // 2

    def first(out):
        for l in range(count):
            x = layer(l)
            out[l] = x[0:8]
            out[count + l % half, 4 * (l // half) : 4 * (l // half) + 4, :] = x[8:HX]

    def last(out):
        for l in range(count):
            x = layer(l)
            out[l] = x[rows - 8 : rows]
            out[count + l % half, 4 * (l // half) : 4 * (l // half) + 4, :] = x[rows - HX : rows - 8]

    @pl.when(even)
    def _():
        last(a_out)
        first(b_out)

    @pl.when(jnp.logical_not(even))
    def _():
        first(a_out)
        last(b_out)


def forcing_kernel(rs, kh, kv, xa, xb, panels, ext, sub_out, strip_out):
    depth, rows, cols = rs.shape
    count = depth + 2
    half = count // 2
    tile = lax.axis_index("tile")
    even = tile % 2 == 0
    high = rows + HX

    def upper(x):
        for l in range(count):
            ext[l, 0:4, :] = x[count + l % half, 4 * (l // half) : 4 * (l // half) + 4, :]
            ext[l, 4:HX, :] = x[l]

    def lower(x):
        for l in range(count):
            ext[l, high : high + 8, :] = x[l]
            ext[l, high + 8 : high + HX, :] = x[count + l % half, 4 * (l // half) : 4 * (l // half) + 4, :]

    @pl.when(even)
    def _():
        lower(xa)
        upper(xb)

    @pl.when(jnp.logical_not(even))
    def _():
        upper(xa)
        lower(xb)

    for l in range(depth):
        ext[l, HX:high, :] = rs[l]
    ext[depth, HX:high, :] = kh[...]
    ext[depth + 1, HX:high, :] = kv[...]

    span = rows + 2 * HX
    total = jnp.zeros((span, cols), jnp.float32)
    left, right = [], []
    for g in range(panels.shape[0]):
        for k in range(4):
            code = panels[g, k : k + 1, :].astype(jnp.int32)
            value = panels[g, 4 + k : 5 + k, :]
            row = code // cols - (tile * rows - HX)
            col = code % cols
            hit = row == lax.broadcasted_iota(jnp.int32, (span, 128), 0)
            left.append(jnp.where(hit, value, 0.0))
            right.append(
                jnp.where(col == lax.broadcasted_iota(jnp.int32, (cols, 128), 0), 1.0, 0.0).astype(jnp.bfloat16)
            )
    left = jnp.concatenate(left, 1)
    right = jnp.concatenate(right, 1)
    high_part = left.astype(jnp.bfloat16)
    rest = left - high_part.astype(jnp.float32)
    mid_part = rest.astype(jnp.bfloat16)
    low_part = (rest - mid_part.astype(jnp.float32)).astype(jnp.bfloat16)
    for part in (high_part, mid_part, low_part):
        total = total + lax.dot_general(
            part, right, (((1,), (1,)), ((), ())), preferred_element_type=jnp.float32
        )
    ext[depth - 1] = ext[depth - 1] + total

    y = lax.axis_index("strip") * lax.axis_size("sub") + lax.axis_index("sub")
    y_even = y % 2 == 0
    lane = lax.broadcasted_iota(jnp.int32, (span, 128), 1)

    def slab(g, at_right):
        out = jnp.zeros((span, 128), jnp.float32)
        for k in range(SLABS):
            if at_right:
                x = pltpu.roll(ext[SLABS * g + k, :, cols - 128 : cols], (HY + HY * k) % 128, 1)
            else:
                x = ext[SLABS * g + k, :, 0:128]
                x = pltpu.roll(x, HY * k, 1) if k else x
            out = jnp.where((lane >= HY * k) & (lane < HY * (k + 1)), x, out)
        return out

    for g in range(count // SLABS):
        to_right = slab(g, True)
        to_left = slab(g, False)
        sub_out[g] = jnp.where(y_even, to_right, to_left)
        strip_out[g] = jnp.where(y_even, to_left, to_right)


def down_kernel(
    ext, ysub, ystrip, c1, c2,
    b_out, k_out, u_out, k1_out, b1_out, u1_out, c_out, a_msg, b_msg,
    b0, u0, u0n, r0, w0, al0, be0, w1, al1, be1, u1, u1n, r1,
):
    depth = ext.shape[0] - 2
    span, cols = ext.shape[1], ext.shape[2]
    count = depth + 2
    tiles = lax.axis_size("tile")
    tile = lax.axis_index("tile")
    y_count = lax.axis_size("strip") * lax.axis_size("sub")
    y = lax.axis_index("strip") * lax.axis_size("sub") + lax.axis_index("sub")
    y_even = y % 2 == 0
    rows = span - 2 * HX
    lane = lax.broadcasted_iota(jnp.int32, (span, 128), 1)

    for g in range(count // SLABS):
        from_right = jnp.where(y_even, ysub[g], ystrip[g])
        from_left = jnp.where(y_even, ystrip[g], ysub[g])
        for k in range(SLABS):
            l = SLABS * g + k
            right = pltpu.roll(from_right, 128 - HY * k, 1) if k else from_right
            left = pltpu.roll(from_left, 128 - HY - HY * k, 1) if (128 - HY - HY * k) % 128 else from_left
            b0[l, :, 0:cols] = ext[l]
            b0[l, :, cols : cols + 128] = jnp.where(lane < HY, right, jnp.where(lane >= 128 - HY, left, 0.0))

    def inside_of(shape, first_row, row_end, own, halo):
        row = first_row + lax.broadcasted_iota(jnp.int32, shape, 0)
        column = lax.broadcasted_iota(jnp.int32, shape, 1)
        right = (column >= own) & (column < own + halo) & (y < y_count - 1)
        left = (column >= shape[1] - halo) & (y > 0)
        return (row >= 0) & (row < row_end) & ((column < own) | right | left)

    lanes = cols + 128
    kh, kv = b0[depth], b0[depth + 1]
    weights(kh, kv, 1.0, inside_of((span, lanes), tile * rows - HX, tiles * rows, cols, HY), w0, al0, be0)
    zero = jnp.zeros((span, lanes), jnp.float32)
    u0[0] = zero
    u0[depth + 1] = zero
    u0n[0] = zero
    u0n[depth + 1] = zero

    def first(z, c):
        u0[z + 1] = w0[jnp.minimum(z, 1)] * b0[z]
        return c

    lax.fori_loop(0, depth, first, 0)
    sweep(u0, u0n, u0.at[pl.ds(1, depth)], al0, be0, depth)

    low, top = 8, span - 8
    pad = r0.shape[2] - span
    for l in range(count):
        for j in range(r0.shape[1]):
            r0[l, j, span : span + pad, :] = jnp.zeros((pad, 128), jnp.float32)
    blocks_out(r0, depth, kh)
    blocks_out(r0, depth + 1, kv)
    k_out[0] = kh[low:top]
    k_out[1] = kv[low:top]

    def rest(z, c):
        b = b0[z]
        blocks_out(r0, z, residual_of(u0n, z, b, b0[depth], b0[depth + 1], 1.0))
        b_out[z] = b[low:top]
        u_out[z] = u0n[z + 1][low:top]
        return c

    lax.fori_loop(0, depth, rest, 0)

    def coarse_rows(ref, l, n):
        return jnp.concatenate(
            [
                ref[l, j, pl.ds(0, n, stride=2), :] + ref[l, j, pl.ds(1, n, stride=2), :]
                for j in range(ref.shape[1])
            ],
            1,
        )

    span1 = r0.shape[2] // 2
    half = cols
    pairs = jnp.concatenate([coarse_rows(r0, l, span1) for l in range(count)], 0)
    b1 = exact_dot(pairs, c1[...]).reshape(count, span1, half)
    b1_out[...] = b1[0:depth]
    k1_out[...] = b1[depth:]
    kh1, kv1 = k1_out[0], k1_out[1]
    weights(
        kh1, kv1, 0.25,
        inside_of((span1, half), tile * (rows // 2) - HX // 2, tiles * (rows // 2), cols // 2, HY // 2),
        w1, al1, be1,
    )
    zero1 = jnp.zeros((span1, half), jnp.float32)
    u1[0] = zero1
    u1[depth + 1] = zero1
    u1n[0] = zero1
    u1n[depth + 1] = zero1

    def first1(z, c):
        u1[z + 1] = w1[jnp.minimum(z, 1)] * b1_out[z]
        return c

    lax.fori_loop(0, depth, first1, 0)
    sweep(u1, u1n, u1.at[pl.ds(1, depth)], al1, be1, depth)

    def rest1(z, c):
        blocks_out(r1, z, residual_of(u1n, z, b1_out[z], k1_out[0], k1_out[1], 0.25))
        u1_out[z] = u1n[z + 1]
        return c

    lax.fori_loop(0, depth, rest1, 0)
    blocks_out(r1, depth, kh1)
    blocks_out(r1, depth + 1, kv1)
    span2 = span1 // 2
    pairs = jnp.concatenate([coarse_rows(r1, l, span2) for l in range(count)], 0)
    b2 = exact_dot(pairs, c2[...]).reshape(count, span2, cols // 2)
    c_out[...] = b2

    own2 = HX // 4
    rows2 = rows // 4
    even = tile % 2 == 0

    def send(out, start):
        for l in range(count):
            out[count + l // 8, l % 8 : l % 8 + 1, :] = c_out[l, start : start + 1, :]
            out[l] = c_out[l, start + 1 : start + HX2, :]

    @pl.when(even)
    def _():
        send(a_msg, own2 - 1)
        send(b_msg, own2)

    @pl.when(jnp.logical_not(even))
    def _():
        send(a_msg, own2)
        send(b_msg, own2 - 1)


def up_kernel(
    c_in, xa, xb, b0, k0, u0, k1, b1, u1, p1, p2,
    potential, residual,
    b2, w2, al2, be2, wb2, u2, u2n, w1, al1, be1, wb1, f1, f1n, w0, al0, be0, wb0, f0, f0n, e1, e0,
):
    count = c_in.shape[0]
    depth = count - 2
    cols = potential.shape[2]
    rows = potential.shape[1]
    rows2 = rows // 4
    tiles = lax.axis_size("tile")
    tile = lax.axis_index("tile")
    y_count = lax.axis_size("strip") * lax.axis_size("sub")
    y = lax.axis_index("strip") * lax.axis_size("sub") + lax.axis_index("sub")
    even = tile % 2 == 0
    own2 = HX // 4
    span2 = b2.shape[1]
    end2 = rows2 + 2 * HX2

    def inside_of(shape, first_row, row_end, own, halo):
        row = first_row + lax.broadcasted_iota(jnp.int32, shape, 0)
        column = lax.broadcasted_iota(jnp.int32, shape, 1)
        right = (column >= own) & (column < own + halo) & (y < y_count - 1)
        left = (column >= shape[1] - halo) & (y > 0)
        return (row >= 0) & (row < row_end) & ((column < own) | right | left)

    def put(x, start):
        for l in range(count):
            b2[l, start : start + 1, :] = x[count + l // 8, l % 8 : l % 8 + 1, :]
            b2[l, start + 1 : start + HX2, :] = x[l]

    @pl.when(even)
    def _():
        put(xa, HX2 + rows2)
        put(xb, 0)

    @pl.when(jnp.logical_not(even))
    def _():
        put(xa, 0)
        put(xb, HX2 + rows2)

    lanes2 = b2.shape[2]
    for l in range(count):
        b2[l, HX2 : HX2 + rows2, :] = c_in[l, own2 : own2 + rows2, :]
        b2[l, end2:span2, :] = jnp.zeros((span2 - end2, lanes2), jnp.float32)
    row = lax.broadcasted_iota(jnp.int32, (span2, lanes2), 0)
    inside2 = inside_of((span2, lanes2), tile * rows2 - HX2, tiles * rows2, cols // 4, (HY - 2) // 4)
    weights(b2[depth], b2[depth + 1], 0.0625, inside2 & (row < end2), w2, al2, be2)

    def zero_ends(ref):
        z = jnp.zeros(ref.shape[1:], jnp.float32)
        ref[0] = z
        ref[depth + 1] = z

    for ref in (u2, u2n, f1, f1n, f0, f0n):
        zero_ends(ref)

    def first2(z, c):
        v = w2[jnp.minimum(z, 1)] * b2[z]
        wb2[z] = v
        u2[z + 1] = v
        return c

    lax.fori_loop(0, depth, first2, 0)
    src, dst = u2, u2n
    for _ in range(COARSE - 1):
        sweep(src, dst, wb2, al2, be2, depth)
        src, dst = dst, src

    span1, lanes1 = u1.shape[1], u1.shape[2]
    kh1, kv1 = k1[0], k1[1]
    weights(
        kh1, kv1, 0.25,
        inside_of((span1, lanes1), tile * (rows // 2) - HX // 2, tiles * (rows // 2), cols // 2, HY // 2),
        w1, al1, be1,
    )
    off2 = HX2 - own2
    coarse = jnp.concatenate([src[z + 1][off2 : off2 + span1 // 2] for z in range(depth)], 0)
    fine = exact_dot(coarse, p2[...])
    for z in range(depth):
        rows_doubled(e1, z, fine[z * (span1 // 2) : (z + 1) * (span1 // 2)])

    def first1(z, c):
        f1[z + 1] = u1[z] + blocks_in(e1, z)
        wb1[z] = w1[jnp.minimum(z, 1)] * b1[z]
        return c

    lax.fori_loop(0, depth, first1, 0)
    sweep(f1, f1n, wb1, al1, be1, depth)
    sweep(f1n, f1, wb1, al1, be1, depth)

    span0, lanes0 = b0.shape[1], b0.shape[2]
    above = (span0 - rows) // 2
    weights(
        k0[0], k0[1], 1.0,
        inside_of((span0, lanes0), tile * rows - above, tiles * rows, cols, HY),
        w0, al0, be0,
    )
    off1 = (HX - above) // 2
    fine = exact_dot(f1[pl.ds(1, depth)].reshape(depth * span1, lanes1), p1[...])
    for z in range(depth):
        rows_doubled(e0, z, fine[z * span1 + off1 : z * span1 + off1 + span0 // 2])

    def first0(z, c):
        f0[z + 1] = u0[z] + blocks_in(e0, z)
        wb0[z] = w0[jnp.minimum(z, 1)] * b0[z]
        return c

    lax.fori_loop(0, depth, first0, 0)
    sweep(f0, f0n, wb0, al0, be0, depth)
    sweep(f0n, f0, wb0, al0, be0, depth)

    def last(z, c):
        r = residual_of(f0, z, b0[z], k0[0], k0[1], 1.0)
        residual[z] = r[above : above + rows, 0:cols]
        potential[z] = f0[z + 1][above : above + rows, 0:cols]
        return c

    lax.fori_loop(0, depth, last, 0)


VM = pl.BlockSpec(memory_space=pltpu.VMEM)


def call(kernel, outs, scratch, *args):
    f32 = lambda shape: jax.ShapeDtypeStruct(shape, jnp.float32)
    return pl.pallas_call(
        kernel,
        out_shape=[f32(s) for s in outs],
        in_specs=[VM] * len(args),
        out_specs=[VM] * len(outs),
        scratch_shapes=[pltpu.VMEM(s, jnp.float32) for s in scratch],
        compiler_params=pltpu.CompilerParams(vmem_limit_bytes=40 << 20),
    )(*args)


def body(right_side, horiz_coef, vert_coef, panel_owner, panel_cell, panel_pressure):
    depth, rows, cols = right_side.shape
    tiles = lax.axis_size("tile")
    y_axes = ("strip", "sub")
    y_count = lax.axis_size("strip") * lax.axis_size("sub")
    count = depth + 2
    span = rows + 2 * HX
    one, two = lane_maps(cols)
    c1 = jnp.asarray(0.25 * selection(one, cols), jnp.bfloat16)
    c2 = jnp.asarray(0.25 * selection(two, cols // 2), jnp.bfloat16)
    p1 = jnp.asarray(selection(one, cols).T, jnp.bfloat16)
    p2 = jnp.asarray(selection(two, cols // 2).T, jnp.bfloat16)

    code = (panel_owner[:, 0] * (rows * cols) + panel_cell).astype(jnp.float32)
    panels = jnp.concatenate([code.reshape(4, -1), panel_pressure.reshape(4, -1)], 0)[None]
    step = 1
    while step < tiles:
        swap = [(i, i ^ step) for i in range(tiles)]
        panels = jnp.concatenate([panels, lax.ppermute(panels, "tile", swap)], 0)
        step *= 2

    message = (count + count // 2, 8, cols)
    a, b = call(pack_rows_kernel, [message] * 2, [], right_side, horiz_coef, vert_coef)
    a = lax.ppermute(a, "tile", edge_pairs(tiles, False))
    b = lax.ppermute(b, "tile", edge_pairs(tiles, True))

    slabs = (count // SLABS, span, 128)
    ext, sub, strip = call(
        forcing_kernel, [(count, span, cols), slabs, slabs], [],
        right_side, horiz_coef, vert_coef, a, b, panels,
    )
    sub = lax.ppermute(sub, y_axes, edge_pairs(y_count, False))
    strip = lax.ppermute(strip, y_axes, edge_pairs(y_count, True))

    lanes = cols + 128
    small = span - 16
    span1 = (span + 8) // 2
    span2 = span1 // 2
    message2 = (count + (count + 7) // 8, 8, cols // 2)
    field = (depth + 2, span, lanes)
    field1 = (depth + 2, span1, cols)
    pair, pair1 = (2, span, lanes), (2, span1, cols)
    b0, k0, u0, k1, b1, u1, c2_own, a2, b2 = call(
        down_kernel,
        [
            (depth, small, lanes), (2, small, lanes), (depth, small, lanes), (2, span1, cols),
            (depth, span1, cols), (depth, span1, cols), (count, span2, cols // 2), message2, message2,
        ],
        [
            (count, span, lanes), field, field, (count, lanes // 128, span + 8, 128), pair, pair, pair,
            pair1, pair1, pair1, field1, field1, (count, cols // 128, span1, 128),
        ],
        ext, sub, strip, c1, c2,
    )
    a2 = lax.ppermute(a2, "tile", edge_pairs(tiles, False))
    b2 = lax.ppermute(b2, "tile", edge_pairs(tiles, True))

    wide2 = 32
    pair2, pair0 = (2, wide2, cols // 2), (2, small, lanes)
    field2 = (depth + 2, wide2, cols // 2)
    field0 = (depth + 2, small, lanes)
    potential, residual = call(
        up_kernel, [right_side.shape, right_side.shape],
        [
            (count, wide2, cols // 2), pair2, pair2, pair2, (depth, wide2, cols // 2), field2, field2,
            pair1, pair1, pair1, (depth, span1, cols), field1, field1,
            pair0, pair0, pair0, (depth, small, lanes), field0, field0,
            (depth, cols // 128, span1, 128), (depth, lanes // 128, small, 128),
        ],
        c2_own, a2, b2, b0, k0, u0, k1, b1, u1, p1, p2,
    )
    return potential, residual


def solution(mesh):
    return jax.shard_map(
        body,
        mesh=mesh,
        in_specs=(
            jax.P("group", "tile", ("strip", "sub")),
            jax.P(("group", "tile"), ("strip", "sub")),
            jax.P(("group", "tile"), ("strip", "sub")),
            jax.P(("group", "tile", "strip", "sub"), None),
            jax.P(("group", "tile", "strip", "sub")),
            jax.P(("group", "tile", "strip", "sub")),
        ),
        out_specs=(
            jax.P("group", "tile", ("strip", "sub")),
            jax.P("group", "tile", ("strip", "sub")),
        ),
        check_vma=False,
    )
```

```python
import jax
import jax.numpy as jnp
import numpy as np
from jax import lax
from jax.experimental import pallas as pl
from jax.experimental.pallas import tpu as pltpu

COARSE = 8
OMEGA = 0.8

HX = 12
HX2 = 9
HY = 42
LIMIT = 512
SLABS = 3


def edge_pairs(count, odd):
    out = []
    for i in range(1 if odd else 0, count - 1, 2):
        out += [(i, i + 1), (i + 1, i)]
    return out


def lane_maps(cols):
    one = -np.ones(cols + 128, np.int64)
    half = cols // 2
    one[:cols] = np.arange(cols) // 2
    one[cols : cols + HY] = half + np.arange(HY) // 2
    one[cols + 128 - HY :] = 2 * half - HY // 2 + np.arange(HY) // 2
    h1 = HY // 2
    two = -np.ones(2 * half, np.int64)
    quarter = half // 2
    two[:half] = np.arange(half) // 2
    two[half : half + h1 - 1] = quarter + np.arange(h1 - 1) // 2
    two[2 * half - h1 + 1 :] = 2 * quarter - (h1 - 1) // 2 + np.arange(h1 - 1) // 2
    return one, two


def selection(lanes, width):
    return (lanes[:, None] == np.arange(width)[None, :]).astype(np.float32)


def exact_dot(left, right):
    high = left.astype(jnp.bfloat16)
    rest = left - high.astype(jnp.float32)
    mid = rest.astype(jnp.bfloat16)
    low = (rest - mid.astype(jnp.float32)).astype(jnp.bfloat16)
    dot = lambda part: jnp.dot(part, right, preferred_element_type=jnp.float32)
    return dot(high) + dot(mid) + dot(low)


def neighbours(u):
    rows, lanes = u.shape
    return (
        pltpu.roll(u, 1, 0)
        + pltpu.roll(u, rows - 1, 0)
        + pltpu.roll(u, 1, 1)
        + pltpu.roll(u, lanes - 1, 1)
    )


def weights(kh, kv, scale, inside, w_ref, a_ref, b_ref):
    for i, layers in enumerate((1.0, 2.0)):
        diag = 4.0 * scale * kh + layers * kv
        w = jnp.where(inside, OMEGA / jnp.where(inside, diag, 1.0), 0.0)
        if w_ref is not None:
            w_ref[i] = w
        a_ref[i] = w * (scale * kh)
        b_ref[i] = w * kv


def loop(depth, fn, vregs):
    lax.fori_loop(0, depth, fn, 0, unroll=max(1, min(depth, LIMIT // vregs)))


def sweep(src, dst, wb, a_ref, b_ref, depth):
    def layer(z, c):
        i = jnp.minimum(z, 1)
        u = src[z + 1]
        dst[z + 1] = (
            (1.0 - OMEGA) * u
            + wb[z]
            + a_ref[i] * neighbours(u)
            + b_ref[i] * (src[z] + src[z + 2])
        )
        return c

    loop(depth, layer, src.shape[1] * src.shape[2] // 1024)


def residual_of(src, z, b, kh, kv, scale):
    layers = jnp.where(z == 0, 1.0, 2.0)
    u = src[z + 1]
    return b + (scale * kh) * (neighbours(u) - 4.0 * u) + kv * (src[z] + src[z + 2] - layers * u)


def blocks_out(ref, l, x):
    for j in range(ref.shape[1]):
        ref[l, j, 0 : x.shape[0], :] = x[:, 128 * j : 128 * (j + 1)]


def blocks_in(ref, l):
    return jnp.concatenate([ref[l, j] for j in range(ref.shape[1])], 1)


def rows_doubled(ref, l, part):
    n = part.shape[0]
    for j in range(ref.shape[1]):
        for s in (0, 1):
            ref[l, j, pl.ds(s, n, stride=2), :] = part[:, 128 * j : 128 * (j + 1)]


def pack_rows_kernel(rs, kh, kv, a_out, b_out):
    depth, rows, _ = rs.shape
    even = lax.axis_index("tile") % 2 == 0

    def layer(l):
        return rs[l] if l < depth else (kh[...] if l == depth else kv[...])

    count = depth + 2
    half = count // 2

    def first(out):
        for l in range(count):
            x = layer(l)
            out[l] = x[0:8]
            out[count + l % half, 4 * (l // half) : 4 * (l // half) + 4, :] = x[8:HX]

    def last(out):
        for l in range(count):
            x = layer(l)
            out[l] = x[rows - 8 : rows]
            out[count + l % half, 4 * (l // half) : 4 * (l // half) + 4, :] = x[rows - HX : rows - 8]

    @pl.when(even)
    def _():
        last(a_out)
        first(b_out)

    @pl.when(jnp.logical_not(even))
    def _():
        first(a_out)
        last(b_out)


def forcing_kernel(rs, kh, kv, xa, xb, panels, ext, sub_out, strip_out):
    depth, rows, cols = rs.shape
    count = depth + 2
    half = count // 2
    tile = lax.axis_index("tile")
    even = tile % 2 == 0
    high = rows + HX

    def upper(x):
        for l in range(count):
            ext[l, 0:4, :] = x[count + l % half, 4 * (l // half) : 4 * (l // half) + 4, :]
            ext[l, 4:HX, :] = x[l]

    def lower(x):
        for l in range(count):
            ext[l, high : high + 8, :] = x[l]
            ext[l, high + 8 : high + HX, :] = x[count + l % half, 4 * (l // half) : 4 * (l // half) + 4, :]

    @pl.when(even)
    def _():
        lower(xa)
        upper(xb)

    @pl.when(jnp.logical_not(even))
    def _():
        upper(xa)
        lower(xb)

    for l in range(depth):
        ext[l, HX:high, :] = rs[l]
    ext[depth, HX:high, :] = kh[...]
    ext[depth + 1, HX:high, :] = kv[...]

    span = rows + 2 * HX
    total = jnp.zeros((span, cols), jnp.float32)
    left, right = [], []
    for g in range(panels.shape[0]):
        for k in range(4):
            code = panels[g, k : k + 1, :].astype(jnp.int32)
            value = panels[g, 4 + k : 5 + k, :]
            row = code // cols - (tile * rows - HX)
            col = code % cols
            hit = row == lax.broadcasted_iota(jnp.int32, (span, 128), 0)
            left.append(jnp.where(hit, value, 0.0))
            right.append(
                jnp.where(col == lax.broadcasted_iota(jnp.int32, (cols, 128), 0), 1.0, 0.0).astype(jnp.bfloat16)
            )
    left = jnp.concatenate(left, 1)
    right = jnp.concatenate(right, 1)
    high_part = left.astype(jnp.bfloat16)
    rest = left - high_part.astype(jnp.float32)
    mid_part = rest.astype(jnp.bfloat16)
    low_part = (rest - mid_part.astype(jnp.float32)).astype(jnp.bfloat16)
    for part in (high_part, mid_part, low_part):
        total = total + lax.dot_general(
            part, right, (((1,), (1,)), ((), ())), preferred_element_type=jnp.float32
        )
    ext[depth - 1] = ext[depth - 1] + total

    y = lax.axis_index("strip") * lax.axis_size("sub") + lax.axis_index("sub")
    y_even = y % 2 == 0
    lane = lax.broadcasted_iota(jnp.int32, (span, 128), 1)

    def slab(g, at_right):
        out = jnp.zeros((span, 128), jnp.float32)
        for k in range(SLABS):
            if at_right:
                x = pltpu.roll(ext[SLABS * g + k, :, cols - 128 : cols], (HY + HY * k) % 128, 1)
            else:
                x = ext[SLABS * g + k, :, 0:128]
                x = pltpu.roll(x, HY * k, 1) if k else x
            out = jnp.where((lane >= HY * k) & (lane < HY * (k + 1)), x, out)
        return out

    for g in range(count // SLABS):
        to_right = slab(g, True)
        to_left = slab(g, False)
        sub_out[g] = jnp.where(y_even, to_right, to_left)
        strip_out[g] = jnp.where(y_even, to_left, to_right)


def down_kernel(
    ext, ysub, ystrip, c1, c2,
    b_out, k_out, u_out, k1_out, b1_out, u1_out, c_out, a_msg, b_msg,
    b0, u0, u0n, r0, w0, al0, be0, w1, al1, be1, u1, u1n, r1,
):
    depth = ext.shape[0] - 2
    span, cols = ext.shape[1], ext.shape[2]
    count = depth + 2
    tiles = lax.axis_size("tile")
    tile = lax.axis_index("tile")
    y_count = lax.axis_size("strip") * lax.axis_size("sub")
    y = lax.axis_index("strip") * lax.axis_size("sub") + lax.axis_index("sub")
    y_even = y % 2 == 0
    rows = span - 2 * HX
    lane = lax.broadcasted_iota(jnp.int32, (span, 128), 1)

    for g in range(count // SLABS):
        from_right = jnp.where(y_even, ysub[g], ystrip[g])
        from_left = jnp.where(y_even, ystrip[g], ysub[g])
        for k in range(SLABS):
            l = SLABS * g + k
            right = pltpu.roll(from_right, 128 - HY * k, 1) if k else from_right
            left = pltpu.roll(from_left, 128 - HY - HY * k, 1) if (128 - HY - HY * k) % 128 else from_left
            b0[l, :, 0:cols] = ext[l]
            b0[l, :, cols : cols + 128] = jnp.where(lane < HY, right, jnp.where(lane >= 128 - HY, left, 0.0))

    def inside_of(shape, first_row, row_end, own, halo):
        row = first_row + lax.broadcasted_iota(jnp.int32, shape, 0)
        column = lax.broadcasted_iota(jnp.int32, shape, 1)
        right = (column >= own) & (column < own + halo) & (y < y_count - 1)
        left = (column >= shape[1] - halo) & (y > 0)
        return (row >= 0) & (row < row_end) & ((column < own) | right | left)

    lanes = cols + 128
    kh, kv = b0[depth], b0[depth + 1]
    weights(kh, kv, 1.0, inside_of((span, lanes), tile * rows - HX, tiles * rows, cols, HY), w0, al0, be0)
    zero = jnp.zeros((span, lanes), jnp.float32)
    u0[0] = zero
    u0[depth + 1] = zero
    u0n[0] = zero
    u0n[depth + 1] = zero

    def first(z, c):
        u0[z + 1] = w0[jnp.minimum(z, 1)] * b0[z]
        return c

    loop(depth, first, 21)
    sweep(u0, u0n, u0.at[pl.ds(1, depth)], al0, be0, depth)

    low, top = 8, span - 8
    pad = r0.shape[2] - span
    for l in range(count):
        for j in range(r0.shape[1]):
            r0[l, j, span : span + pad, :] = jnp.zeros((pad, 128), jnp.float32)
    blocks_out(r0, depth, kh)
    blocks_out(r0, depth + 1, kv)
    k_out[0] = kh[low:top]
    k_out[1] = kv[low:top]

    def rest(z, c):
        b = b0[z]
        blocks_out(r0, z, residual_of(u0n, z, b, b0[depth], b0[depth + 1], 1.0))
        b_out[z] = b[low:top]
        u_out[z] = u0n[z + 1][low:top]
        return c

    loop(depth, rest, 21)

    def coarse_rows(ref, l, n):
        return jnp.concatenate(
            [
                ref[l, j, pl.ds(0, n, stride=2), :] + ref[l, j, pl.ds(1, n, stride=2), :]
                for j in range(ref.shape[1])
            ],
            1,
        )

    span1 = r0.shape[2] // 2
    half = cols
    pairs = jnp.concatenate([coarse_rows(r0, l, span1) for l in range(count)], 0)
    b1 = exact_dot(pairs, c1[...]).reshape(count, span1, half)
    b1_out[...] = b1[0:depth]
    k1_out[...] = b1[depth:]
    kh1, kv1 = k1_out[0], k1_out[1]
    weights(
        kh1, kv1, 0.25,
        inside_of((span1, half), tile * (rows // 2) - HX // 2, tiles * (rows // 2), cols // 2, HY // 2),
        w1, al1, be1,
    )
    zero1 = jnp.zeros((span1, half), jnp.float32)
    u1[0] = zero1
    u1[depth + 1] = zero1
    u1n[0] = zero1
    u1n[depth + 1] = zero1

    def first1(z, c):
        u1[z + 1] = w1[jnp.minimum(z, 1)] * b1_out[z]
        return c

    loop(depth, first1, 8)
    sweep(u1, u1n, u1.at[pl.ds(1, depth)], al1, be1, depth)

    def rest1(z, c):
        blocks_out(r1, z, residual_of(u1n, z, b1_out[z], k1_out[0], k1_out[1], 0.25))
        u1_out[z] = u1n[z + 1]
        return c

    loop(depth, rest1, 8)
    blocks_out(r1, depth, kh1)
    blocks_out(r1, depth + 1, kv1)
    span2 = span1 // 2
    pairs = jnp.concatenate([coarse_rows(r1, l, span2) for l in range(count)], 0)
    b2 = exact_dot(pairs, c2[...]).reshape(count, span2, cols // 2)
    c_out[...] = b2

    own2 = HX // 4
    rows2 = rows // 4
    even = tile % 2 == 0

    def send(out, start):
        for l in range(count):
            out[count + l // 8, l % 8 : l % 8 + 1, :] = c_out[l, start : start + 1, :]
            out[l] = c_out[l, start + 1 : start + HX2, :]

    @pl.when(even)
    def _():
        send(a_msg, own2 - 1)
        send(b_msg, own2)

    @pl.when(jnp.logical_not(even))
    def _():
        send(a_msg, own2)
        send(b_msg, own2 - 1)


def up_kernel(
    c_in, xa, xb, b0, k0, u0, k1, b1, u1, p1, p2,
    potential, residual,
    b2, w2, al2, be2, wb2, u2, u2n, w1, al1, be1, wb1, f1, f1n, w0, al0, be0, wb0, f0, f0n, e1, e0,
):
    count = c_in.shape[0]
    depth = count - 2
    cols = potential.shape[2]
    rows = potential.shape[1]
    rows2 = rows // 4
    tiles = lax.axis_size("tile")
    tile = lax.axis_index("tile")
    y_count = lax.axis_size("strip") * lax.axis_size("sub")
    y = lax.axis_index("strip") * lax.axis_size("sub") + lax.axis_index("sub")
    even = tile % 2 == 0
    own2 = HX // 4
    span2 = b2.shape[1]
    end2 = rows2 + 2 * HX2

    def inside_of(shape, first_row, row_end, own, halo):
        row = first_row + lax.broadcasted_iota(jnp.int32, shape, 0)
        column = lax.broadcasted_iota(jnp.int32, shape, 1)
        right = (column >= own) & (column < own + halo) & (y < y_count - 1)
        left = (column >= shape[1] - halo) & (y > 0)
        return (row >= 0) & (row < row_end) & ((column < own) | right | left)

    def put(x, start):
        for l in range(count):
            b2[l, start : start + 1, :] = x[count + l // 8, l % 8 : l % 8 + 1, :]
            b2[l, start + 1 : start + HX2, :] = x[l]

    @pl.when(even)
    def _():
        put(xa, HX2 + rows2)
        put(xb, 0)

    @pl.when(jnp.logical_not(even))
    def _():
        put(xa, 0)
        put(xb, HX2 + rows2)

    lanes2 = b2.shape[2]
    for l in range(count):
        b2[l, HX2 : HX2 + rows2, :] = c_in[l, own2 : own2 + rows2, :]
        b2[l, end2:span2, :] = jnp.zeros((span2 - end2, lanes2), jnp.float32)
    row = lax.broadcasted_iota(jnp.int32, (span2, lanes2), 0)
    inside2 = inside_of((span2, lanes2), tile * rows2 - HX2, tiles * rows2, cols // 4, (HY - 2) // 4)
    weights(b2[depth], b2[depth + 1], 0.0625, inside2 & (row < end2), w2, al2, be2)

    def zero_ends(ref):
        z = jnp.zeros(ref.shape[1:], jnp.float32)
        ref[0] = z
        ref[depth + 1] = z

    for ref in (u2, u2n, f1, f1n, f0, f0n):
        zero_ends(ref)

    def first2(z, c):
        v = w2[jnp.minimum(z, 1)] * b2[z]
        wb2[z] = v
        u2[z + 1] = v
        return c

    loop(depth, first2, 4)
    src, dst = u2, u2n
    for _ in range(COARSE - 1):
        sweep(src, dst, wb2, al2, be2, depth)
        src, dst = dst, src

    span1, lanes1 = u1.shape[1], u1.shape[2]
    kh1, kv1 = k1[0], k1[1]
    weights(
        kh1, kv1, 0.25,
        inside_of((span1, lanes1), tile * (rows // 2) - HX // 2, tiles * (rows // 2), cols // 2, HY // 2),
        w1, al1, be1,
    )
    off2 = HX2 - own2
    coarse = jnp.concatenate([src[z + 1][off2 : off2 + span1 // 2] for z in range(depth)], 0)
    fine = exact_dot(coarse, p2[...])
    for z in range(depth):
        rows_doubled(e1, z, fine[z * (span1 // 2) : (z + 1) * (span1 // 2)])

    def first1(z, c):
        f1[z + 1] = u1[z] + blocks_in(e1, z)
        wb1[z] = w1[jnp.minimum(z, 1)] * b1[z]
        return c

    loop(depth, first1, 8)
    sweep(f1, f1n, wb1, al1, be1, depth)
    sweep(f1n, f1, wb1, al1, be1, depth)

    span0, lanes0 = b0.shape[1], b0.shape[2]
    above = (span0 - rows) // 2
    weights(
        k0[0], k0[1], 1.0,
        inside_of((span0, lanes0), tile * rows - above, tiles * rows, cols, HY),
        w0, al0, be0,
    )
    off1 = (HX - above) // 2
    fine = exact_dot(f1[pl.ds(1, depth)].reshape(depth * span1, lanes1), p1[...])
    for z in range(depth):
        rows_doubled(e0, z, fine[z * span1 + off1 : z * span1 + off1 + span0 // 2])

    def first0(z, c):
        f0[z + 1] = u0[z] + blocks_in(e0, z)
        wb0[z] = w0[jnp.minimum(z, 1)] * b0[z]
        return c

    loop(depth, first0, 15)
    sweep(f0, f0n, wb0, al0, be0, depth)
    sweep(f0n, f0, wb0, al0, be0, depth)

    def last(z, c):
        r = residual_of(f0, z, b0[z], k0[0], k0[1], 1.0)
        residual[z] = r[above : above + rows, 0:cols]
        potential[z] = f0[z + 1][above : above + rows, 0:cols]
        return c

    loop(depth, last, 15)


VM = pl.BlockSpec(memory_space=pltpu.VMEM)


def call(kernel, outs, scratch, *args):
    f32 = lambda shape: jax.ShapeDtypeStruct(shape, jnp.float32)
    return pl.pallas_call(
        kernel,
        out_shape=[f32(s) for s in outs],
        in_specs=[VM] * len(args),
        out_specs=[VM] * len(outs),
        scratch_shapes=[pltpu.VMEM(s, jnp.float32) for s in scratch],
        compiler_params=pltpu.CompilerParams(vmem_limit_bytes=40 << 20),
    )(*args)


def body(right_side, horiz_coef, vert_coef, panel_owner, panel_cell, panel_pressure):
    depth, rows, cols = right_side.shape
    tiles = lax.axis_size("tile")
    y_axes = ("strip", "sub")
    y_count = lax.axis_size("strip") * lax.axis_size("sub")
    count = depth + 2
    span = rows + 2 * HX
    one, two = lane_maps(cols)
    c1 = jnp.asarray(0.25 * selection(one, cols), jnp.bfloat16)
    c2 = jnp.asarray(0.25 * selection(two, cols // 2), jnp.bfloat16)
    p1 = jnp.asarray(selection(one, cols).T, jnp.bfloat16)
    p2 = jnp.asarray(selection(two, cols // 2).T, jnp.bfloat16)

    code = (panel_owner[:, 0] * (rows * cols) + panel_cell).astype(jnp.float32)
    panels = jnp.concatenate([code.reshape(4, -1), panel_pressure.reshape(4, -1)], 0)[None]
    step = 1
    while step < tiles:
        swap = [(i, i ^ step) for i in range(tiles)]
        panels = jnp.concatenate([panels, lax.ppermute(panels, "tile", swap)], 0)
        step *= 2

    message = (count + count // 2, 8, cols)
    a, b = call(pack_rows_kernel, [message] * 2, [], right_side, horiz_coef, vert_coef)
    a = lax.ppermute(a, "tile", edge_pairs(tiles, False))
    b = lax.ppermute(b, "tile", edge_pairs(tiles, True))

    slabs = (count // SLABS, span, 128)
    ext, sub, strip = call(
        forcing_kernel, [(count, span, cols), slabs, slabs], [],
        right_side, horiz_coef, vert_coef, a, b, panels,
    )
    sub = lax.ppermute(sub, y_axes, edge_pairs(y_count, False))
    strip = lax.ppermute(strip, y_axes, edge_pairs(y_count, True))

    lanes = cols + 128
    small = span - 16
    span1 = (span + 8) // 2
    span2 = span1 // 2
    message2 = (count + (count + 7) // 8, 8, cols // 2)
    field = (depth + 2, span, lanes)
    field1 = (depth + 2, span1, cols)
    pair, pair1 = (2, span, lanes), (2, span1, cols)
    b0, k0, u0, k1, b1, u1, c2_own, a2, b2 = call(
        down_kernel,
        [
            (depth, small, lanes), (2, small, lanes), (depth, small, lanes), (2, span1, cols),
            (depth, span1, cols), (depth, span1, cols), (count, span2, cols // 2), message2, message2,
        ],
        [
            (count, span, lanes), field, field, (count, lanes // 128, span + 8, 128), pair, pair, pair,
            pair1, pair1, pair1, field1, field1, (count, cols // 128, span1, 128),
        ],
        ext, sub, strip, c1, c2,
    )
    a2 = lax.ppermute(a2, "tile", edge_pairs(tiles, False))
    b2 = lax.ppermute(b2, "tile", edge_pairs(tiles, True))

    wide2 = 32
    pair2, pair0 = (2, wide2, cols // 2), (2, small, lanes)
    field2 = (depth + 2, wide2, cols // 2)
    field0 = (depth + 2, small, lanes)
    potential, residual = call(
        up_kernel, [right_side.shape, right_side.shape],
        [
            (count, wide2, cols // 2), pair2, pair2, pair2, (depth, wide2, cols // 2), field2, field2,
            pair1, pair1, pair1, (depth, span1, cols), field1, field1,
            pair0, pair0, pair0, (depth, small, lanes), field0, field0,
            (depth, cols // 128, span1, 128), (depth, lanes // 128, small, 128),
        ],
        c2_own, a2, b2, b0, k0, u0, k1, b1, u1, p1, p2,
    )
    return potential, residual


def solution(mesh):
    return jax.shard_map(
        body,
        mesh=mesh,
        in_specs=(
            jax.P("group", "tile", ("strip", "sub")),
            jax.P(("group", "tile"), ("strip", "sub")),
            jax.P(("group", "tile"), ("strip", "sub")),
            jax.P(("group", "tile", "strip", "sub"), None),
            jax.P(("group", "tile", "strip", "sub")),
            jax.P(("group", "tile", "strip", "sub")),
        ),
        out_specs=(
            jax.P("group", "tile", ("strip", "sub")),
            jax.P("group", "tile", ("strip", "sub")),
        ),
        check_vma=False,
    )
```

```python
import jax
import jax.numpy as jnp
import numpy as np
from jax import lax
from jax.experimental import pallas as pl
from jax.experimental.pallas import tpu as pltpu

COARSE = 8
OMEGA = 0.8

HX = 12
HX2 = 9
HY = 42
LIMIT = 512
SLABS = 3


def edge_pairs(count, odd):
    out = []
    for i in range(1 if odd else 0, count - 1, 2):
        out += [(i, i + 1), (i + 1, i)]
    return out


def lane_maps(cols):
    one = -np.ones(cols + 128, np.int64)
    half = cols // 2
    one[:cols] = np.arange(cols) // 2
    one[cols : cols + HY] = half + np.arange(HY) // 2
    one[cols + 128 - HY :] = 2 * half - HY // 2 + np.arange(HY) // 2
    h1 = HY // 2
    two = -np.ones(2 * half, np.int64)
    quarter = half // 2
    two[:half] = np.arange(half) // 2
    two[half : half + h1 - 1] = quarter + np.arange(h1 - 1) // 2
    two[2 * half - h1 + 1 :] = 2 * quarter - (h1 - 1) // 2 + np.arange(h1 - 1) // 2
    return one, two


def selection(lanes, width):
    return (lanes[:, None] == np.arange(width)[None, :]).astype(np.float32)


def split(x, parts):
    out = []
    for _ in range(parts):
        out.append(x.astype(jnp.bfloat16))
        x = x - out[-1].astype(jnp.float32)
    return out


def exact_dot(left, right):
    return sum(jnp.dot(part, right, preferred_element_type=jnp.float32) for part in split(left, 2))


def neighbours(u):
    rows, lanes = u.shape
    return (
        pltpu.roll(u, 1, 0)
        + pltpu.roll(u, rows - 1, 0)
        + pltpu.roll(u, 1, 1)
        + pltpu.roll(u, lanes - 1, 1)
    )


def weights(kh, kv, scale, inside, w_ref, a_ref, b_ref):
    for i, layers in enumerate((1.0, 2.0)):
        diag = 4.0 * scale * kh + layers * kv
        w = jnp.where(inside, OMEGA / jnp.where(inside, diag, 1.0), 0.0)
        if w_ref is not None:
            w_ref[i] = w
        a_ref[i] = w * (scale * kh)
        b_ref[i] = w * kv


def loop(depth, fn, vregs):
    lax.fori_loop(0, depth, fn, 0, unroll=max(1, min(depth, LIMIT // vregs)))


def sweep(src, dst, wb, a_ref, b_ref, depth):
    def layer(z, c):
        i = jnp.minimum(z, 1)
        u = src[z + 1]
        dst[z + 1] = (
            (1.0 - OMEGA) * u
            + wb[z]
            + a_ref[i] * neighbours(u)
            + b_ref[i] * (src[z] + src[z + 2])
        )
        return c

    loop(depth, layer, src.shape[1] * src.shape[2] // 1024)


def residual_of(src, z, b, kh, kv, scale):
    layers = jnp.where(z == 0, 1.0, 2.0)
    u = src[z + 1]
    return b + (scale * kh) * (neighbours(u) - 4.0 * u) + kv * (src[z] + src[z + 2] - layers * u)


def blocks_out(ref, l, x):
    for j in range(ref.shape[1]):
        ref[l, j, 0 : x.shape[0], :] = x[:, 128 * j : 128 * (j + 1)]


def blocks_in(ref, l):
    return jnp.concatenate([ref[l, j] for j in range(ref.shape[1])], 1)


def rows_doubled(ref, l, part):
    n = part.shape[0]
    for j in range(ref.shape[1]):
        for s in (0, 1):
            ref[l, j, pl.ds(s, n, stride=2), :] = part[:, 128 * j : 128 * (j + 1)]


def load_kernel(rs, kh, kv, owner, cell, pressure, x, panels, a_out, b_out, ints, sems):
    depth, rows, cols = rs.shape
    count = depth + 2
    half = count // 2
    even = lax.axis_index("tile") % 2 == 0
    copies = [
        pltpu.make_async_copy(src, dst, sems.at[i])
        for i, (src, dst) in enumerate(
            (
                (owner, ints.at[0]),
                (cell, ints.at[1]),
                (pressure, panels.at[0, pl.ds(4, 4)]),
                (rs, x.at[pl.ds(0, depth)]),
                (kh, x.at[depth]),
                (kv, x.at[depth + 1]),
            )
        )
    ]
    for copy in copies:
        copy.start()
    for copy in copies:
        copy.wait()
    panels[0, 0:4, :] = (ints[0] * (rows * cols) + ints[1]).astype(jnp.float32)

    def first(out):
        for l in range(count):
            out[l] = x[l, 0:8, :]
            out[count + l % half, 4 * (l // half) : 4 * (l // half) + 4, :] = x[l, 8:HX, :]

    def last(out):
        for l in range(count):
            out[l] = x[l, rows - 8 : rows, :]
            out[count + l % half, 4 * (l // half) : 4 * (l // half) + 4, :] = x[l, rows - HX : rows - 8, :]

    @pl.when(even)
    def _():
        last(a_out)
        first(b_out)

    @pl.when(jnp.logical_not(even))
    def _():
        first(a_out)
        last(b_out)


def forcing_kernel(x_own, xa, xb, panels, ext, sub_out, strip_out):
    count, rows, cols = x_own.shape
    depth = count - 2
    half = count // 2
    tile = lax.axis_index("tile")
    even = tile % 2 == 0
    high = rows + HX

    def upper(x):
        for l in range(count):
            ext[l, 0:4, :] = x[count + l % half, 4 * (l // half) : 4 * (l // half) + 4, :]
            ext[l, 4:HX, :] = x[l]

    def lower(x):
        for l in range(count):
            ext[l, high : high + 8, :] = x[l]
            ext[l, high + 8 : high + HX, :] = x[count + l % half, 4 * (l // half) : 4 * (l // half) + 4, :]

    @pl.when(even)
    def _():
        lower(xa)
        upper(xb)

    @pl.when(jnp.logical_not(even))
    def _():
        upper(xa)
        lower(xb)

    for l in range(count):
        ext[l, HX:high, :] = x_own[l]

    span = rows + 2 * HX
    left, right = [], []
    for g in range(panels.shape[0]):
        group = panels[g]
        for k in range(4):
            code = group[k : k + 1].astype(jnp.int32)
            value = group[4 + k : 5 + k]
            row = code // cols - (tile * rows - HX)
            col = code % cols
            hit = row == lax.broadcasted_iota(jnp.int32, (span, 128), 0)
            left.append(jnp.where(hit, value, 0.0))
            right.append(
                jnp.where(col == lax.broadcasted_iota(jnp.int32, (cols, 128), 0), 1.0, 0.0).astype(jnp.bfloat16)
            )
    left = jnp.concatenate(left, 1)
    right = jnp.concatenate(right, 1)
    parts = lax.dot_general(
        jnp.concatenate(split(left, 3), 0), right, (((1,), (1,)), ((), ())), preferred_element_type=jnp.float32
    )
    total = parts[0:span] + parts[span : 2 * span] + parts[2 * span :]
    ext[depth - 1] = ext[depth - 1] + total

    y = lax.axis_index("strip") * lax.axis_size("sub") + lax.axis_index("sub")
    y_even = y % 2 == 0
    lane = lax.broadcasted_iota(jnp.int32, (span, 128), 1)

    def slab(g, at_right):
        out = jnp.zeros((span, 128), jnp.float32)
        for k in range(SLABS):
            if at_right:
                x = pltpu.roll(ext[SLABS * g + k, :, cols - 128 : cols], (HY + HY * k) % 128, 1)
            else:
                x = ext[SLABS * g + k, :, 0:128]
                x = pltpu.roll(x, HY * k, 1) if k else x
            out = jnp.where((lane >= HY * k) & (lane < HY * (k + 1)), x, out)
        return out

    for g in range(count // SLABS):
        to_right = slab(g, True)
        to_left = slab(g, False)
        sub_out[g] = jnp.where(y_even, to_right, to_left)
        strip_out[g] = jnp.where(y_even, to_left, to_right)


def down_kernel(
    ext, ysub, ystrip, c1, c2,
    b_out, k_out, u_out, k1_out, b1_out, u1_out, c_out, a_msg, b_msg,
    b0, u0, u0n, r0, w0, al0, be0, w1, al1, be1, u1, u1n, r1,
):
    depth = ext.shape[0] - 2
    span, cols = ext.shape[1], ext.shape[2]
    count = depth + 2
    tiles = lax.axis_size("tile")
    tile = lax.axis_index("tile")
    y_count = lax.axis_size("strip") * lax.axis_size("sub")
    y = lax.axis_index("strip") * lax.axis_size("sub") + lax.axis_index("sub")
    y_even = y % 2 == 0
    rows = span - 2 * HX
    lane = lax.broadcasted_iota(jnp.int32, (span, 128), 1)

    for g in range(count // SLABS):
        from_right = jnp.where(y_even, ysub[g], ystrip[g])
        from_left = jnp.where(y_even, ystrip[g], ysub[g])
        for k in range(SLABS):
            l = SLABS * g + k
            right = pltpu.roll(from_right, 128 - HY * k, 1) if k else from_right
            left = pltpu.roll(from_left, 128 - HY - HY * k, 1) if (128 - HY - HY * k) % 128 else from_left
            b0[l, :, 0:cols] = ext[l]
            b0[l, :, cols : cols + 128] = jnp.where(lane < HY, right, jnp.where(lane >= 128 - HY, left, 0.0))

    def inside_of(shape, first_row, row_end, own, halo):
        row = first_row + lax.broadcasted_iota(jnp.int32, shape, 0)
        column = lax.broadcasted_iota(jnp.int32, shape, 1)
        right = (column >= own) & (column < own + halo) & (y < y_count - 1)
        left = (column >= shape[1] - halo) & (y > 0)
        return (row >= 0) & (row < row_end) & ((column < own) | right | left)

    lanes = cols + 128
    kh, kv = b0[depth], b0[depth + 1]
    weights(kh, kv, 1.0, inside_of((span, lanes), tile * rows - HX, tiles * rows, cols, HY), w0, al0, be0)
    zero = jnp.zeros((span, lanes), jnp.float32)
    u0[0] = zero
    u0[depth + 1] = zero
    u0n[0] = zero
    u0n[depth + 1] = zero

    def first(z, c):
        u0[z + 1] = w0[jnp.minimum(z, 1)] * b0[z]
        return c

    loop(depth, first, 21)
    sweep(u0, u0n, u0.at[pl.ds(1, depth)], al0, be0, depth)

    low, top = 8, span - 8
    pad = r0.shape[2] - span
    for l in range(count):
        for j in range(r0.shape[1]):
            r0[l, j, span : span + pad, :] = jnp.zeros((pad, 128), jnp.float32)
    blocks_out(r0, depth, kh)
    blocks_out(r0, depth + 1, kv)
    k_out[0] = kh[low:top]
    k_out[1] = kv[low:top]

    def rest(z, c):
        b = b0[z]
        blocks_out(r0, z, residual_of(u0n, z, b, b0[depth], b0[depth + 1], 1.0))
        b_out[z] = b[low:top]
        u_out[z] = u0n[z + 1][low:top]
        return c

    loop(depth, rest, 21)

    def coarse_rows(ref, l, n):
        return jnp.concatenate(
            [
                ref[l, j, pl.ds(0, n, stride=2), :] + ref[l, j, pl.ds(1, n, stride=2), :]
                for j in range(ref.shape[1])
            ],
            1,
        )

    span1 = r0.shape[2] // 2
    half = cols
    pairs = jnp.concatenate([coarse_rows(r0, l, span1) for l in range(count)], 0)
    b1 = exact_dot(pairs, c1[...]).reshape(count, span1, half)
    b1_out[...] = b1[0:depth]
    k1_out[...] = b1[depth:]
    kh1, kv1 = k1_out[0], k1_out[1]
    weights(
        kh1, kv1, 0.25,
        inside_of((span1, half), tile * (rows // 2) - HX // 2, tiles * (rows // 2), cols // 2, HY // 2),
        w1, al1, be1,
    )
    zero1 = jnp.zeros((span1, half), jnp.float32)
    u1[0] = zero1
    u1[depth + 1] = zero1
    u1n[0] = zero1
    u1n[depth + 1] = zero1

    def first1(z, c):
        u1[z + 1] = w1[jnp.minimum(z, 1)] * b1_out[z]
        return c

    loop(depth, first1, 8)
    sweep(u1, u1n, u1.at[pl.ds(1, depth)], al1, be1, depth)

    def rest1(z, c):
        blocks_out(r1, z, residual_of(u1n, z, b1_out[z], k1_out[0], k1_out[1], 0.25))
        u1_out[z] = u1n[z + 1]
        return c

    loop(depth, rest1, 8)
    blocks_out(r1, depth, kh1)
    blocks_out(r1, depth + 1, kv1)
    span2 = span1 // 2
    pairs = jnp.concatenate([coarse_rows(r1, l, span2) for l in range(count)], 0)
    b2 = exact_dot(pairs, c2[...]).reshape(count, span2, cols // 2)
    c_out[...] = b2

    own2 = HX // 4
    rows2 = rows // 4
    even = tile % 2 == 0

    def send(out, start):
        for l in range(count):
            out[count + l // 8, l % 8 : l % 8 + 1, :] = c_out[l, start : start + 1, :]
            out[l] = c_out[l, start + 1 : start + HX2, :]

    @pl.when(even)
    def _():
        send(a_msg, own2 - 1)
        send(b_msg, own2)

    @pl.when(jnp.logical_not(even))
    def _():
        send(a_msg, own2)
        send(b_msg, own2 - 1)


def up_kernel(
    c_in, xa, xb, b0, k0, u0, k1, b1, u1, p1, p2,
    potential, residual,
    b2, w2, al2, be2, wb2, u2, u2n, w1, al1, be1, wb1, f1, f1n, w0, al0, be0, wb0, f0, f0n, e1, e0,
):
    count = c_in.shape[0]
    depth = count - 2
    cols = potential.shape[2]
    rows = potential.shape[1]
    rows2 = rows // 4
    tiles = lax.axis_size("tile")
    tile = lax.axis_index("tile")
    y_count = lax.axis_size("strip") * lax.axis_size("sub")
    y = lax.axis_index("strip") * lax.axis_size("sub") + lax.axis_index("sub")
    even = tile % 2 == 0
    own2 = HX // 4
    span2 = b2.shape[1]
    end2 = rows2 + 2 * HX2

    def inside_of(shape, first_row, row_end, own, halo):
        row = first_row + lax.broadcasted_iota(jnp.int32, shape, 0)
        column = lax.broadcasted_iota(jnp.int32, shape, 1)
        right = (column >= own) & (column < own + halo) & (y < y_count - 1)
        left = (column >= shape[1] - halo) & (y > 0)
        return (row >= 0) & (row < row_end) & ((column < own) | right | left)

    def put(x, start):
        for l in range(count):
            b2[l, start : start + 1, :] = x[count + l // 8, l % 8 : l % 8 + 1, :]
            b2[l, start + 1 : start + HX2, :] = x[l]

    @pl.when(even)
    def _():
        put(xa, HX2 + rows2)
        put(xb, 0)

    @pl.when(jnp.logical_not(even))
    def _():
        put(xa, 0)
        put(xb, HX2 + rows2)

    lanes2 = b2.shape[2]
    for l in range(count):
        b2[l, HX2 : HX2 + rows2, :] = c_in[l, own2 : own2 + rows2, :]
        b2[l, end2:span2, :] = jnp.zeros((span2 - end2, lanes2), jnp.float32)
    row = lax.broadcasted_iota(jnp.int32, (span2, lanes2), 0)
    inside2 = inside_of((span2, lanes2), tile * rows2 - HX2, tiles * rows2, cols // 4, (HY - 2) // 4)
    weights(b2[depth], b2[depth + 1], 0.0625, inside2 & (row < end2), w2, al2, be2)

    def zero_ends(ref):
        z = jnp.zeros(ref.shape[1:], jnp.float32)
        ref[0] = z
        ref[depth + 1] = z

    for ref in (u2, u2n, f1, f1n, f0, f0n):
        zero_ends(ref)

    def first2(z, c):
        v = w2[jnp.minimum(z, 1)] * b2[z]
        wb2[z] = v
        u2[z + 1] = v
        return c

    loop(depth, first2, 4)
    src, dst = u2, u2n
    for _ in range(COARSE - 1):
        sweep(src, dst, wb2, al2, be2, depth)
        src, dst = dst, src

    span1, lanes1 = u1.shape[1], u1.shape[2]
    kh1, kv1 = k1[0], k1[1]
    weights(
        kh1, kv1, 0.25,
        inside_of((span1, lanes1), tile * (rows // 2) - HX // 2, tiles * (rows // 2), cols // 2, HY // 2),
        w1, al1, be1,
    )
    off2 = HX2 - own2
    coarse = jnp.concatenate([src[z + 1][off2 : off2 + span1 // 2] for z in range(depth)], 0)
    fine = exact_dot(coarse, p2[...])
    for z in range(depth):
        rows_doubled(e1, z, fine[z * (span1 // 2) : (z + 1) * (span1 // 2)])

    def first1(z, c):
        f1[z + 1] = u1[z] + blocks_in(e1, z)
        wb1[z] = w1[jnp.minimum(z, 1)] * b1[z]
        return c

    loop(depth, first1, 8)
    sweep(f1, f1n, wb1, al1, be1, depth)
    sweep(f1n, f1, wb1, al1, be1, depth)

    span0, lanes0 = b0.shape[1], b0.shape[2]
    above = (span0 - rows) // 2
    weights(
        k0[0], k0[1], 1.0,
        inside_of((span0, lanes0), tile * rows - above, tiles * rows, cols, HY),
        w0, al0, be0,
    )
    off1 = (HX - above) // 2
    fine = exact_dot(f1[pl.ds(1, depth)].reshape(depth * span1, lanes1), p1[...])
    for z in range(depth):
        rows_doubled(e0, z, fine[z * span1 + off1 : z * span1 + off1 + span0 // 2])

    def first0(z, c):
        f0[z + 1] = u0[z] + blocks_in(e0, z)
        wb0[z] = w0[jnp.minimum(z, 1)] * b0[z]
        return c

    loop(depth, first0, 15)
    sweep(f0, f0n, wb0, al0, be0, depth)
    sweep(f0n, f0, wb0, al0, be0, depth)

    def last(z, c):
        r = residual_of(f0, z, b0[z], k0[0], k0[1], 1.0)
        residual[z] = r[above : above + rows, 0:cols]
        potential[z] = f0[z + 1][above : above + rows, 0:cols]
        return c

    loop(depth, last, 15)


VM = pl.BlockSpec(memory_space=pltpu.VMEM)


def call(kernel, outs, scratch, *args):
    f32 = lambda shape: jax.ShapeDtypeStruct(shape, jnp.float32)
    return pl.pallas_call(
        kernel,
        out_shape=[f32(s) for s in outs],
        in_specs=[VM] * len(args),
        out_specs=[VM] * len(outs),
        scratch_shapes=[pltpu.VMEM(s, jnp.float32) for s in scratch],
        compiler_params=pltpu.CompilerParams(vmem_limit_bytes=40 << 20),
    )(*args)


def body(right_side, horiz_coef, vert_coef, panel_owner, panel_cell, panel_pressure):
    depth, rows, cols = right_side.shape
    tiles = lax.axis_size("tile")
    y_axes = ("strip", "sub")
    y_count = lax.axis_size("strip") * lax.axis_size("sub")
    count = depth + 2
    span = rows + 2 * HX
    one, two = lane_maps(cols)
    c1 = jnp.asarray(0.25 * selection(one, cols), jnp.bfloat16)
    c2 = jnp.asarray(0.25 * selection(two, cols // 2), jnp.bfloat16)
    p1 = jnp.asarray(selection(one, cols).T, jnp.bfloat16)
    p2 = jnp.asarray(selection(two, cols // 2).T, jnp.bfloat16)

    message = (count + count // 2, 8, cols)
    f32 = lambda shape: jax.ShapeDtypeStruct(shape, jnp.float32)
    x_own, panels, a, b = pl.pallas_call(
        load_kernel,
        out_shape=[f32((count, rows, cols)), f32((1, 8, 128)), f32(message), f32(message)],
        in_specs=[pl.BlockSpec(memory_space=pltpu.HBM)] * 6,
        out_specs=[VM] * 4,
        scratch_shapes=[pltpu.VMEM((2, 4, 128), jnp.int32), pltpu.SemaphoreType.DMA((6,))],
        compiler_params=pltpu.CompilerParams(vmem_limit_bytes=8 << 20),
    )(
        *[
            pltpu.with_memory_space_constraint(x, pltpu.HBM)
            for x in (
                right_side, horiz_coef, vert_coef,
                panel_owner.reshape(4, -1), panel_cell.reshape(4, -1), panel_pressure.reshape(4, -1),
            )
        ]
    )
    near = lax.ppermute(panels, "tile", [(i, i ^ 1) for i in range(tiles)])
    a = lax.ppermute(a, "tile", edge_pairs(tiles, False))
    b = lax.ppermute(b, "tile", edge_pairs(tiles, True))
    panels = jnp.concatenate([panels, near], 0)
    step = 2
    while step < tiles:
        swap = [(i, i ^ step) for i in range(tiles)]
        panels = jnp.concatenate([panels, lax.ppermute(panels, "tile", swap)], 0)
        step *= 2

    slabs = (count // SLABS, span, 128)
    ext, sub, strip = call(
        forcing_kernel, [(count, span, cols), slabs, slabs], [],
        x_own, a, b, panels,
    )
    sub = lax.ppermute(sub, y_axes, edge_pairs(y_count, False))
    strip = lax.ppermute(strip, y_axes, edge_pairs(y_count, True))

    lanes = cols + 128
    small = span - 16
    span1 = (span + 8) // 2
    span2 = span1 // 2
    message2 = (count + (count + 7) // 8, 8, cols // 2)
    field = (depth + 2, span, lanes)
    field1 = (depth + 2, span1, cols)
    pair, pair1 = (2, span, lanes), (2, span1, cols)
    b0, k0, u0, k1, b1, u1, c2_own, a2, b2 = call(
        down_kernel,
        [
            (depth, small, lanes), (2, small, lanes), (depth, small, lanes), (2, span1, cols),
            (depth, span1, cols), (depth, span1, cols), (count, span2, cols // 2), message2, message2,
        ],
        [
            (count, span, lanes), field, field, (count, lanes // 128, span + 8, 128), pair, pair, pair,
            pair1, pair1, pair1, field1, field1, (count, cols // 128, span1, 128),
        ],
        ext, sub, strip, c1, c2,
    )
    a2 = lax.ppermute(a2, "tile", edge_pairs(tiles, False))
    b2 = lax.ppermute(b2, "tile", edge_pairs(tiles, True))

    wide2 = 32
    pair2, pair0 = (2, wide2, cols // 2), (2, small, lanes)
    field2 = (depth + 2, wide2, cols // 2)
    field0 = (depth + 2, small, lanes)
    potential, residual = call(
        up_kernel, [right_side.shape, right_side.shape],
        [
            (count, wide2, cols // 2), pair2, pair2, pair2, (depth, wide2, cols // 2), field2, field2,
            pair1, pair1, pair1, (depth, span1, cols), field1, field1,
            pair0, pair0, pair0, (depth, small, lanes), field0, field0,
            (depth, cols // 128, span1, 128), (depth, lanes // 128, small, 128),
        ],
        c2_own, a2, b2, b0, k0, u0, k1, b1, u1, p1, p2,
    )
    return potential, residual


def solution(mesh):
    return jax.shard_map(
        body,
        mesh=mesh,
        in_specs=(
            jax.P("group", "tile", ("strip", "sub")),
            jax.P(("group", "tile"), ("strip", "sub")),
            jax.P(("group", "tile"), ("strip", "sub")),
            jax.P(("group", "tile", "strip", "sub"), None),
            jax.P(("group", "tile", "strip", "sub")),
            jax.P(("group", "tile", "strip", "sub")),
        ),
        out_specs=(
            jax.P("group", "tile", ("strip", "sub")),
            jax.P("group", "tile", ("strip", "sub")),
        ),
        check_vma=False,
    )
```

```python
import jax
import jax.numpy as jnp
import numpy as np
from jax import lax
from jax.experimental import pallas as pl
from jax.experimental.pallas import tpu as pltpu

COARSE = 8
OMEGA = 0.8

HX = 12
HX2 = 9
HY = 42
LIMIT = 512
SLABS = 3


def neighbour_swap(x, axis, odd, spare):
    axis = axis if isinstance(axis, tuple) else (axis,)
    count = lax.axis_size(axis)
    twins = lax.axis_size(spare)
    leading = spare == "group"
    place = lambda i, twin: twin * count + i if leading else i * twins + twin
    pairs = []
    for twin in range(twins):
        for i in range(count):
            j, other = (i + 1 if i % 2 == odd else i - 1), twin
            if not 0 <= j < count:
                j, other = i, twin ^ 1
            pairs.append((place(i, twin), place(j, other)))
    return lax.ppermute(x, (spare,) + axis if leading else axis + (spare,), pairs)


def lane_maps(cols):
    one = -np.ones(cols + 128, np.int64)
    half = cols // 2
    one[:cols] = np.arange(cols) // 2
    one[cols : cols + HY] = half + np.arange(HY) // 2
    one[cols + 128 - HY :] = 2 * half - HY // 2 + np.arange(HY) // 2
    h1 = HY // 2
    two = -np.ones(2 * half, np.int64)
    quarter = half // 2
    two[:half] = np.arange(half) // 2
    two[half : half + h1 - 1] = quarter + np.arange(h1 - 1) // 2
    two[2 * half - h1 + 1 :] = 2 * quarter - (h1 - 1) // 2 + np.arange(h1 - 1) // 2
    return one, two


def selection(lanes, width):
    return (lanes[:, None] == np.arange(width)[None, :]).astype(np.float32)


def split(x, parts):
    out = []
    for _ in range(parts):
        out.append(x.astype(jnp.bfloat16))
        x = x - out[-1].astype(jnp.float32)
    return out


def exact_dot(left, right):
    return sum(jnp.dot(part, right, preferred_element_type=jnp.float32) for part in split(left, 2))


def neighbours(u):
    rows, lanes = u.shape
    return (
        pltpu.roll(u, 1, 0)
        + pltpu.roll(u, rows - 1, 0)
        + pltpu.roll(u, 1, 1)
        + pltpu.roll(u, lanes - 1, 1)
    )


def weights(kh, kv, scale, inside, w_ref, a_ref, b_ref):
    for i, layers in enumerate((1.0, 2.0)):
        diag = 4.0 * scale * kh + layers * kv
        w = jnp.where(inside, OMEGA / jnp.where(inside, diag, 1.0), 0.0)
        if w_ref is not None:
            w_ref[i] = w
        a_ref[i] = w * (scale * kh)
        b_ref[i] = w * kv


def loop(depth, fn, vregs):
    lax.fori_loop(0, depth, fn, 0, unroll=max(1, min(depth, LIMIT // vregs)))


def sweep(src, dst, wb, a_ref, b_ref, depth):
    def layer(z, c):
        i = jnp.minimum(z, 1)
        u = src[z + 1]
        dst[z + 1] = (
            (1.0 - OMEGA) * u
            + wb[z]
            + a_ref[i] * neighbours(u)
            + b_ref[i] * (src[z] + src[z + 2])
        )
        return c

    loop(depth, layer, src.shape[1] * src.shape[2] // 1024)


def residual_of(src, z, b, kh, kv, scale):
    layers = jnp.where(z == 0, 1.0, 2.0)
    u = src[z + 1]
    return b + (scale * kh) * (neighbours(u) - 4.0 * u) + kv * (src[z] + src[z + 2] - layers * u)


def blocks_out(ref, l, x):
    for j in range(ref.shape[1]):
        ref[l, j, 0 : x.shape[0], :] = x[:, 128 * j : 128 * (j + 1)]


def blocks_in(ref, l):
    return jnp.concatenate([ref[l, j] for j in range(ref.shape[1])], 1)


def rows_doubled(ref, l, part):
    n = part.shape[0]
    for j in range(ref.shape[1]):
        for s in (0, 1):
            ref[l, j, pl.ds(s, n, stride=2), :] = part[:, 128 * j : 128 * (j + 1)]


def load_kernel(rs, kh, kv, owner, cell, pressure, x, panels, a_out, b_out, ints, sems):
    depth, rows, cols = rs.shape
    count = depth + 2
    half = count // 2
    even = lax.axis_index("tile") % 2 == 0
    copies = [
        pltpu.make_async_copy(src, dst, sems.at[i])
        for i, (src, dst) in enumerate(
            (
                (owner, ints.at[0]),
                (cell, ints.at[1]),
                (pressure, panels.at[0, pl.ds(4, 4)]),
                (rs, x.at[pl.ds(0, depth)]),
                (kh, x.at[depth]),
                (kv, x.at[depth + 1]),
            )
        )
    ]
    for copy in copies:
        copy.start()
    for copy in copies:
        copy.wait()
    panels[0, 0:4, :] = (ints[0] * (rows * cols) + ints[1]).astype(jnp.float32)

    def first(out):
        for l in range(count):
            out[l] = x[l, 0:8, :]
            out[count + l % half, 4 * (l // half) : 4 * (l // half) + 4, :] = x[l, 8:HX, :]

    def last(out):
        for l in range(count):
            out[l] = x[l, rows - 8 : rows, :]
            out[count + l % half, 4 * (l // half) : 4 * (l // half) + 4, :] = x[l, rows - HX : rows - 8, :]

    @pl.when(even)
    def _():
        last(a_out)
        first(b_out)

    @pl.when(jnp.logical_not(even))
    def _():
        first(a_out)
        last(b_out)


def forcing_kernel(x_own, xa, xb, panels, ext, sub_out, strip_out):
    count, rows, cols = x_own.shape
    depth = count - 2
    half = count // 2
    tile = lax.axis_index("tile")
    even = tile % 2 == 0
    high = rows + HX

    def upper(x):
        for l in range(count):
            ext[l, 0:4, :] = x[count + l % half, 4 * (l // half) : 4 * (l // half) + 4, :]
            ext[l, 4:HX, :] = x[l]

    def lower(x):
        for l in range(count):
            ext[l, high : high + 8, :] = x[l]
            ext[l, high + 8 : high + HX, :] = x[count + l % half, 4 * (l // half) : 4 * (l // half) + 4, :]

    @pl.when(even)
    def _():
        lower(xa)
        upper(xb)

    @pl.when(jnp.logical_not(even))
    def _():
        upper(xa)
        lower(xb)

    for l in range(count):
        ext[l, HX:high, :] = x_own[l]

    span = rows + 2 * HX
    left, right = [], []
    for g in range(panels.shape[0]):
        group = panels[g]
        for k in range(4):
            code = group[k : k + 1].astype(jnp.int32)
            value = group[4 + k : 5 + k]
            row = code // cols - (tile * rows - HX)
            col = code % cols
            hit = row == lax.broadcasted_iota(jnp.int32, (span, 128), 0)
            left.append(jnp.where(hit, value, 0.0))
            right.append(
                jnp.where(col == lax.broadcasted_iota(jnp.int32, (cols, 128), 0), 1.0, 0.0).astype(jnp.bfloat16)
            )
    left = jnp.concatenate(left, 1)
    right = jnp.concatenate(right, 1)
    parts = lax.dot_general(
        jnp.concatenate(split(left, 3), 0), right, (((1,), (1,)), ((), ())), preferred_element_type=jnp.float32
    )
    total = parts[0:span] + parts[span : 2 * span] + parts[2 * span :]
    ext[depth - 1] = ext[depth - 1] + total

    y = lax.axis_index("strip") * lax.axis_size("sub") + lax.axis_index("sub")
    y_even = y % 2 == 0
    lane = lax.broadcasted_iota(jnp.int32, (span, 128), 1)

    def slab(g, at_right):
        out = jnp.zeros((span, 128), jnp.float32)
        for k in range(SLABS):
            if at_right:
                x = pltpu.roll(ext[SLABS * g + k, :, cols - 128 : cols], (HY + HY * k) % 128, 1)
            else:
                x = ext[SLABS * g + k, :, 0:128]
                x = pltpu.roll(x, HY * k, 1) if k else x
            out = jnp.where((lane >= HY * k) & (lane < HY * (k + 1)), x, out)
        return out

    for g in range(count // SLABS):
        to_right = slab(g, True)
        to_left = slab(g, False)
        sub_out[g] = jnp.where(y_even, to_right, to_left)
        strip_out[g] = jnp.where(y_even, to_left, to_right)


def down_kernel(
    ext, ysub, ystrip, c1, c2,
    b_out, k_out, u_out, k1_out, b1_out, u1_out, c_out, a_msg, b_msg,
    b0, u0, u0n, r0, w0, al0, be0, w1, al1, be1, u1, u1n, r1,
):
    depth = ext.shape[0] - 2
    span, cols = ext.shape[1], ext.shape[2]
    count = depth + 2
    tiles = lax.axis_size("tile")
    tile = lax.axis_index("tile")
    y_count = lax.axis_size("strip") * lax.axis_size("sub")
    y = lax.axis_index("strip") * lax.axis_size("sub") + lax.axis_index("sub")
    y_even = y % 2 == 0
    rows = span - 2 * HX
    lane = lax.broadcasted_iota(jnp.int32, (span, 128), 1)

    for g in range(count // SLABS):
        from_right = jnp.where(y_even, ysub[g], ystrip[g])
        from_left = jnp.where(y_even, ystrip[g], ysub[g])
        for k in range(SLABS):
            l = SLABS * g + k
            right = pltpu.roll(from_right, 128 - HY * k, 1) if k else from_right
            left = pltpu.roll(from_left, 128 - HY - HY * k, 1) if (128 - HY - HY * k) % 128 else from_left
            b0[l, :, 0:cols] = ext[l]
            b0[l, :, cols : cols + 128] = jnp.where(lane < HY, right, jnp.where(lane >= 128 - HY, left, 0.0))

    def inside_of(shape, first_row, row_end, own, halo):
        row = first_row + lax.broadcasted_iota(jnp.int32, shape, 0)
        column = lax.broadcasted_iota(jnp.int32, shape, 1)
        right = (column >= own) & (column < own + halo) & (y < y_count - 1)
        left = (column >= shape[1] - halo) & (y > 0)
        return (row >= 0) & (row < row_end) & ((column < own) | right | left)

    lanes = cols + 128
    kh, kv = b0[depth], b0[depth + 1]
    weights(kh, kv, 1.0, inside_of((span, lanes), tile * rows - HX, tiles * rows, cols, HY), w0, al0, be0)
    zero = jnp.zeros((span, lanes), jnp.float32)
    u0[0] = zero
    u0[depth + 1] = zero
    u0n[0] = zero
    u0n[depth + 1] = zero

    def first(z, c):
        u0[z + 1] = w0[jnp.minimum(z, 1)] * b0[z]
        return c

    loop(depth, first, 21)
    sweep(u0, u0n, u0.at[pl.ds(1, depth)], al0, be0, depth)

    low, top = 8, span - 8
    pad = r0.shape[2] - span
    for l in range(count):
        for j in range(r0.shape[1]):
            r0[l, j, span : span + pad, :] = jnp.zeros((pad, 128), jnp.float32)
    blocks_out(r0, depth, kh)
    blocks_out(r0, depth + 1, kv)
    k_out[0] = kh[low:top]
    k_out[1] = kv[low:top]

    def rest(z, c):
        b = b0[z]
        blocks_out(r0, z, residual_of(u0n, z, b, b0[depth], b0[depth + 1], 1.0))
        b_out[z] = b[low:top]
        u_out[z] = u0n[z + 1][low:top]
        return c

    loop(depth, rest, 21)

    def coarse_rows(ref, l, n):
        return jnp.concatenate(
            [
                ref[l, j, pl.ds(0, n, stride=2), :] + ref[l, j, pl.ds(1, n, stride=2), :]
                for j in range(ref.shape[1])
            ],
            1,
        )

    span1 = r0.shape[2] // 2
    half = cols
    pairs = jnp.concatenate([coarse_rows(r0, l, span1) for l in range(count)], 0)
    b1 = exact_dot(pairs, c1[...]).reshape(count, span1, half)
    b1_out[...] = b1[0:depth]
    k1_out[...] = b1[depth:]
    kh1, kv1 = k1_out[0], k1_out[1]
    weights(
        kh1, kv1, 0.25,
        inside_of((span1, half), tile * (rows // 2) - HX // 2, tiles * (rows // 2), cols // 2, HY // 2),
        w1, al1, be1,
    )
    zero1 = jnp.zeros((span1, half), jnp.float32)
    u1[0] = zero1
    u1[depth + 1] = zero1
    u1n[0] = zero1
    u1n[depth + 1] = zero1

    def first1(z, c):
        u1[z + 1] = w1[jnp.minimum(z, 1)] * b1_out[z]
        return c

    loop(depth, first1, 8)
    sweep(u1, u1n, u1.at[pl.ds(1, depth)], al1, be1, depth)

    def rest1(z, c):
        blocks_out(r1, z, residual_of(u1n, z, b1_out[z], k1_out[0], k1_out[1], 0.25))
        u1_out[z] = u1n[z + 1]
        return c

    loop(depth, rest1, 8)
    blocks_out(r1, depth, kh1)
    blocks_out(r1, depth + 1, kv1)
    span2 = span1 // 2
    pairs = jnp.concatenate([coarse_rows(r1, l, span2) for l in range(count)], 0)
    b2 = exact_dot(pairs, c2[...]).reshape(count, span2, cols // 2)
    c_out[...] = b2

    own2 = HX // 4
    rows2 = rows // 4
    even = tile % 2 == 0

    def send(out, start):
        for l in range(count):
            out[count + l // 8, l % 8 : l % 8 + 1, :] = c_out[l, start : start + 1, :]
            out[l] = c_out[l, start + 1 : start + HX2, :]

    @pl.when(even)
    def _():
        send(a_msg, own2 - 1)
        send(b_msg, own2)

    @pl.when(jnp.logical_not(even))
    def _():
        send(a_msg, own2)
        send(b_msg, own2 - 1)


def up_kernel(
    c_in, xa, xb, b0, k0, u0, k1, b1, u1, p1, p2,
    potential, residual,
    b2, w2, al2, be2, wb2, u2, u2n, w1, al1, be1, wb1, f1, f1n, w0, al0, be0, wb0, f0, f0n, e1, e0,
):
    count = c_in.shape[0]
    depth = count - 2
    cols = potential.shape[2]
    rows = potential.shape[1]
    rows2 = rows // 4
    tiles = lax.axis_size("tile")
    tile = lax.axis_index("tile")
    y_count = lax.axis_size("strip") * lax.axis_size("sub")
    y = lax.axis_index("strip") * lax.axis_size("sub") + lax.axis_index("sub")
    even = tile % 2 == 0
    own2 = HX // 4
    span2 = b2.shape[1]
    end2 = rows2 + 2 * HX2

    def inside_of(shape, first_row, row_end, own, halo):
        row = first_row + lax.broadcasted_iota(jnp.int32, shape, 0)
        column = lax.broadcasted_iota(jnp.int32, shape, 1)
        right = (column >= own) & (column < own + halo) & (y < y_count - 1)
        left = (column >= shape[1] - halo) & (y > 0)
        return (row >= 0) & (row < row_end) & ((column < own) | right | left)

    def put(x, start):
        for l in range(count):
            b2[l, start : start + 1, :] = x[count + l // 8, l % 8 : l % 8 + 1, :]
            b2[l, start + 1 : start + HX2, :] = x[l]

    @pl.when(even)
    def _():
        put(xa, HX2 + rows2)
        put(xb, 0)

    @pl.when(jnp.logical_not(even))
    def _():
        put(xa, 0)
        put(xb, HX2 + rows2)

    lanes2 = b2.shape[2]
    for l in range(count):
        b2[l, HX2 : HX2 + rows2, :] = c_in[l, own2 : own2 + rows2, :]
        b2[l, end2:span2, :] = jnp.zeros((span2 - end2, lanes2), jnp.float32)
    row = lax.broadcasted_iota(jnp.int32, (span2, lanes2), 0)
    inside2 = inside_of((span2, lanes2), tile * rows2 - HX2, tiles * rows2, cols // 4, (HY - 2) // 4)
    weights(b2[depth], b2[depth + 1], 0.0625, inside2 & (row < end2), w2, al2, be2)

    def zero_ends(ref):
        z = jnp.zeros(ref.shape[1:], jnp.float32)
        ref[0] = z
        ref[depth + 1] = z

    for ref in (u2, u2n, f1, f1n, f0, f0n):
        zero_ends(ref)

    def first2(z, c):
        v = w2[jnp.minimum(z, 1)] * b2[z]
        wb2[z] = v
        u2[z + 1] = v
        return c

    loop(depth, first2, 4)
    src, dst = u2, u2n
    for _ in range(COARSE - 1):
        sweep(src, dst, wb2, al2, be2, depth)
        src, dst = dst, src

    span1, lanes1 = u1.shape[1], u1.shape[2]
    kh1, kv1 = k1[0], k1[1]
    weights(
        kh1, kv1, 0.25,
        inside_of((span1, lanes1), tile * (rows // 2) - HX // 2, tiles * (rows // 2), cols // 2, HY // 2),
        w1, al1, be1,
    )
    off2 = HX2 - own2
    coarse = jnp.concatenate([src[z + 1][off2 : off2 + span1 // 2] for z in range(depth)], 0)
    fine = exact_dot(coarse, p2[...])
    for z in range(depth):
        rows_doubled(e1, z, fine[z * (span1 // 2) : (z + 1) * (span1 // 2)])

    def first1(z, c):
        f1[z + 1] = u1[z] + blocks_in(e1, z)
        wb1[z] = w1[jnp.minimum(z, 1)] * b1[z]
        return c

    loop(depth, first1, 8)
    sweep(f1, f1n, wb1, al1, be1, depth)
    sweep(f1n, f1, wb1, al1, be1, depth)

    span0, lanes0 = b0.shape[1], b0.shape[2]
    above = (span0 - rows) // 2
    weights(
        k0[0], k0[1], 1.0,
        inside_of((span0, lanes0), tile * rows - above, tiles * rows, cols, HY),
        w0, al0, be0,
    )
    off1 = (HX - above) // 2
    fine = exact_dot(f1[pl.ds(1, depth)].reshape(depth * span1, lanes1), p1[...])
    for z in range(depth):
        rows_doubled(e0, z, fine[z * span1 + off1 : z * span1 + off1 + span0 // 2])

    def first0(z, c):
        f0[z + 1] = u0[z] + blocks_in(e0, z)
        wb0[z] = w0[jnp.minimum(z, 1)] * b0[z]
        return c

    loop(depth, first0, 15)
    sweep(f0, f0n, wb0, al0, be0, depth)
    sweep(f0n, f0, wb0, al0, be0, depth)

    def last(z, c):
        r = residual_of(f0, z, b0[z], k0[0], k0[1], 1.0)
        residual[z] = r[above : above + rows, 0:cols]
        potential[z] = f0[z + 1][above : above + rows, 0:cols]
        return c

    loop(depth, last, 15)


VM = pl.BlockSpec(memory_space=pltpu.VMEM)


def call(kernel, outs, scratch, *args):
    f32 = lambda shape: jax.ShapeDtypeStruct(shape, jnp.float32)
    return pl.pallas_call(
        kernel,
        out_shape=[f32(s) for s in outs],
        in_specs=[VM] * len(args),
        out_specs=[VM] * len(outs),
        scratch_shapes=[pltpu.VMEM(s, jnp.float32) for s in scratch],
        compiler_params=pltpu.CompilerParams(vmem_limit_bytes=40 << 20),
    )(*args)


def body(right_side, horiz_coef, vert_coef, panel_owner, panel_cell, panel_pressure):
    depth, rows, cols = right_side.shape
    tiles = lax.axis_size("tile")
    y_axes = ("strip", "sub")
    y_count = lax.axis_size("strip") * lax.axis_size("sub")
    count = depth + 2
    span = rows + 2 * HX
    one, two = lane_maps(cols)
    c1 = jnp.asarray(0.25 * selection(one, cols), jnp.bfloat16)
    c2 = jnp.asarray(0.25 * selection(two, cols // 2), jnp.bfloat16)
    p1 = jnp.asarray(selection(one, cols).T, jnp.bfloat16)
    p2 = jnp.asarray(selection(two, cols // 2).T, jnp.bfloat16)

    message = (count + count // 2, 8, cols)
    f32 = lambda shape: jax.ShapeDtypeStruct(shape, jnp.float32)
    x_own, panels, a, b = pl.pallas_call(
        load_kernel,
        out_shape=[f32((count, rows, cols)), f32((1, 8, 128)), f32(message), f32(message)],
        in_specs=[pl.BlockSpec(memory_space=pltpu.HBM)] * 6,
        out_specs=[VM] * 4,
        scratch_shapes=[pltpu.VMEM((2, 4, 128), jnp.int32), pltpu.SemaphoreType.DMA((6,))],
        compiler_params=pltpu.CompilerParams(vmem_limit_bytes=8 << 20),
    )(
        *[
            pltpu.with_memory_space_constraint(x, pltpu.HBM)
            for x in (
                right_side, horiz_coef, vert_coef,
                panel_owner.reshape(4, -1), panel_cell.reshape(4, -1), panel_pressure.reshape(4, -1),
            )
        ]
    )
    near = lax.ppermute(panels, "tile", [(i, i ^ 1) for i in range(tiles)])
    a = neighbour_swap(a, "tile", 0, "sub")
    b = neighbour_swap(b, "tile", 1, "sub")
    panels = jnp.concatenate([panels, near], 0)
    step = 2
    while step < tiles:
        swap = [(i, i ^ step) for i in range(tiles)]
        panels = jnp.concatenate([panels, lax.ppermute(panels, "tile", swap)], 0)
        step *= 2

    slabs = (count // SLABS, span, 128)
    ext, sub, strip = call(
        forcing_kernel, [(count, span, cols), slabs, slabs], [],
        x_own, a, b, panels,
    )
    sub = neighbour_swap(sub, y_axes, 0, "group")
    strip = neighbour_swap(strip, y_axes, 1, "group")

    lanes = cols + 128
    small = span - 16
    span1 = (span + 8) // 2
    span2 = span1 // 2
    message2 = (count + (count + 7) // 8, 8, cols // 2)
    field = (depth + 2, span, lanes)
    field1 = (depth + 2, span1, cols)
    pair, pair1 = (2, span, lanes), (2, span1, cols)
    b0, k0, u0, k1, b1, u1, c2_own, a2, b2 = call(
        down_kernel,
        [
            (depth, small, lanes), (2, small, lanes), (depth, small, lanes), (2, span1, cols),
            (depth, span1, cols), (depth, span1, cols), (count, span2, cols // 2), message2, message2,
        ],
        [
            (count, span, lanes), field, field, (count, lanes // 128, span + 8, 128), pair, pair, pair,
            pair1, pair1, pair1, field1, field1, (count, cols // 128, span1, 128),
        ],
        ext, sub, strip, c1, c2,
    )
    a2 = neighbour_swap(a2, "tile", 0, "sub")
    b2 = neighbour_swap(b2, "tile", 1, "sub")

    wide2 = 32
    pair2, pair0 = (2, wide2, cols // 2), (2, small, lanes)
    field2 = (depth + 2, wide2, cols // 2)
    field0 = (depth + 2, small, lanes)
    potential, residual = call(
        up_kernel, [right_side.shape, right_side.shape],
        [
            (count, wide2, cols // 2), pair2, pair2, pair2, (depth, wide2, cols // 2), field2, field2,
            pair1, pair1, pair1, (depth, span1, cols), field1, field1,
            pair0, pair0, pair0, (depth, small, lanes), field0, field0,
            (depth, cols // 128, span1, 128), (depth, lanes // 128, small, 128),
        ],
        c2_own, a2, b2, b0, k0, u0, k1, b1, u1, p1, p2,
    )
    return potential, residual


def solution(mesh):
    return jax.shard_map(
        body,
        mesh=mesh,
        in_specs=(
            jax.P("group", "tile", ("strip", "sub")),
            jax.P(("group", "tile"), ("strip", "sub")),
            jax.P(("group", "tile"), ("strip", "sub")),
            jax.P(("group", "tile", "strip", "sub"), None),
            jax.P(("group", "tile", "strip", "sub")),
            jax.P(("group", "tile", "strip", "sub")),
        ),
        out_specs=(
            jax.P("group", "tile", ("strip", "sub")),
            jax.P("group", "tile", ("strip", "sub")),
        ),
        check_vma=False,
    )
```

```python
import jax
import jax.numpy as jnp
import numpy as np
from jax import lax
from jax.experimental import pallas as pl
from jax.experimental.pallas import tpu as pltpu

COARSE = 8
OMEGA = 0.8

HX = 12
HX2 = 9
HY = 42
LIMIT = 512
SLABS = 3
EDGE = 16


def neighbour_swap(x, axis, odd, spare):
    axis = axis if isinstance(axis, tuple) else (axis,)
    count = lax.axis_size(axis)
    twins = lax.axis_size(spare)
    leading = spare == "group"
    place = lambda i, twin: twin * count + i if leading else i * twins + twin
    pairs = []
    for twin in range(twins):
        for i in range(count):
            j, other = (i + 1 if i % 2 == odd else i - 1), twin
            if not 0 <= j < count:
                j, other = i, twin ^ 1
            pairs.append((place(i, twin), place(j, other)))
    return lax.ppermute(x, (spare,) + axis if leading else axis + (spare,), pairs)


def lane_maps(cols):
    half, quarter, h1, h2 = cols // 2, cols // 4, HY // 2, HY // 4
    wide1 = -np.ones(cols + 128, np.int64)
    wide1[:cols] = np.arange(cols) // 2
    wide1[cols : cols + HY] = half + np.arange(HY) // 2
    wide1[cols + 128 - HY :] = 2 * half - h1 + np.arange(HY) // 2
    wide2 = -np.ones(2 * half, np.int64)
    wide2[:half] = np.arange(half) // 2
    wide2[half : half + 2 * h2] = quarter + np.arange(2 * h2) // 2
    wide2[2 * half - 2 * h2 :] = 2 * quarter - h2 + np.arange(2 * h2) // 2
    inner2 = -np.ones(half, np.int64)
    inner2[4 : half - 4] = np.arange(4, half - 4) // 2
    edge1 = -np.ones(128, np.int64)
    edge1[: 2 * HY + EDGE] = np.arange(2 * HY + EDGE) // 2
    edge1[128 - EDGE :] = 128 - EDGE // 2 + np.arange(EDGE) // 2
    edge2 = -np.ones(128, np.int64)
    edge2[: 2 * h2] = quarter + np.arange(2 * h2) // 2
    edge2[2 * h1 - 2 * h2 : 2 * h1] = 2 * quarter - h2 + np.arange(2 * h2) // 2
    edge2[2 * h1 : 2 * h1 + 4] = np.arange(4) // 2
    edge2[124:] = quarter - 2 + np.arange(4) // 2
    return wide1, wide2, inner2, edge1, edge2


def selection(lanes, width):
    return (lanes[:, None] == np.arange(width)[None, :]).astype(np.float32)


def split(x, parts):
    out = []
    for _ in range(parts):
        out.append(x.astype(jnp.bfloat16))
        x = x - out[-1].astype(jnp.float32)
    return out


def exact_dot(left, right):
    return sum(jnp.dot(part, right, preferred_element_type=jnp.float32) for part in split(left, 2))


def neighbours(u):
    rows, lanes = u.shape
    return (
        pltpu.roll(u, 1, 0)
        + pltpu.roll(u, rows - 1, 0)
        + pltpu.roll(u, 1, 1)
        + pltpu.roll(u, lanes - 1, 1)
    )


def weights(kh, kv, scale, inside, w_ref, a_ref, b_ref):
    for i, layers in enumerate((1.0, 2.0)):
        diag = 4.0 * scale * kh + layers * kv
        w = jnp.where(inside, OMEGA / jnp.where(inside, diag, 1.0), 0.0)
        if w_ref is not None:
            w_ref[i] = w
        a_ref[i] = w * (scale * kh)
        b_ref[i] = w * kv


def loop(depth, fn, vregs):
    lax.fori_loop(0, depth, fn, 0, unroll=max(1, min(depth, LIMIT // vregs)))


def sweep(src, dst, wb, a_ref, b_ref, depth):
    def layer(z, c):
        i = jnp.minimum(z, 1)
        u = src[z + 1]
        dst[z + 1] = (
            (1.0 - OMEGA) * u
            + wb[z]
            + a_ref[i] * neighbours(u)
            + b_ref[i] * (src[z] + src[z + 2])
        )
        return c

    loop(depth, layer, src.shape[1] * src.shape[2] // 1024)


def residual_of(src, z, b, kh, kv, scale, lanes=None):
    layers = jnp.where(z == 0, 1.0, 2.0)
    u = src[z + 1]
    around = neighbours(u)[:, :lanes]
    u = u[:, :lanes]
    return b + (scale * kh) * (around - 4.0 * u) + kv * (src[z, :, :lanes] + src[z + 2, :, :lanes] - layers * u)


def blocks_out(ref, l, x):
    for j in range(ref.shape[1]):
        ref[l, j, 0 : x.shape[0], :] = x[:, 128 * j : 128 * (j + 1)]


def blocks_in(ref, l):
    return jnp.concatenate([ref[l, j] for j in range(ref.shape[1])], 1)


def rows_doubled(ref, l, part):
    n = part.shape[0]
    for j in range(ref.shape[1]):
        for s in (0, 1):
            ref[l, j, pl.ds(s, n, stride=2), :] = part[:, 128 * j : 128 * (j + 1)]


def load_kernel(rs, kh, kv, owner, cell, pressure, x, panels, a_out, b_out, ints, sems):
    depth, rows, cols = rs.shape
    count = depth + 2
    half = count // 2
    even = lax.axis_index("tile") % 2 == 0
    copies = [
        pltpu.make_async_copy(src, dst, sems.at[i])
        for i, (src, dst) in enumerate(
            (
                (owner, ints.at[0]),
                (cell, ints.at[1]),
                (pressure, panels.at[0, pl.ds(4, 4)]),
                (rs, x.at[pl.ds(0, depth)]),
                (kh, x.at[depth]),
                (kv, x.at[depth + 1]),
            )
        )
    ]
    for copy in copies:
        copy.start()
    for copy in copies:
        copy.wait()
    panels[0, 0:4, :] = (ints[0] * (rows * cols) + ints[1]).astype(jnp.float32)

    def first(out):
        for l in range(count):
            out[l] = x[l, 0:8, :]
            out[count + l % half, 4 * (l // half) : 4 * (l // half) + 4, :] = x[l, 8:HX, :]

    def last(out):
        for l in range(count):
            out[l] = x[l, rows - 8 : rows, :]
            out[count + l % half, 4 * (l // half) : 4 * (l // half) + 4, :] = x[l, rows - HX : rows - 8, :]

    @pl.when(even)
    def _():
        last(a_out)
        first(b_out)

    @pl.when(jnp.logical_not(even))
    def _():
        first(a_out)
        last(b_out)


def forcing_kernel(x_own, xa, xb, panels, ext, sub_out, strip_out):
    count, rows, cols = x_own.shape
    depth = count - 2
    half = count // 2
    tile = lax.axis_index("tile")
    even = tile % 2 == 0
    high = rows + HX

    def upper(x):
        for l in range(count):
            ext[l, 0:4, :] = x[count + l % half, 4 * (l // half) : 4 * (l // half) + 4, :]
            ext[l, 4:HX, :] = x[l]

    def lower(x):
        for l in range(count):
            ext[l, high : high + 8, :] = x[l]
            ext[l, high + 8 : high + HX, :] = x[count + l % half, 4 * (l // half) : 4 * (l // half) + 4, :]

    @pl.when(even)
    def _():
        lower(xa)
        upper(xb)

    @pl.when(jnp.logical_not(even))
    def _():
        upper(xa)
        lower(xb)

    for l in range(count):
        ext[l, HX:high, :] = x_own[l]

    span = rows + 2 * HX
    left, right = [], []
    for g in range(panels.shape[0]):
        group = panels[g]
        for k in range(4):
            code = group[k : k + 1].astype(jnp.int32)
            value = group[4 + k : 5 + k]
            row = code // cols - (tile * rows - HX)
            col = code % cols
            hit = row == lax.broadcasted_iota(jnp.int32, (span, 128), 0)
            left.append(jnp.where(hit, value, 0.0))
            right.append(
                jnp.where(col == lax.broadcasted_iota(jnp.int32, (cols, 128), 0), 1.0, 0.0).astype(jnp.bfloat16)
            )
    left = jnp.concatenate(left, 1)
    right = jnp.concatenate(right, 1)
    parts = lax.dot_general(
        jnp.concatenate(split(left, 3), 0), right, (((1,), (1,)), ((), ())), preferred_element_type=jnp.float32
    )
    total = parts[0:span] + parts[span : 2 * span] + parts[2 * span :]
    ext[depth - 1] = ext[depth - 1] + total

    y = lax.axis_index("strip") * lax.axis_size("sub") + lax.axis_index("sub")
    y_even = y % 2 == 0
    lane = lax.broadcasted_iota(jnp.int32, (span, 128), 1)

    def slab(g, at_right):
        out = jnp.zeros((span, 128), jnp.float32)
        for k in range(SLABS):
            if at_right:
                x = pltpu.roll(ext[SLABS * g + k, :, cols - 128 : cols], (HY + HY * k) % 128, 1)
            else:
                x = ext[SLABS * g + k, :, 0:128]
                x = pltpu.roll(x, HY * k, 1) if k else x
            out = jnp.where((lane >= HY * k) & (lane < HY * (k + 1)), x, out)
        return out

    for g in range(count // SLABS):
        to_right = slab(g, True)
        to_left = slab(g, False)
        sub_out[g] = jnp.where(y_even, to_right, to_left)
        strip_out[g] = jnp.where(y_even, to_left, to_right)


def row_inside(shape, rows, above):
    row = lax.axis_index("tile") * rows - above + lax.broadcasted_iota(jnp.int32, shape, 0)
    return (row >= 0) & (row < lax.axis_size("tile") * rows)


def y_sides():
    y = lax.axis_index("strip") * lax.axis_size("sub") + lax.axis_index("sub")
    return y > 0, y < lax.axis_size("strip") * lax.axis_size("sub") - 1, y % 2 == 0


def wide_inside(shape, rows, above, own, halo):
    has_left, has_right, _ = y_sides()
    column = lax.broadcasted_iota(jnp.int32, shape, 1)
    right = (column >= own) & (column < own + halo) & has_right
    left = (column >= shape[1] - halo) & has_left
    return row_inside(shape, rows, above) & ((column < own) | right | left)


def edge_inside(shape, rows, above, halo, edge):
    has_left, has_right, _ = y_sides()
    column = lax.broadcasted_iota(jnp.int32, shape, 1)
    right = (column < halo) & has_right
    left = (column >= halo) & (column < 2 * halo) & has_left
    own = ((column >= 2 * halo) & (column < 2 * halo + edge)) | (column >= 128 - edge)
    return row_inside(shape, rows, above) & (own | right | left)


def zero_ends(*refs):
    for ref in refs:
        ref[0] = jnp.zeros(ref.shape[1:], jnp.float32)
        ref[ref.shape[0] - 1] = jnp.zeros(ref.shape[1:], jnp.float32)


def presmooth(source, kh, kv, scale, inside, w, al, be, u, un, depth):
    weights(kh, kv, scale, inside, w, al, be)
    zero_ends(u, un)

    def first(z, c):
        u[z + 1] = w[jnp.minimum(z, 1)] * source[z]
        return c

    loop(depth, first, u.shape[1] * u.shape[2] // 1024)
    sweep(u, un, u.at[pl.ds(1, depth)], al, be, depth)


def restrict(source, un, scale, r, depth, parts):
    kh, kv = source[depth], source[depth + 1]
    rows = kh.shape[0]
    for l in range(depth + 2):
        for j in range(r.shape[1]):
            if r.shape[2] > rows:
                r[l, j, rows:, :] = jnp.zeros((r.shape[2] - rows, 128), jnp.float32)
    blocks_out(r, depth, kh)
    blocks_out(r, depth + 1, kv)

    def rest(z, c):
        blocks_out(r, z, residual_of(un, z, source[z], source[depth], source[depth + 1], scale))
        return c

    loop(depth, rest, rows * kh.shape[1] // 1024)
    n = r.shape[2] // 2
    pairs = jnp.concatenate(
        [
            jnp.concatenate(
                [r[l, j, pl.ds(0, n, stride=2), :] + r[l, j, pl.ds(1, n, stride=2), :] for j in range(r.shape[1])], 1
            )
            for l in range(depth + 2)
        ],
        0,
    )
    return exact_dot(pairs, parts).reshape(depth + 2, n, parts.shape[1])


def inner_kernel(
    ext, c1, c2, u_out, b1_out, u1_out, c_out,
    w0, al0, be0, u0, u0n, r0, w1, al1, be1, u1, u1n, r1,
):
    depth, span, cols = ext.shape[0] - 2, ext.shape[1], ext.shape[2]
    rows = span - 2 * HX
    presmooth(
        ext, ext[depth], ext[depth + 1], 1.0, row_inside((span, cols), rows, HX), w0, al0, be0, u0, u0n, depth
    )
    for z in range(depth):
        u_out[z] = u0n[z + 1, 8 : span - 8, :]
    b1_out[...] = restrict(ext, u0n, 1.0, r0, depth, c1[...])
    span1, half = b1_out.shape[1], b1_out.shape[2]
    presmooth(
        b1_out, b1_out[depth], b1_out[depth + 1], 0.25, row_inside((span1, half), rows // 2, HX // 2),
        w1, al1, be1, u1, u1n, depth,
    )
    u1_out[...] = u1n[pl.ds(1, depth)]
    c_out[...] = restrict(b1_out, u1n, 0.25, r1, depth, c2[...])


def edge_kernel(
    ext, ysub, ystrip, c_inner, c1, c2,
    b_out, u_out, b1_out, u1_out, c_out, a_msg, b_msg,
    w0, al0, be0, u0, u0n, r0, w1, al1, be1, u1, u1n, r1,
):
    depth, span, cols = ext.shape[0] - 2, ext.shape[1], ext.shape[2]
    rows = span - 2 * HX
    count = depth + 2
    even = lax.axis_index("tile") % 2 == 0
    _, _, y_even = y_sides()
    lane = lax.broadcasted_iota(jnp.int32, (span, 128), 1)

    def rolled(x, shift):
        return pltpu.roll(x, shift % 128, 1) if shift % 128 else x

    for g in range(count // SLABS):
        from_right = jnp.where(y_even, ysub[g], ystrip[g])
        from_left = jnp.where(y_even, ystrip[g], ysub[g])
        for k in range(SLABS):
            l = SLABS * g + k
            x = jnp.where(lane >= 128 - EDGE, ext[l, :, cols - 128 : cols], 0.0)
            x = jnp.where((lane >= 2 * HY) & (lane < 2 * HY + EDGE), rolled(ext[l, :, 0:128], 2 * HY), x)
            x = jnp.where((lane >= HY) & (lane < 2 * HY), rolled(from_left, HY - HY * k), x)
            b_out[l] = jnp.where(lane < HY, rolled(from_right, -HY * k), x)
    presmooth(
        b_out, b_out[depth], b_out[depth + 1], 1.0, edge_inside((span, 128), rows, HX, HY, EDGE),
        w0, al0, be0, u0, u0n, depth,
    )
    for z in range(depth):
        u_out[z] = u0n[z + 1, 8 : span - 8, :]
    b1_out[...] = restrict(b_out, u0n, 1.0, r0, depth, c1[...])
    span1 = b1_out.shape[1]
    presmooth(
        b1_out, b1_out[depth], b1_out[depth + 1], 0.25,
        edge_inside((span1, 128), rows // 2, HX // 2, HY // 2, EDGE // 2),
        w1, al1, be1, u1, u1n, depth,
    )
    u1_out[...] = u1n[pl.ds(1, depth)]
    c_out[...] = c_inner[...] + restrict(b1_out, u1n, 0.25, r1, depth, c2[...])
    own2 = HX // 4

    def send(out, start):
        for l in range(count):
            out[count + l // 8, l % 8 : l % 8 + 1, :] = c_out[l, start : start + 1, :]
            out[l] = c_out[l, start + 1 : start + HX2, :]

    @pl.when(even)
    def _():
        send(a_msg, own2 - 1)
        send(b_msg, own2)

    @pl.when(jnp.logical_not(even))
    def _():
        send(a_msg, own2)
        send(b_msg, own2 - 1)


def join_kernel(
    ext, edge, u_in, u_edge, b1_in, b1_edge, u1_in, u1_edge,
    k0, u0, wb0, al0, be0, u1, wb1, al1, be1, w0, w1,
):
    depth, small, cols = u_in.shape
    span = ext.shape[1]
    rows = span - 2 * HX

    def joined(inner, strip, halo, edge, patch):
        own = inner.shape[1]
        lane = lax.broadcasted_iota(jnp.int32, strip.shape, 1)
        turned = pltpu.roll(strip, 128 - 2 * halo, 1)
        outer = jnp.where(lane < halo, strip, jnp.where(lane >= 128 - halo, turned, 0.0))
        blocks = [inner[:, 128 * j : 128 * (j + 1)] for j in range(own // 128)]
        blocks[0] = jnp.where(lane < patch, turned, blocks[0])
        blocks[-1] = jnp.where(lane >= 128 - patch, strip, blocks[-1])
        return jnp.concatenate(blocks + [outer], 1)

    part0 = lambda inner, strip: joined(inner, strip, HY, EDGE, EDGE // 2)
    part1 = lambda inner, strip: joined(inner, strip, HY // 2, EDGE // 2, EDGE // 4)
    low, top = 8, span - 8
    lanes = cols + 128
    for i in (0, 1):
        k0[i] = part0(ext[depth + i, low:top, :], edge[depth + i, low:top, :])
    weights(
        k0[0], k0[1], 1.0, wide_inside((small, lanes), rows, HX - low, cols, HY), w0, al0, be0,
    )
    span1, half = b1_in.shape[1], b1_in.shape[2]
    kh1, kv1 = (part1(b1_in[depth + i], b1_edge[depth + i]) for i in (0, 1))
    weights(
        kh1, kv1, 0.25, wide_inside((span1, 2 * half), rows // 2, HX // 2, half, HY // 2), w1, al1, be1,
    )
    for z in range(depth):
        i = min(z, 1)
        u0[z] = part0(u_in[z], u_edge[z])
        wb0[z] = w0[i] * part0(ext[z, low:top, :], edge[z, low:top, :])
        u1[z] = part1(u1_in[z], u1_edge[z])
        wb1[z] = w1[i] * part1(b1_in[z], b1_edge[z])


def up_kernel(
    c_in, xa, xb, ext, k0, u0, wb0, al0, be0, u1, wb1, al1, be1, p1, p2,
    potential, residual,
    b2, w2, al2, be2, wb2, u2, u2n, f1, f1n, f0, f0n, e1, e0, pot, res, sems,
):
    count = c_in.shape[0]
    depth = count - 2
    rows, cols = potential.shape[1:]
    rows2 = rows // 4
    even = lax.axis_index("tile") % 2 == 0
    own2 = HX // 4
    span2 = b2.shape[1]
    end2 = rows2 + 2 * HX2

    def put(x, start):
        for l in range(count):
            b2[l, start : start + 1, :] = x[count + l // 8, l % 8 : l % 8 + 1, :]
            b2[l, start + 1 : start + HX2, :] = x[l]

    @pl.when(even)
    def _():
        put(xa, HX2 + rows2)
        put(xb, 0)

    @pl.when(jnp.logical_not(even))
    def _():
        put(xa, 0)
        put(xb, HX2 + rows2)

    lanes2 = b2.shape[2]
    for l in range(count):
        b2[l, HX2 : HX2 + rows2, :] = c_in[l, own2 : own2 + rows2, :]
        b2[l, end2:span2, :] = jnp.zeros((span2 - end2, lanes2), jnp.float32)
    row = lax.broadcasted_iota(jnp.int32, (span2, lanes2), 0)
    inside2 = wide_inside((span2, lanes2), rows2, HX2, cols // 4, HY // 4)
    weights(b2[depth], b2[depth + 1], 0.0625, inside2 & (row < end2), w2, al2, be2)
    zero_ends(u2, u2n, f1, f1n, f0, f0n)

    def first2(z, c):
        v = w2[jnp.minimum(z, 1)] * b2[z]
        wb2[z] = v
        u2[z + 1] = v
        return c

    loop(depth, first2, 4)
    src, dst = u2, u2n
    for _ in range(COARSE - 1):
        sweep(src, dst, wb2, al2, be2, depth)
        src, dst = dst, src

    span1, lanes1 = u1.shape[1], u1.shape[2]
    off2 = HX2 - own2
    coarse = jnp.concatenate([src[z + 1][off2 : off2 + span1 // 2] for z in range(depth)], 0)
    fine = exact_dot(coarse, p2[...])
    for z in range(depth):
        rows_doubled(e1, z, fine[z * (span1 // 2) : (z + 1) * (span1 // 2)])

    def first1(z, c):
        f1[z + 1] = u1[z] + blocks_in(e1, z)
        return c

    loop(depth, first1, 8)
    sweep(f1, f1n, wb1, al1, be1, depth)
    sweep(f1n, f1, wb1, al1, be1, depth)

    span0, lanes0 = u0.shape[1], u0.shape[2]
    above = (span0 - rows) // 2
    off1 = (HX - above) // 2
    fine = exact_dot(f1[pl.ds(1, depth)].reshape(depth * span1, lanes1), p1[...])
    for z in range(depth):
        rows_doubled(e0, z, fine[z * span1 + off1 : z * span1 + off1 + span0 // 2])

    def first0(z, c):
        f0[z + 1] = u0[z] + blocks_in(e0, z)
        return c

    loop(depth, first0, 15)
    sweep(f0, f0n, wb0, al0, be0, depth)
    sweep(f0n, f0, wb0, al0, be0, depth)

    copies = []

    def ship(src, dst, first, n):
        copy = pltpu.make_async_copy(src.at[pl.ds(first, n)], dst.at[pl.ds(first, n)], sems.at[len(copies)])
        copy.start()
        copies.append(copy)

    for z in range(depth):
        pot[z] = f0[z + 1, above : above + rows, 0:cols]
    ship(pot, potential, 0, depth)
    chunk = depth // 4
    for z in range(depth):
        b = ext[z, HX - above : HX - above + span0, :]
        r = residual_of(f0, z, b, k0[0, :, 0:cols], k0[1, :, 0:cols], 1.0, cols)
        res[z] = r[above : above + rows]
        if z % chunk == chunk - 1:
            ship(res, residual, z + 1 - chunk, chunk)
    for copy in copies:
        copy.wait()


VM = pl.BlockSpec(memory_space=pltpu.VMEM)


def call(kernel, outs, scratch, *args):
    f32 = lambda shape: jax.ShapeDtypeStruct(shape, jnp.float32)
    return pl.pallas_call(
        kernel,
        out_shape=[f32(s) for s in outs],
        in_specs=[VM] * len(args),
        out_specs=[VM] * len(outs),
        scratch_shapes=[pltpu.VMEM(s, jnp.float32) for s in scratch],
        compiler_params=pltpu.CompilerParams(vmem_limit_bytes=24 << 20),
    )(*args)


def body(right_side, horiz_coef, vert_coef, panel_owner, panel_cell, panel_pressure):
    depth, rows, cols = right_side.shape
    tiles = lax.axis_size("tile")
    y_axes = ("strip", "sub")
    y_count = lax.axis_size("strip") * lax.axis_size("sub")
    count = depth + 2
    span = rows + 2 * HX
    wide1, wide2, inner2, edge1, edge2 = lane_maps(cols)
    mean = lambda lanes, width: jnp.asarray(0.25 * selection(lanes, width), jnp.bfloat16)
    spread = lambda lanes, width: jnp.asarray(selection(lanes, width).T, jnp.bfloat16)
    c1_inner, c2_inner = mean(wide1[:cols], cols // 2), mean(inner2, cols // 2)
    c1_edge, c2_edge = mean(edge1, 128), mean(edge2, cols // 2)
    p1, p2 = spread(wide1, cols), spread(wide2, cols // 2)

    message = (count + count // 2, 8, cols)
    f32 = lambda shape: jax.ShapeDtypeStruct(shape, jnp.float32)
    x_own, panels, a, b = pl.pallas_call(
        load_kernel,
        out_shape=[f32((count, rows, cols)), f32((1, 8, 128)), f32(message), f32(message)],
        in_specs=[pl.BlockSpec(memory_space=pltpu.HBM)] * 6,
        out_specs=[VM] * 4,
        scratch_shapes=[pltpu.VMEM((2, 4, 128), jnp.int32), pltpu.SemaphoreType.DMA((6,))],
        compiler_params=pltpu.CompilerParams(vmem_limit_bytes=8 << 20),
    )(
        *[
            pltpu.with_memory_space_constraint(x, pltpu.HBM)
            for x in (
                right_side, horiz_coef, vert_coef,
                panel_owner.reshape(4, -1), panel_cell.reshape(4, -1), panel_pressure.reshape(4, -1),
            )
        ]
    )
    near = lax.ppermute(panels, "tile", [(i, i ^ 1) for i in range(tiles)])
    a = neighbour_swap(a, "tile", 0, "sub")
    b = neighbour_swap(b, "tile", 1, "sub")
    panels = jnp.concatenate([panels, near], 0)
    step = 2
    while step < tiles:
        swap = [(i, i ^ step) for i in range(tiles)]
        panels = jnp.concatenate([panels, lax.ppermute(panels, "tile", swap)], 0)
        step *= 2

    slabs = (count // SLABS, span, 128)
    ext, sub, strip = call(
        forcing_kernel, [(count, span, cols), slabs, slabs], [],
        x_own, a, b, panels,
    )
    sub = neighbour_swap(sub, y_axes, 0, "group")
    strip = neighbour_swap(strip, y_axes, 1, "group")

    lanes, half = cols + 128, cols // 2
    small = span - 16
    span1 = (span + 8) // 2
    span2 = span1 // 2

    def down_scratch(width, width1):
        return (
            [(2, span, width)] * 3 + [(depth + 2, span, width)] * 2 + [(count, width // 128, span + 8, 128)]
            + [(2, span1, width1)] * 3 + [(depth + 2, span1, width1)] * 2 + [(count, width1 // 128, span1, 128)]
        )

    u_in, b1_in, u1_in, c_in = call(
        inner_kernel,
        [(depth, small, cols), (count, span1, half), (depth, span1, half), (count, span2, half)],
        down_scratch(cols, half),
        ext, c1_inner, c2_inner,
    )
    message2 = (count + (count + 7) // 8, 8, half)
    edge, u_edge, b1_edge, u1_edge, c_own, a2, b2 = call(
        edge_kernel,
        [
            (count, span, 128), (depth, small, 128), (count, span1, 128), (depth, span1, 128),
            (count, span2, half), message2, message2,
        ],
        down_scratch(128, 128),
        ext, sub, strip, c_in, c1_edge, c2_edge,
    )
    a2 = neighbour_swap(a2, "tile", 0, "sub")
    b2 = neighbour_swap(b2, "tile", 1, "sub")

    pair0, field = (2, small, lanes), (depth, small, lanes)
    pair1, field1 = (2, span1, cols), (depth, span1, cols)
    state = call(
        join_kernel,
        [pair0, field, field, pair0, pair0, field1, field1, pair1, pair1],
        [pair0, pair1],
        ext, edge, u_in, u_edge, b1_in, b1_edge, u1_in, u1_edge,
    )

    wide2 = 32
    field2 = (depth + 2, wide2, half)
    own = right_side.shape
    potential, residual = pl.pallas_call(
        up_kernel,
        out_shape=[f32(own), f32(own)],
        in_specs=[VM] * (6 + len(state)),
        out_specs=[pl.BlockSpec(memory_space=pltpu.HBM)] * 2,
        scratch_shapes=[
            pltpu.VMEM(shape, jnp.float32)
            for shape in (
                (count, wide2, half), (2, wide2, half), (2, wide2, half), (2, wide2, half), (depth, wide2, half),
                field2, field2, (depth + 2, span1, cols), (depth + 2, span1, cols),
                (depth + 2, small, lanes), (depth + 2, small, lanes),
                (depth, cols // 128, span1, 128), (depth, lanes // 128, small, 128), own, own,
            )
        ]
        + [pltpu.SemaphoreType.DMA((5,))],
        compiler_params=pltpu.CompilerParams(vmem_limit_bytes=24 << 20),
    )(c_own, a2, b2, ext, *state, p1, p2)
    return potential, residual


def solution(mesh):
    return jax.shard_map(
        body,
        mesh=mesh,
        in_specs=(
            jax.P("group", "tile", ("strip", "sub")),
            jax.P(("group", "tile"), ("strip", "sub")),
            jax.P(("group", "tile"), ("strip", "sub")),
            jax.P(("group", "tile", "strip", "sub"), None),
            jax.P(("group", "tile", "strip", "sub")),
            jax.P(("group", "tile", "strip", "sub")),
        ),
        out_specs=(
            jax.P("group", "tile", ("strip", "sub")),
            jax.P("group", "tile", ("strip", "sub")),
        ),
        check_vma=False,
    )
```

```python
import jax
import jax.numpy as jnp
import numpy as np
from jax import lax
from jax.experimental import pallas as pl
from jax.experimental.pallas import tpu as pltpu

COARSE = 8
OMEGA = 0.8

HX = 12
HX2 = 9
HY = 42
LIMIT = 512
SLABS = 3
EDGE = 16


def neighbour_swap(x, axis, odd, spare):
    axis = axis if isinstance(axis, tuple) else (axis,)
    count = lax.axis_size(axis)
    twins = lax.axis_size(spare)
    leading = spare == "group"
    place = lambda i, twin: twin * count + i if leading else i * twins + twin
    pairs = []
    for twin in range(twins):
        for i in range(count):
            j, other = (i + 1 if i % 2 == odd else i - 1), twin
            if not 0 <= j < count:
                j, other = i, twin ^ 1
            pairs.append((place(i, twin), place(j, other)))
    return lax.ppermute(x, (spare,) + axis if leading else axis + (spare,), pairs)


def lane_maps(cols):
    half, quarter, h1, h2 = cols // 2, cols // 4, HY // 2, HY // 4
    wide1 = -np.ones(cols + 128, np.int64)
    wide1[:cols] = np.arange(cols) // 2
    wide1[cols : cols + HY] = half + np.arange(HY) // 2
    wide1[cols + 128 - HY :] = 2 * half - h1 + np.arange(HY) // 2
    wide2 = -np.ones(2 * half, np.int64)
    wide2[:half] = np.arange(half) // 2
    wide2[half : half + 2 * h2] = quarter + np.arange(2 * h2) // 2
    wide2[2 * half - 2 * h2 :] = 2 * quarter - h2 + np.arange(2 * h2) // 2
    inner2 = -np.ones(half, np.int64)
    inner2[4 : half - 4] = np.arange(4, half - 4) // 2
    edge1 = -np.ones(128, np.int64)
    edge1[: 2 * HY + EDGE] = np.arange(2 * HY + EDGE) // 2
    edge1[128 - EDGE :] = 128 - EDGE // 2 + np.arange(EDGE) // 2
    edge2 = -np.ones(128, np.int64)
    edge2[: 2 * h2] = quarter + np.arange(2 * h2) // 2
    edge2[2 * h1 - 2 * h2 : 2 * h1] = 2 * quarter - h2 + np.arange(2 * h2) // 2
    edge2[2 * h1 : 2 * h1 + 4] = np.arange(4) // 2
    edge2[124:] = quarter - 2 + np.arange(4) // 2
    return wide1, wide2, inner2, edge1, edge2


def selection(lanes, width):
    return (lanes[:, None] == np.arange(width)[None, :]).astype(np.float32)


def split(x, parts):
    out = []
    for _ in range(parts):
        out.append(x.astype(jnp.bfloat16))
        x = x - out[-1].astype(jnp.float32)
    return out


def exact_dot(left, right):
    return sum(jnp.dot(part, right, preferred_element_type=jnp.float32) for part in split(left, 2))


def neighbours(u):
    rows, lanes = u.shape
    return (
        pltpu.roll(u, 1, 0)
        + pltpu.roll(u, rows - 1, 0)
        + pltpu.roll(u, 1, 1)
        + pltpu.roll(u, lanes - 1, 1)
    )


def weights(kh, kv, scale, inside, w_ref, a_ref, b_ref):
    for i, layers in enumerate((1.0, 2.0)):
        diag = 4.0 * scale * kh + layers * kv
        w = jnp.where(inside, OMEGA / jnp.where(inside, diag, 1.0), 0.0)
        if w_ref is not None:
            w_ref[i] = w
        a_ref[i] = w * (scale * kh)
        b_ref[i] = w * kv


def loop(depth, fn, vregs):
    lax.fori_loop(0, depth, fn, 0, unroll=max(1, min(depth, LIMIT // vregs)))


def sweep(src, dst, wb, a_ref, b_ref, depth):
    def layer(z, c):
        i = jnp.minimum(z, 1)
        u = src[z + 1]
        dst[z + 1] = (
            (1.0 - OMEGA) * u
            + wb[z]
            + a_ref[i] * neighbours(u)
            + b_ref[i] * (src[z] + src[z + 2])
        )
        return c

    loop(depth, layer, src.shape[1] * src.shape[2] // 1024)


def residual_of(src, z, b, kh, kv, scale, lanes=None):
    layers = jnp.where(z == 0, 1.0, 2.0)
    u = src[z + 1]
    around = neighbours(u)[:, :lanes]
    u = u[:, :lanes]
    return b + (scale * kh) * (around - 4.0 * u) + kv * (src[z, :, :lanes] + src[z + 2, :, :lanes] - layers * u)


def blocks_out(ref, l, x):
    for j in range(ref.shape[1]):
        ref[l, j, 0 : x.shape[0], :] = x[:, 128 * j : 128 * (j + 1)]


def blocks_in(ref, l):
    return jnp.concatenate([ref[l, j] for j in range(ref.shape[1])], 1)


def rows_doubled(ref, l, part):
    n = part.shape[0]
    for j in range(ref.shape[1]):
        for s in (0, 1):
            ref[l, j, pl.ds(s, n, stride=2), :] = part[:, 128 * j : 128 * (j + 1)]


def slab_of(layers, at_right):
    shape = layers[0].shape
    lane = lax.broadcasted_iota(jnp.int32, shape, 1)
    out = jnp.zeros(shape, jnp.float32)
    for k, x in enumerate(layers):
        shift = (HY * (k + 1) if at_right else HY * k) % 128
        x = pltpu.roll(x, shift, 1) if shift else x
        out = jnp.where((lane >= HY * k) & (lane < HY * (k + 1)), x, out)
    return out


def load_kernel(rs, kh, kv, owner, cell, pressure, x, panels, a_out, b_out, ints, sems):
    depth, rows, cols = rs.shape
    count = depth + 2
    half = count // 2
    even = lax.axis_index("tile") % 2 == 0
    copies = [
        pltpu.make_async_copy(src, dst, sems.at[i])
        for i, (src, dst) in enumerate(
            (
                (owner, ints.at[0]),
                (cell, ints.at[1]),
                (pressure, panels.at[0, pl.ds(4, 4)]),
                (rs, x.at[pl.ds(0, depth)]),
                (kh, x.at[depth]),
                (kv, x.at[depth + 1]),
            )
        )
    ]
    for copy in copies:
        copy.start()
    for copy in copies:
        copy.wait()
    panels[0, 0:4, :] = (ints[0] * (rows * cols) + ints[1]).astype(jnp.float32)

    def first(out):
        for l in range(count):
            out[l] = x[l, 0:8, :]
            out[count + l % half, 4 * (l // half) : 4 * (l // half) + 4, :] = x[l, 8:HX, :]

    def last(out):
        for l in range(count):
            out[l] = x[l, rows - 8 : rows, :]
            out[count + l % half, 4 * (l // half) : 4 * (l // half) + 4, :] = x[l, rows - HX : rows - 8, :]

    @pl.when(even)
    def _():
        last(a_out)
        first(b_out)

    @pl.when(jnp.logical_not(even))
    def _():
        first(a_out)
        last(b_out)


def own_columns_kernel(x, sub_out, strip_out):
    count, _, cols = x.shape
    _, _, y_even = y_sides()
    for g in range(count // SLABS):
        layers = range(SLABS * g, SLABS * g + SLABS)
        to_right = slab_of([x[l, :, cols - 128 : cols] for l in layers], True)
        to_left = slab_of([x[l, :, 0:128] for l in layers], False)
        sub_out[g] = jnp.where(y_even, to_right, to_left)
        strip_out[g] = jnp.where(y_even, to_left, to_right)


def forcing_kernel(x_own, xa, xb, panels, ext, sub_out, strip_out):
    count, rows, cols = x_own.shape
    depth = count - 2
    half = count // 2
    tile = lax.axis_index("tile")
    even = tile % 2 == 0
    high = rows + HX

    def upper(x):
        for l in range(count):
            ext[l, 0:4, :] = x[count + l % half, 4 * (l // half) : 4 * (l // half) + 4, :]
            ext[l, 4:HX, :] = x[l]

    def lower(x):
        for l in range(count):
            ext[l, high : high + 8, :] = x[l]
            ext[l, high + 8 : high + HX, :] = x[count + l % half, 4 * (l // half) : 4 * (l // half) + 4, :]

    @pl.when(even)
    def _():
        lower(xa)
        upper(xb)

    @pl.when(jnp.logical_not(even))
    def _():
        upper(xa)
        lower(xb)

    for l in range(count):
        ext[l, HX:high, :] = x_own[l]

    span = rows + 2 * HX
    left, right = [], []
    for g in range(panels.shape[0]):
        group = panels[g]
        for k in range(4):
            code = group[k : k + 1].astype(jnp.int32)
            value = group[4 + k : 5 + k]
            row = code // cols - (tile * rows - HX)
            col = code % cols
            hit = row == lax.broadcasted_iota(jnp.int32, (span, 128), 0)
            left.append(jnp.where(hit, value, 0.0))
            right.append(
                jnp.where(col == lax.broadcasted_iota(jnp.int32, (cols, 128), 0), 1.0, 0.0).astype(jnp.bfloat16)
            )
    left = jnp.concatenate(left, 1)
    right = jnp.concatenate(right, 1)
    parts = lax.dot_general(
        jnp.concatenate(split(left, 3), 0), right, (((1,), (1,)), ((), ())), preferred_element_type=jnp.float32
    )
    total = parts[0:span] + parts[span : 2 * span] + parts[2 * span :]
    ext[depth - 1] = ext[depth - 1] + total

    _, _, y_even = y_sides()
    slabs = count // SLABS

    def send(g, to_right, to_left):
        sub_out[g] = jnp.where(y_even, to_right, to_left)
        strip_out[g] = jnp.where(y_even, to_left, to_right)

    def corners(l, first):
        return jnp.concatenate(
            [ext[l, 0:HX, first : first + 128], ext[l, high : high + HX, first : first + 128]], 0
        )

    for g in range(slabs):
        layers = range(SLABS * g, SLABS * g + SLABS)
        send(g, slab_of([corners(l, cols - 128) for l in layers], True), slab_of([corners(l, 0) for l in layers], False))
    pad = jnp.zeros((2 * HX - rows // 2, 128), jnp.float32)
    halves = [total[HX : HX + rows // 2], total[HX + rows // 2 : high]]
    send(
        slabs,
        jnp.concatenate([slab_of([x[:, cols - 128 :] for x in halves], True), pad], 0),
        jnp.concatenate([slab_of([x[:, :128] for x in halves], False), pad], 0),
    )


def rolled(x, shift):
    return pltpu.roll(x, shift % 128, 1) if shift % 128 else x


def base_kernel(ext, ysub, ystrip, base):
    count, span, cols = ext.shape
    high = span - HX
    _, _, y_even = y_sides()
    lane = lax.broadcasted_iota(jnp.int32, (span, 128), 1)
    lane_own = lane[HX:high]
    for g in range(count // SLABS):
        from_right = jnp.where(y_even, ysub[g], ystrip[g])
        from_left = jnp.where(y_even, ystrip[g], ysub[g])
        for k in range(SLABS):
            l = SLABS * g + k
            x = jnp.where(lane >= 128 - EDGE, ext[l, :, cols - 128 : cols], 0.0)
            x = jnp.where((lane >= 2 * HY) & (lane < 2 * HY + EDGE), rolled(ext[l, :, 0:128], 2 * HY), x)
            base[l] = x
            outer = jnp.where(lane_own < HY, rolled(from_right, -HY * k), rolled(from_left, HY - HY * k))
            base[l, HX:high, :] = jnp.where(lane_own < 2 * HY, outer, x[HX:high])


def row_inside(shape, rows, above):
    row = lax.axis_index("tile") * rows - above + lax.broadcasted_iota(jnp.int32, shape, 0)
    return (row >= 0) & (row < lax.axis_size("tile") * rows)


def y_sides():
    y = lax.axis_index("strip") * lax.axis_size("sub") + lax.axis_index("sub")
    return y > 0, y < lax.axis_size("strip") * lax.axis_size("sub") - 1, y % 2 == 0


def wide_inside(shape, rows, above, own, halo):
    has_left, has_right, _ = y_sides()
    column = lax.broadcasted_iota(jnp.int32, shape, 1)
    right = (column >= own) & (column < own + halo) & has_right
    left = (column >= shape[1] - halo) & has_left
    return row_inside(shape, rows, above) & ((column < own) | right | left)


def edge_inside(shape, rows, above, halo, edge):
    has_left, has_right, _ = y_sides()
    column = lax.broadcasted_iota(jnp.int32, shape, 1)
    right = (column < halo) & has_right
    left = (column >= halo) & (column < 2 * halo) & has_left
    own = ((column >= 2 * halo) & (column < 2 * halo + edge)) | (column >= 128 - edge)
    return row_inside(shape, rows, above) & (own | right | left)


def zero_ends(*refs):
    for ref in refs:
        ref[0] = jnp.zeros(ref.shape[1:], jnp.float32)
        ref[ref.shape[0] - 1] = jnp.zeros(ref.shape[1:], jnp.float32)


def presmooth(source, kh, kv, scale, inside, w, al, be, u, un, depth):
    weights(kh, kv, scale, inside, w, al, be)
    zero_ends(u, un)

    def first(z, c):
        u[z + 1] = w[jnp.minimum(z, 1)] * source[z]
        return c

    loop(depth, first, u.shape[1] * u.shape[2] // 1024)
    sweep(u, un, u.at[pl.ds(1, depth)], al, be, depth)


def restrict(source, un, scale, r, depth, parts):
    kh, kv = source[depth], source[depth + 1]
    rows = kh.shape[0]
    for l in range(depth + 2):
        for j in range(r.shape[1]):
            if r.shape[2] > rows:
                r[l, j, rows:, :] = jnp.zeros((r.shape[2] - rows, 128), jnp.float32)
    blocks_out(r, depth, kh)
    blocks_out(r, depth + 1, kv)

    def rest(z, c):
        blocks_out(r, z, residual_of(un, z, source[z], source[depth], source[depth + 1], scale))
        return c

    loop(depth, rest, rows * kh.shape[1] // 1024)
    n = r.shape[2] // 2
    pairs = jnp.concatenate(
        [
            jnp.concatenate(
                [r[l, j, pl.ds(0, n, stride=2), :] + r[l, j, pl.ds(1, n, stride=2), :] for j in range(r.shape[1])], 1
            )
            for l in range(depth + 2)
        ],
        0,
    )
    return exact_dot(pairs, parts).reshape(depth + 2, n, parts.shape[1])


def inner_kernel(
    ext, c1, c2, u_out, b1_out, u1_out, c_out,
    w0, al0, be0, u0, u0n, r0, w1, al1, be1, u1, u1n, r1,
):
    depth, span, cols = ext.shape[0] - 2, ext.shape[1], ext.shape[2]
    rows = span - 2 * HX
    presmooth(
        ext, ext[depth], ext[depth + 1], 1.0, row_inside((span, cols), rows, HX), w0, al0, be0, u0, u0n, depth
    )
    for z in range(depth):
        u_out[z] = u0n[z + 1, 8 : span - 8, :]
    b1_out[...] = restrict(ext, u0n, 1.0, r0, depth, c1[...])
    span1, half = b1_out.shape[1], b1_out.shape[2]
    presmooth(
        b1_out, b1_out[depth], b1_out[depth + 1], 0.25, row_inside((span1, half), rows // 2, HX // 2),
        w1, al1, be1, u1, u1n, depth,
    )
    u1_out[...] = u1n[pl.ds(1, depth)]
    c_out[...] = restrict(b1_out, u1n, 0.25, r1, depth, c2[...])


def edge_kernel(
    base, ysub, ystrip, c_inner, c1, c2,
    b_out, u_out, b1_out, u1_out, c_out, a_msg, b_msg,
    w0, al0, be0, u0, u0n, r0, w1, al1, be1, u1, u1n, r1,
):
    count, span = base.shape[:2]
    depth = count - 2
    rows = span - 2 * HX
    high = span - HX
    even = lax.axis_index("tile") % 2 == 0
    _, _, y_even = y_sides()
    slabs = count // SLABS
    lane = lax.broadcasted_iota(jnp.int32, (2 * HX, 128), 1)
    for g in range(slabs):
        from_right = jnp.where(y_even, ysub[g], ystrip[g])
        from_left = jnp.where(y_even, ystrip[g], ysub[g])
        for k in range(SLABS):
            l = SLABS * g + k
            outer = jnp.where(lane < HY, rolled(from_right, -HY * k), rolled(from_left, HY - HY * k))
            b_out[l, 0:HX, :] = jnp.where(lane[:HX] < 2 * HY, outer[:HX], base[l, 0:HX, :])
            b_out[l, high:span, :] = jnp.where(lane[HX:] < 2 * HY, outer[HX:], base[l, high:span, :])
    half = rows // 2
    lane = lane[:half]
    from_right = jnp.where(y_even, ysub[slabs, :half], ystrip[slabs, :half])
    from_left = jnp.where(y_even, ystrip[slabs, :half], ysub[slabs, :half])
    for k in (0, 1):
        force = jnp.where(lane < HY, rolled(from_right, -HY * k), rolled(from_left, HY - HY * k))
        part = pl.ds(HX + half * k, half)
        b_out[depth - 1, part, :] = base[depth - 1, part, :] + jnp.where(lane < 2 * HY, force, 0.0)
    presmooth(
        b_out, b_out[depth], b_out[depth + 1], 1.0, edge_inside((span, 128), rows, HX, HY, EDGE),
        w0, al0, be0, u0, u0n, depth,
    )
    for z in range(depth):
        u_out[z] = u0n[z + 1, 8 : span - 8, :]
    b1_out[...] = restrict(b_out, u0n, 1.0, r0, depth, c1[...])
    span1 = b1_out.shape[1]
    presmooth(
        b1_out, b1_out[depth], b1_out[depth + 1], 0.25,
        edge_inside((span1, 128), rows // 2, HX // 2, HY // 2, EDGE // 2),
        w1, al1, be1, u1, u1n, depth,
    )
    u1_out[...] = u1n[pl.ds(1, depth)]
    c_out[...] = c_inner[...] + restrict(b1_out, u1n, 0.25, r1, depth, c2[...])
    own2 = HX // 4

    def send(out, start):
        for l in range(count):
            out[count + l // 8, l % 8 : l % 8 + 1, :] = c_out[l, start : start + 1, :]
            out[l] = c_out[l, start + 1 : start + HX2, :]

    @pl.when(even)
    def _():
        send(a_msg, own2 - 1)
        send(b_msg, own2)

    @pl.when(jnp.logical_not(even))
    def _():
        send(a_msg, own2)
        send(b_msg, own2 - 1)


def join_kernel(
    ext, edge, u_in, u_edge, b1_in, b1_edge, u1_in, u1_edge,
    k0, u0, wb0, al0, be0, u1, wb1, al1, be1, w0, w1,
):
    depth, small, cols = u_in.shape
    span = ext.shape[1]
    rows = span - 2 * HX

    def joined(inner, strip, halo, edge, patch):
        own = inner.shape[1]
        lane = lax.broadcasted_iota(jnp.int32, strip.shape, 1)
        turned = pltpu.roll(strip, 128 - 2 * halo, 1)
        outer = jnp.where(lane < halo, strip, jnp.where(lane >= 128 - halo, turned, 0.0))
        blocks = [inner[:, 128 * j : 128 * (j + 1)] for j in range(own // 128)]
        blocks[0] = jnp.where(lane < patch, turned, blocks[0])
        blocks[-1] = jnp.where(lane >= 128 - patch, strip, blocks[-1])
        return jnp.concatenate(blocks + [outer], 1)

    part0 = lambda inner, strip: joined(inner, strip, HY, EDGE, EDGE // 2)
    part1 = lambda inner, strip: joined(inner, strip, HY // 2, EDGE // 2, EDGE // 4)
    low, top = 8, span - 8
    lanes = cols + 128
    for i in (0, 1):
        k0[i] = part0(ext[depth + i, low:top, :], edge[depth + i, low:top, :])
    weights(
        k0[0], k0[1], 1.0, wide_inside((small, lanes), rows, HX - low, cols, HY), w0, al0, be0,
    )
    span1, half = b1_in.shape[1], b1_in.shape[2]
    kh1, kv1 = (part1(b1_in[depth + i], b1_edge[depth + i]) for i in (0, 1))
    weights(
        kh1, kv1, 0.25, wide_inside((span1, 2 * half), rows // 2, HX // 2, half, HY // 2), w1, al1, be1,
    )
    for z in range(depth):
        i = min(z, 1)
        u0[z] = part0(u_in[z], u_edge[z])
        wb0[z] = w0[i] * part0(ext[z, low:top, :], edge[z, low:top, :])
        u1[z] = part1(u1_in[z], u1_edge[z])
        wb1[z] = w1[i] * part1(b1_in[z], b1_edge[z])


def up_kernel(
    c_in, xa, xb, ext, k0, u0, wb0, al0, be0, u1, wb1, al1, be1, p1, p2,
    potential, residual,
    b2, w2, al2, be2, wb2, u2, u2n, f1, f1n, f0, f0n, e1, e0, pot, res, sems,
):
    count = c_in.shape[0]
    depth = count - 2
    rows, cols = potential.shape[1:]
    rows2 = rows // 4
    even = lax.axis_index("tile") % 2 == 0
    own2 = HX // 4
    span2 = b2.shape[1]
    end2 = rows2 + 2 * HX2

    def put(x, start):
        for l in range(count):
            b2[l, start : start + 1, :] = x[count + l // 8, l % 8 : l % 8 + 1, :]
            b2[l, start + 1 : start + HX2, :] = x[l]

    @pl.when(even)
    def _():
        put(xa, HX2 + rows2)
        put(xb, 0)

    @pl.when(jnp.logical_not(even))
    def _():
        put(xa, 0)
        put(xb, HX2 + rows2)

    lanes2 = b2.shape[2]
    for l in range(count):
        b2[l, HX2 : HX2 + rows2, :] = c_in[l, own2 : own2 + rows2, :]
        b2[l, end2:span2, :] = jnp.zeros((span2 - end2, lanes2), jnp.float32)
    row = lax.broadcasted_iota(jnp.int32, (span2, lanes2), 0)
    inside2 = wide_inside((span2, lanes2), rows2, HX2, cols // 4, HY // 4)
    weights(b2[depth], b2[depth + 1], 0.0625, inside2 & (row < end2), w2, al2, be2)
    zero_ends(u2, u2n, f1, f1n, f0, f0n)

    def first2(z, c):
        v = w2[jnp.minimum(z, 1)] * b2[z]
        wb2[z] = v
        u2[z + 1] = v
        return c

    loop(depth, first2, 4)
    src, dst = u2, u2n
    for _ in range(COARSE - 1):
        sweep(src, dst, wb2, al2, be2, depth)
        src, dst = dst, src

    span1, lanes1 = u1.shape[1], u1.shape[2]
    off2 = HX2 - own2
    coarse = jnp.concatenate([src[z + 1][off2 : off2 + span1 // 2] for z in range(depth)], 0)
    fine = exact_dot(coarse, p2[...])
    for z in range(depth):
        rows_doubled(e1, z, fine[z * (span1 // 2) : (z + 1) * (span1 // 2)])

    def first1(z, c):
        f1[z + 1] = u1[z] + blocks_in(e1, z)
        return c

    loop(depth, first1, 8)
    sweep(f1, f1n, wb1, al1, be1, depth)
    sweep(f1n, f1, wb1, al1, be1, depth)

    span0, lanes0 = u0.shape[1], u0.shape[2]
    above = (span0 - rows) // 2
    off1 = (HX - above) // 2
    fine = exact_dot(f1[pl.ds(1, depth)].reshape(depth * span1, lanes1), p1[...])
    for z in range(depth):
        rows_doubled(e0, z, fine[z * span1 + off1 : z * span1 + off1 + span0 // 2])

    def first0(z, c):
        f0[z + 1] = u0[z] + blocks_in(e0, z)
        return c

    loop(depth, first0, 15)
    sweep(f0, f0n, wb0, al0, be0, depth)
    sweep(f0n, f0, wb0, al0, be0, depth)

    copies = []

    def ship(src, dst, first, n):
        copy = pltpu.make_async_copy(src.at[pl.ds(first, n)], dst.at[pl.ds(first, n)], sems.at[len(copies)])
        copy.start()
        copies.append(copy)

    for z in range(depth):
        pot[z] = f0[z + 1, above : above + rows, 0:cols]
    ship(pot, potential, 0, depth)
    chunk = depth // 4
    for z in range(depth):
        b = ext[z, HX - above : HX - above + span0, :]
        r = residual_of(f0, z, b, k0[0, :, 0:cols], k0[1, :, 0:cols], 1.0, cols)
        res[z] = r[above : above + rows]
        if z % chunk == chunk - 1:
            ship(res, residual, z + 1 - chunk, chunk)
    for copy in copies:
        copy.wait()


VM = pl.BlockSpec(memory_space=pltpu.VMEM)


def call(kernel, outs, scratch, *args, aliases={}):
    f32 = lambda shape: jax.ShapeDtypeStruct(shape, jnp.float32)
    return pl.pallas_call(
        kernel,
        out_shape=[f32(s) for s in outs],
        in_specs=[VM] * len(args),
        out_specs=[VM] * len(outs),
        scratch_shapes=[pltpu.VMEM(s, jnp.float32) for s in scratch],
        input_output_aliases=aliases,
        compiler_params=pltpu.CompilerParams(vmem_limit_bytes=24 << 20),
    )(*args)


def body(right_side, horiz_coef, vert_coef, panel_owner, panel_cell, panel_pressure):
    depth, rows, cols = right_side.shape
    tiles = lax.axis_size("tile")
    y_axes = ("strip", "sub")
    y_count = lax.axis_size("strip") * lax.axis_size("sub")
    count = depth + 2
    span = rows + 2 * HX
    wide1, wide2, inner2, edge1, edge2 = lane_maps(cols)
    mean = lambda lanes, width: jnp.asarray(0.25 * selection(lanes, width), jnp.bfloat16)
    spread = lambda lanes, width: jnp.asarray(selection(lanes, width).T, jnp.bfloat16)
    c1_inner, c2_inner = mean(wide1[:cols], cols // 2), mean(inner2, cols // 2)
    c1_edge, c2_edge = mean(edge1, 128), mean(edge2, cols // 2)
    p1, p2 = spread(wide1, cols), spread(wide2, cols // 2)

    message = (count + count // 2, 8, cols)
    f32 = lambda shape: jax.ShapeDtypeStruct(shape, jnp.float32)
    early = (count // SLABS, rows, 128)
    x_own, panels, a, b = pl.pallas_call(
        load_kernel,
        out_shape=[f32((count, rows, cols)), f32((1, 8, 128)), f32(message), f32(message)],
        in_specs=[pl.BlockSpec(memory_space=pltpu.HBM)] * 6,
        out_specs=[VM] * 4,
        scratch_shapes=[pltpu.VMEM((2, 4, 128), jnp.int32), pltpu.SemaphoreType.DMA((6,))],
        compiler_params=pltpu.CompilerParams(vmem_limit_bytes=8 << 20),
    )(
        *[
            pltpu.with_memory_space_constraint(x, pltpu.HBM)
            for x in (
                right_side, horiz_coef, vert_coef,
                panel_owner.reshape(4, -1), panel_cell.reshape(4, -1), panel_pressure.reshape(4, -1),
            )
        ]
    )
    near = lax.ppermute(panels, "tile", [(i, i ^ 1) for i in range(tiles)])
    a = neighbour_swap(a, "tile", 0, "sub")
    b = neighbour_swap(b, "tile", 1, "sub")
    sub_own, strip_own = call(own_columns_kernel, [early, early], [], x_own)
    sub_own = neighbour_swap(sub_own, y_axes, 0, "group")
    strip_own = neighbour_swap(strip_own, y_axes, 1, "group")
    panels = jnp.concatenate([panels, near], 0)
    step = 2
    while step < tiles:
        swap = [(i, i ^ step) for i in range(tiles)]
        panels = jnp.concatenate([panels, lax.ppermute(panels, "tile", swap)], 0)
        step *= 2

    slabs = (count // SLABS + 1, 2 * HX, 128)
    ext, sub, strip = call(
        forcing_kernel, [(count, span, cols), slabs, slabs], [],
        x_own, a, b, panels,
    )
    sub = neighbour_swap(sub, y_axes, 0, "group")
    strip = neighbour_swap(strip, y_axes, 1, "group")

    lanes, half = cols + 128, cols // 2
    small = span - 16
    span1 = (span + 8) // 2
    span2 = span1 // 2

    def down_scratch(width, width1):
        return (
            [(2, span, width)] * 3 + [(depth + 2, span, width)] * 2 + [(count, width // 128, span + 8, 128)]
            + [(2, span1, width1)] * 3 + [(depth + 2, span1, width1)] * 2 + [(count, width1 // 128, span1, 128)]
        )

    u_in, b1_in, u1_in, c_in = call(
        inner_kernel,
        [(depth, small, cols), (count, span1, half), (depth, span1, half), (count, span2, half)],
        down_scratch(cols, half),
        ext, c1_inner, c2_inner,
    )
    (base,) = call(base_kernel, [(count, span, 128)], [], ext, sub_own, strip_own)
    message2 = (count + (count + 7) // 8, 8, half)
    edge, u_edge, b1_edge, u1_edge, c_own, a2, b2 = call(
        edge_kernel,
        [
            (count, span, 128), (depth, small, 128), (count, span1, 128), (depth, span1, 128),
            (count, span2, half), message2, message2,
        ],
        down_scratch(128, 128),
        base, sub, strip, c_in, c1_edge, c2_edge,
        aliases={0: 0},
    )
    a2 = neighbour_swap(a2, "tile", 0, "sub")
    b2 = neighbour_swap(b2, "tile", 1, "sub")

    pair0, field = (2, small, lanes), (depth, small, lanes)
    pair1, field1 = (2, span1, cols), (depth, span1, cols)
    state = call(
        join_kernel,
        [pair0, field, field, pair0, pair0, field1, field1, pair1, pair1],
        [pair0, pair1],
        ext, edge, u_in, u_edge, b1_in, b1_edge, u1_in, u1_edge,
    )

    wide2 = 32
    field2 = (depth + 2, wide2, half)
    own = right_side.shape
    potential, residual = pl.pallas_call(
        up_kernel,
        out_shape=[f32(own), f32(own)],
        in_specs=[VM] * (6 + len(state)),
        out_specs=[pl.BlockSpec(memory_space=pltpu.HBM)] * 2,
        scratch_shapes=[
            pltpu.VMEM(shape, jnp.float32)
            for shape in (
                (count, wide2, half), (2, wide2, half), (2, wide2, half), (2, wide2, half), (depth, wide2, half),
                field2, field2, (depth + 2, span1, cols), (depth + 2, span1, cols),
                (depth + 2, small, lanes), (depth + 2, small, lanes),
                (depth, cols // 128, span1, 128), (depth, lanes // 128, small, 128), own, own,
            )
        ]
        + [pltpu.SemaphoreType.DMA((5,))],
        compiler_params=pltpu.CompilerParams(vmem_limit_bytes=24 << 20),
    )(c_own, a2, b2, ext, *state, p1, p2)
    return potential, residual


def solution(mesh):
    return jax.shard_map(
        body,
        mesh=mesh,
        in_specs=(
            jax.P("group", "tile", ("strip", "sub")),
            jax.P(("group", "tile"), ("strip", "sub")),
            jax.P(("group", "tile"), ("strip", "sub")),
            jax.P(("group", "tile", "strip", "sub"), None),
            jax.P(("group", "tile", "strip", "sub")),
            jax.P(("group", "tile", "strip", "sub")),
        ),
        out_specs=(
            jax.P("group", "tile", ("strip", "sub")),
            jax.P("group", "tile", ("strip", "sub")),
        ),
        check_vma=False,
    )
```

```python
import jax
import jax.numpy as jnp
import numpy as np
from jax import lax
from jax.experimental import pallas as pl
from jax.experimental.pallas import tpu as pltpu

COARSE = 8
OMEGA = 0.8

HX = 12
HX2 = 9
HY = 42
LIMIT = 512
SLABS = 3
EDGE = 16


def neighbour_swap(x, axis, odd, spare):
    axis = axis if isinstance(axis, tuple) else (axis,)
    count = lax.axis_size(axis)
    twins = lax.axis_size(spare)
    leading = spare == "group"
    place = lambda i, twin: twin * count + i if leading else i * twins + twin
    pairs = []
    for twin in range(twins):
        for i in range(count):
            j, other = (i + 1 if i % 2 == odd else i - 1), twin
            if not 0 <= j < count:
                j, other = i, twin ^ 1
            pairs.append((place(i, twin), place(j, other)))
    return lax.ppermute(x, (spare,) + axis if leading else axis + (spare,), pairs)


def lane_maps(cols):
    half, quarter, h1, h2 = cols // 2, cols // 4, HY // 2, HY // 4
    wide1 = -np.ones(cols + 128, np.int64)
    wide1[:cols] = np.arange(cols) // 2
    wide1[cols : cols + HY] = half + np.arange(HY) // 2
    wide1[cols + 128 - HY :] = 2 * half - h1 + np.arange(HY) // 2
    wide2 = -np.ones(2 * half, np.int64)
    wide2[:half] = np.arange(half) // 2
    wide2[half : half + 2 * h2] = quarter + np.arange(2 * h2) // 2
    wide2[2 * half - 2 * h2 :] = 2 * quarter - h2 + np.arange(2 * h2) // 2
    inner2 = -np.ones(half, np.int64)
    inner2[4 : half - 4] = np.arange(4, half - 4) // 2
    edge1 = -np.ones(128, np.int64)
    edge1[: 2 * HY + EDGE] = np.arange(2 * HY + EDGE) // 2
    edge1[128 - EDGE :] = 128 - EDGE // 2 + np.arange(EDGE) // 2
    edge2 = -np.ones(128, np.int64)
    edge2[: 2 * h2] = quarter + np.arange(2 * h2) // 2
    edge2[2 * h1 - 2 * h2 : 2 * h1] = 2 * quarter - h2 + np.arange(2 * h2) // 2
    edge2[2 * h1 : 2 * h1 + 4] = np.arange(4) // 2
    edge2[124:] = quarter - 2 + np.arange(4) // 2
    return wide1, wide2, inner2, edge1, edge2


def selection(lanes, width):
    return (lanes[:, None] == np.arange(width)[None, :]).astype(np.float32)


def split(x, parts):
    out = []
    for _ in range(parts):
        out.append(x.astype(jnp.bfloat16))
        x = x - out[-1].astype(jnp.float32)
    return out


def exact_dot(left, right):
    return jnp.dot(jnp.concatenate(split(left, 2), 1), jnp.concatenate([right, right], 0), preferred_element_type=jnp.float32)


def neighbours(u):
    rows, lanes = u.shape
    return (
        pltpu.roll(u, 1, 0)
        + pltpu.roll(u, rows - 1, 0)
        + pltpu.roll(u, 1, 1)
        + pltpu.roll(u, lanes - 1, 1)
    )


def weights(kh, kv, scale, inside, w_ref, a_ref, b_ref):
    for i, layers in enumerate((1.0, 2.0)):
        diag = 4.0 * scale * kh + layers * kv
        w = jnp.where(inside, OMEGA / jnp.where(inside, diag, 1.0), 0.0)
        if w_ref is not None:
            w_ref[i] = w
        a_ref[i] = w * (scale * kh)
        b_ref[i] = w * kv


def loop(depth, fn, vregs):
    lax.fori_loop(0, depth, fn, 0, unroll=max(1, min(depth, LIMIT // vregs)))


def sweep(src, dst, wb, a_ref, b_ref, depth):
    def layer(z, c):
        i = jnp.minimum(z, 1)
        u = src[z + 1]
        dst[z + 1] = (
            (1.0 - OMEGA) * u
            + wb[z]
            + a_ref[i] * neighbours(u)
            + b_ref[i] * (src[z] + src[z + 2])
        )
        return c

    loop(depth, layer, src.shape[1] * src.shape[2] // 1024)


def residual_of(src, z, b, kh, kv, scale, lanes=None):
    layers = jnp.where(z == 0, 1.0, 2.0)
    u = src[z + 1]
    around = neighbours(u)[:, :lanes]
    u = u[:, :lanes]
    return b + (scale * kh) * (around - 4.0 * u) + kv * (src[z, :, :lanes] + src[z + 2, :, :lanes] - layers * u)


def blocks_out(ref, l, x):
    for j in range(ref.shape[1]):
        ref[l, j, 0 : x.shape[0], :] = x[:, 128 * j : 128 * (j + 1)]


def blocks_in(ref, l):
    return jnp.concatenate([ref[l, j] for j in range(ref.shape[1])], 1)


def rows_doubled(ref, l, part):
    n = part.shape[0]
    for j in range(ref.shape[1]):
        for s in (0, 1):
            ref[l, j, pl.ds(s, n, stride=2), :] = part[:, 128 * j : 128 * (j + 1)]


def slab_of(layers, at_right):
    shape = layers[0].shape
    lane = lax.broadcasted_iota(jnp.int32, shape, 1)
    out = jnp.zeros(shape, jnp.float32)
    for k, x in enumerate(layers):
        shift = (HY * (k + 1) if at_right else HY * k) % 128
        x = pltpu.roll(x, shift, 1) if shift else x
        out = jnp.where((lane >= HY * k) & (lane < HY * (k + 1)), x, out)
    return out


def load_kernel(rs, kh, kv, owner, cell, pressure, x, panels, a_out, b_out, ints, sems):
    depth, rows, cols = rs.shape
    count = depth + 2
    half = count // 2
    even = lax.axis_index("tile") % 2 == 0
    copies = [
        pltpu.make_async_copy(src, dst, sems.at[i])
        for i, (src, dst) in enumerate(
            (
                (owner, ints.at[0]),
                (cell, ints.at[1]),
                (pressure, panels.at[0, pl.ds(4, 4)]),
                (rs, x.at[pl.ds(0, depth)]),
                (kh, x.at[depth]),
                (kv, x.at[depth + 1]),
            )
        )
    ]
    for copy in copies:
        copy.start()
    for copy in copies:
        copy.wait()
    panels[0, 0:4, :] = (ints[0] * (rows * cols) + ints[1]).astype(jnp.float32)

    def first(out):
        for l in range(count):
            out[l] = x[l, 0:8, :]
            out[count + l % half, 4 * (l // half) : 4 * (l // half) + 4, :] = x[l, 8:HX, :]

    def last(out):
        for l in range(count):
            out[l] = x[l, rows - 8 : rows, :]
            out[count + l % half, 4 * (l // half) : 4 * (l // half) + 4, :] = x[l, rows - HX : rows - 8, :]

    @pl.when(even)
    def _():
        last(a_out)
        first(b_out)

    @pl.when(jnp.logical_not(even))
    def _():
        first(a_out)
        last(b_out)


def own_columns_kernel(x, sub_out, strip_out):
    count, _, cols = x.shape
    _, _, y_even = y_sides()
    for g in range(count // SLABS):
        layers = range(SLABS * g, SLABS * g + SLABS)
        to_right = slab_of([x[l, :, cols - 128 : cols] for l in layers], True)
        to_left = slab_of([x[l, :, 0:128] for l in layers], False)
        sub_out[g] = jnp.where(y_even, to_right, to_left)
        strip_out[g] = jnp.where(y_even, to_left, to_right)


def forcing_kernel(x_own, xa, xb, panels, ext, sub_out, strip_out):
    count, rows, cols = x_own.shape
    depth = count - 2
    half = count // 2
    tile = lax.axis_index("tile")
    even = tile % 2 == 0
    high = rows + HX

    def upper(x):
        for l in range(count):
            ext[l, 0:4, :] = x[count + l % half, 4 * (l // half) : 4 * (l // half) + 4, :]
            ext[l, 4:HX, :] = x[l]

    def lower(x):
        for l in range(count):
            ext[l, high : high + 8, :] = x[l]
            ext[l, high + 8 : high + HX, :] = x[count + l % half, 4 * (l // half) : 4 * (l // half) + 4, :]

    @pl.when(even)
    def _():
        lower(xa)
        upper(xb)

    @pl.when(jnp.logical_not(even))
    def _():
        upper(xa)
        lower(xb)

    for l in range(count):
        ext[l, HX:high, :] = x_own[l]

    span = rows + 2 * HX
    left, right = [], []
    for g in range(panels.shape[0]):
        group = panels[g]
        for k in range(4):
            code = group[k : k + 1].astype(jnp.int32)
            value = group[4 + k : 5 + k]
            row = code // cols - (tile * rows - HX)
            col = code % cols
            hit = row == lax.broadcasted_iota(jnp.int32, (span, 128), 0)
            left.append(jnp.where(hit, value, 0.0))
            right.append(
                jnp.where(col == lax.broadcasted_iota(jnp.int32, (cols, 128), 0), 1.0, 0.0).astype(jnp.bfloat16)
            )
    left = jnp.concatenate(left, 1)
    right = jnp.concatenate(right, 1)
    parts = lax.dot_general(
        jnp.concatenate(split(left, 3), 0), right, (((1,), (1,)), ((), ())), preferred_element_type=jnp.float32
    )
    total = parts[0:span] + parts[span : 2 * span] + parts[2 * span :]
    ext[depth - 1] = ext[depth - 1] + total

    _, _, y_even = y_sides()
    slabs = count // SLABS

    def send(g, to_right, to_left):
        sub_out[g] = jnp.where(y_even, to_right, to_left)
        strip_out[g] = jnp.where(y_even, to_left, to_right)

    def corners(l, first):
        return jnp.concatenate(
            [ext[l, 0:HX, first : first + 128], ext[l, high : high + HX, first : first + 128]], 0
        )

    for g in range(slabs):
        layers = range(SLABS * g, SLABS * g + SLABS)
        send(g, slab_of([corners(l, cols - 128) for l in layers], True), slab_of([corners(l, 0) for l in layers], False))
    pad = jnp.zeros((2 * HX - rows // 2, 128), jnp.float32)
    halves = [total[HX : HX + rows // 2], total[HX + rows // 2 : high]]
    send(
        slabs,
        jnp.concatenate([slab_of([x[:, cols - 128 :] for x in halves], True), pad], 0),
        jnp.concatenate([slab_of([x[:, :128] for x in halves], False), pad], 0),
    )


def rolled(x, shift):
    return pltpu.roll(x, shift % 128, 1) if shift % 128 else x


def base_kernel(ext, ysub, ystrip, base):
    count, span, cols = ext.shape
    high = span - HX
    _, _, y_even = y_sides()
    lane = lax.broadcasted_iota(jnp.int32, (span, 128), 1)
    lane_own = lane[HX:high]
    for g in range(count // SLABS):
        from_right = jnp.where(y_even, ysub[g], ystrip[g])
        from_left = jnp.where(y_even, ystrip[g], ysub[g])
        for k in range(SLABS):
            l = SLABS * g + k
            x = jnp.where(lane >= 128 - EDGE, ext[l, :, cols - 128 : cols], 0.0)
            x = jnp.where((lane >= 2 * HY) & (lane < 2 * HY + EDGE), rolled(ext[l, :, 0:128], 2 * HY), x)
            base[l] = x
            outer = jnp.where(lane_own < HY, rolled(from_right, -HY * k), rolled(from_left, HY - HY * k))
            base[l, HX:high, :] = jnp.where(lane_own < 2 * HY, outer, x[HX:high])


def row_inside(shape, rows, above):
    row = lax.axis_index("tile") * rows - above + lax.broadcasted_iota(jnp.int32, shape, 0)
    return (row >= 0) & (row < lax.axis_size("tile") * rows)


def y_sides():
    y = lax.axis_index("strip") * lax.axis_size("sub") + lax.axis_index("sub")
    return y > 0, y < lax.axis_size("strip") * lax.axis_size("sub") - 1, y % 2 == 0


def wide_inside(shape, rows, above, own, halo):
    has_left, has_right, _ = y_sides()
    column = lax.broadcasted_iota(jnp.int32, shape, 1)
    right = (column >= own) & (column < own + halo) & has_right
    left = (column >= shape[1] - halo) & has_left
    return row_inside(shape, rows, above) & ((column < own) | right | left)


def edge_inside(shape, rows, above, halo, edge):
    has_left, has_right, _ = y_sides()
    column = lax.broadcasted_iota(jnp.int32, shape, 1)
    right = (column < halo) & has_right
    left = (column >= halo) & (column < 2 * halo) & has_left
    own = ((column >= 2 * halo) & (column < 2 * halo + edge)) | (column >= 128 - edge)
    return row_inside(shape, rows, above) & (own | right | left)


def zero_ends(*refs):
    for ref in refs:
        ref[0] = jnp.zeros(ref.shape[1:], jnp.float32)
        ref[ref.shape[0] - 1] = jnp.zeros(ref.shape[1:], jnp.float32)


def presmooth(source, kh, kv, scale, inside, w, al, be, u, un, depth):
    weights(kh, kv, scale, inside, w, al, be)
    zero_ends(u, un)

    def first(z, c):
        u[z + 1] = w[jnp.minimum(z, 1)] * source[z]
        return c

    loop(depth, first, u.shape[1] * u.shape[2] // 1024)
    sweep(u, un, u.at[pl.ds(1, depth)], al, be, depth)


def restrict(source, un, scale, r, depth, parts):
    kh, kv = source[depth], source[depth + 1]
    rows = kh.shape[0]
    for l in range(depth + 2):
        for j in range(r.shape[1]):
            if r.shape[2] > rows:
                r[l, j, rows:, :] = jnp.zeros((r.shape[2] - rows, 128), jnp.float32)
    blocks_out(r, depth, kh)
    blocks_out(r, depth + 1, kv)

    def rest(z, c):
        blocks_out(r, z, residual_of(un, z, source[z], source[depth], source[depth + 1], scale))
        return c

    loop(depth, rest, rows * kh.shape[1] // 1024)
    n = r.shape[2] // 2
    pairs = jnp.concatenate(
        [
            jnp.concatenate(
                [r[l, j, pl.ds(0, n, stride=2), :] + r[l, j, pl.ds(1, n, stride=2), :] for j in range(r.shape[1])], 1
            )
            for l in range(depth + 2)
        ],
        0,
    )
    return exact_dot(pairs, parts).reshape(depth + 2, n, parts.shape[1])


def inner_kernel(
    ext, c1, c2, u_out, b1_out, u1_out, c_out,
    w0, al0, be0, u0, u0n, r0, w1, al1, be1, u1, u1n, r1,
):
    depth, span, cols = ext.shape[0] - 2, ext.shape[1], ext.shape[2]
    rows = span - 2 * HX
    presmooth(
        ext, ext[depth], ext[depth + 1], 1.0, row_inside((span, cols), rows, HX), w0, al0, be0, u0, u0n, depth
    )
    for z in range(depth):
        u_out[z] = u0n[z + 1, 8 : span - 8, :]
    b1_out[...] = restrict(ext, u0n, 1.0, r0, depth, c1[...])
    span1, half = b1_out.shape[1], b1_out.shape[2]
    presmooth(
        b1_out, b1_out[depth], b1_out[depth + 1], 0.25, row_inside((span1, half), rows // 2, HX // 2),
        w1, al1, be1, u1, u1n, depth,
    )
    u1_out[...] = u1n[pl.ds(1, depth)]
    c_out[...] = restrict(b1_out, u1n, 0.25, r1, depth, c2[...])


def edge_kernel(
    base, ysub, ystrip, c_inner, c1, c2,
    b_out, u_out, b1_out, u1_out, c_out, a_msg, b_msg,
    w0, al0, be0, u0, u0n, r0, w1, al1, be1, u1, u1n, r1,
):
    count, span = base.shape[:2]
    depth = count - 2
    rows = span - 2 * HX
    high = span - HX
    even = lax.axis_index("tile") % 2 == 0
    _, _, y_even = y_sides()
    slabs = count // SLABS
    lane = lax.broadcasted_iota(jnp.int32, (2 * HX, 128), 1)
    for g in range(slabs):
        from_right = jnp.where(y_even, ysub[g], ystrip[g])
        from_left = jnp.where(y_even, ystrip[g], ysub[g])
        for k in range(SLABS):
            l = SLABS * g + k
            outer = jnp.where(lane < HY, rolled(from_right, -HY * k), rolled(from_left, HY - HY * k))
            b_out[l, 0:HX, :] = jnp.where(lane[:HX] < 2 * HY, outer[:HX], base[l, 0:HX, :])
            b_out[l, high:span, :] = jnp.where(lane[HX:] < 2 * HY, outer[HX:], base[l, high:span, :])
    half = rows // 2
    lane = lane[:half]
    from_right = jnp.where(y_even, ysub[slabs, :half], ystrip[slabs, :half])
    from_left = jnp.where(y_even, ystrip[slabs, :half], ysub[slabs, :half])
    for k in (0, 1):
        force = jnp.where(lane < HY, rolled(from_right, -HY * k), rolled(from_left, HY - HY * k))
        part = pl.ds(HX + half * k, half)
        b_out[depth - 1, part, :] = base[depth - 1, part, :] + jnp.where(lane < 2 * HY, force, 0.0)
    presmooth(
        b_out, b_out[depth], b_out[depth + 1], 1.0, edge_inside((span, 128), rows, HX, HY, EDGE),
        w0, al0, be0, u0, u0n, depth,
    )
    for z in range(depth):
        u_out[z] = u0n[z + 1, 8 : span - 8, :]
    b1_out[...] = restrict(b_out, u0n, 1.0, r0, depth, c1[...])
    span1 = b1_out.shape[1]
    presmooth(
        b1_out, b1_out[depth], b1_out[depth + 1], 0.25,
        edge_inside((span1, 128), rows // 2, HX // 2, HY // 2, EDGE // 2),
        w1, al1, be1, u1, u1n, depth,
    )
    u1_out[...] = u1n[pl.ds(1, depth)]
    c_out[...] = c_inner[...] + restrict(b1_out, u1n, 0.25, r1, depth, c2[...])
    own2 = HX // 4

    def send(out, start):
        for l in range(count):
            out[count + l // 8, l % 8 : l % 8 + 1, :] = c_out[l, start : start + 1, :]
            out[l] = c_out[l, start + 1 : start + HX2, :]

    @pl.when(even)
    def _():
        send(a_msg, own2 - 1)
        send(b_msg, own2)

    @pl.when(jnp.logical_not(even))
    def _():
        send(a_msg, own2)
        send(b_msg, own2 - 1)


def join_kernel(
    ext, edge, u_in, u_edge, b1_in, b1_edge, u1_in, u1_edge,
    k0, u0, wb0, al0, be0, u1, wb1, al1, be1, w0, w1,
):
    depth, small, cols = u_in.shape
    span = ext.shape[1]
    rows = span - 2 * HX

    def joined(inner, strip, halo, edge, patch):
        own = inner.shape[1]
        lane = lax.broadcasted_iota(jnp.int32, strip.shape, 1)
        turned = pltpu.roll(strip, 128 - 2 * halo, 1)
        outer = jnp.where(lane < halo, strip, jnp.where(lane >= 128 - halo, turned, 0.0))
        blocks = [inner[:, 128 * j : 128 * (j + 1)] for j in range(own // 128)]
        blocks[0] = jnp.where(lane < patch, turned, blocks[0])
        blocks[-1] = jnp.where(lane >= 128 - patch, strip, blocks[-1])
        return jnp.concatenate(blocks + [outer], 1)

    part0 = lambda inner, strip: joined(inner, strip, HY, EDGE, EDGE // 2)
    part1 = lambda inner, strip: joined(inner, strip, HY // 2, EDGE // 2, EDGE // 4)
    low, top = 8, span - 8
    lanes = cols + 128
    for i in (0, 1):
        k0[i] = part0(ext[depth + i, low:top, :], edge[depth + i, low:top, :])
    weights(
        k0[0], k0[1], 1.0, wide_inside((small, lanes), rows, HX - low, cols, HY), w0, al0, be0,
    )
    span1, half = b1_in.shape[1], b1_in.shape[2]
    kh1, kv1 = (part1(b1_in[depth + i], b1_edge[depth + i]) for i in (0, 1))
    weights(
        kh1, kv1, 0.25, wide_inside((span1, 2 * half), rows // 2, HX // 2, half, HY // 2), w1, al1, be1,
    )
    for z in range(depth):
        i = min(z, 1)
        u0[z] = part0(u_in[z], u_edge[z])
        wb0[z] = w0[i] * part0(ext[z, low:top, :], edge[z, low:top, :])
        u1[z] = part1(u1_in[z], u1_edge[z])
        wb1[z] = w1[i] * part1(b1_in[z], b1_edge[z])


def up_kernel(
    c_in, xa, xb, ext, k0, u0, wb0, al0, be0, u1, wb1, al1, be1, p1, p2,
    potential, residual,
    b2, w2, al2, be2, wb2, u2, u2n, f1, f1n, f0, f0n, e1, e0, pot, res, sems,
):
    count = c_in.shape[0]
    depth = count - 2
    rows, cols = potential.shape[1:]
    rows2 = rows // 4
    even = lax.axis_index("tile") % 2 == 0
    own2 = HX // 4
    span2 = b2.shape[1]
    end2 = rows2 + 2 * HX2

    def put(x, start):
        for l in range(count):
            b2[l, start : start + 1, :] = x[count + l // 8, l % 8 : l % 8 + 1, :]
            b2[l, start + 1 : start + HX2, :] = x[l]

    @pl.when(even)
    def _():
        put(xa, HX2 + rows2)
        put(xb, 0)

    @pl.when(jnp.logical_not(even))
    def _():
        put(xa, 0)
        put(xb, HX2 + rows2)

    lanes2 = b2.shape[2]
    for l in range(count):
        b2[l, HX2 : HX2 + rows2, :] = c_in[l, own2 : own2 + rows2, :]
        b2[l, end2:span2, :] = jnp.zeros((span2 - end2, lanes2), jnp.float32)
    row = lax.broadcasted_iota(jnp.int32, (span2, lanes2), 0)
    inside2 = wide_inside((span2, lanes2), rows2, HX2, cols // 4, HY // 4)
    weights(b2[depth], b2[depth + 1], 0.0625, inside2 & (row < end2), w2, al2, be2)
    zero_ends(u2, u2n, f1, f1n, f0, f0n)

    def first2(z, c):
        v = w2[jnp.minimum(z, 1)] * b2[z]
        wb2[z] = v
        u2[z + 1] = v
        return c

    loop(depth, first2, 4)
    src, dst = u2, u2n
    for _ in range(COARSE - 1):
        sweep(src, dst, wb2, al2, be2, depth)
        src, dst = dst, src

    span1, lanes1 = u1.shape[1], u1.shape[2]
    off2 = HX2 - own2
    coarse = jnp.concatenate([src[z + 1][off2 : off2 + span1 // 2] for z in range(depth)], 0)
    fine = exact_dot(coarse, p2[...])
    for z in range(depth):
        rows_doubled(e1, z, fine[z * (span1 // 2) : (z + 1) * (span1 // 2)])

    def first1(z, c):
        f1[z + 1] = u1[z] + blocks_in(e1, z)
        return c

    loop(depth, first1, 8)
    sweep(f1, f1n, wb1, al1, be1, depth)
    sweep(f1n, f1, wb1, al1, be1, depth)

    span0, lanes0 = u0.shape[1], u0.shape[2]
    above = (span0 - rows) // 2
    off1 = (HX - above) // 2
    fine = exact_dot(f1[pl.ds(1, depth)].reshape(depth * span1, lanes1), p1[...])
    for z in range(depth):
        rows_doubled(e0, z, fine[z * span1 + off1 : z * span1 + off1 + span0 // 2])

    def first0(z, c):
        f0[z + 1] = u0[z] + blocks_in(e0, z)
        return c

    loop(depth, first0, 15)
    sweep(f0, f0n, wb0, al0, be0, depth)
    sweep(f0n, f0, wb0, al0, be0, depth)

    copies = []

    def ship(src, dst, first, n):
        copy = pltpu.make_async_copy(src.at[pl.ds(first, n)], dst.at[pl.ds(first, n)], sems.at[len(copies)])
        copy.start()
        copies.append(copy)

    for z in range(depth):
        pot[z] = f0[z + 1, above : above + rows, 0:cols]
    ship(pot, potential, 0, depth)
    chunk = depth // 4
    for z in range(depth):
        b = ext[z, HX - above : HX - above + span0, :]
        r = residual_of(f0, z, b, k0[0, :, 0:cols], k0[1, :, 0:cols], 1.0, cols)
        res[z] = r[above : above + rows]
        if z % chunk == chunk - 1:
            ship(res, residual, z + 1 - chunk, chunk)
    for copy in copies:
        copy.wait()


VM = pl.BlockSpec(memory_space=pltpu.VMEM)


def call(kernel, outs, scratch, *args, aliases={}):
    f32 = lambda shape: jax.ShapeDtypeStruct(shape, jnp.float32)
    return pl.pallas_call(
        kernel,
        out_shape=[f32(s) for s in outs],
        in_specs=[VM] * len(args),
        out_specs=[VM] * len(outs),
        scratch_shapes=[pltpu.VMEM(s, jnp.float32) for s in scratch],
        input_output_aliases=aliases,
        compiler_params=pltpu.CompilerParams(vmem_limit_bytes=24 << 20),
    )(*args)


def body(right_side, horiz_coef, vert_coef, panel_owner, panel_cell, panel_pressure):
    depth, rows, cols = right_side.shape
    tiles = lax.axis_size("tile")
    y_axes = ("strip", "sub")
    y_count = lax.axis_size("strip") * lax.axis_size("sub")
    count = depth + 2
    span = rows + 2 * HX
    wide1, wide2, inner2, edge1, edge2 = lane_maps(cols)
    mean = lambda lanes, width: jnp.asarray(0.25 * selection(lanes, width), jnp.bfloat16)
    spread = lambda lanes, width: jnp.asarray(selection(lanes, width).T, jnp.bfloat16)
    c1_inner, c2_inner = mean(wide1[:cols], cols // 2), mean(inner2, cols // 2)
    c1_edge, c2_edge = mean(edge1, 128), mean(edge2, cols // 2)
    p1, p2 = spread(wide1, cols), spread(wide2, cols // 2)

    message = (count + count // 2, 8, cols)
    f32 = lambda shape: jax.ShapeDtypeStruct(shape, jnp.float32)
    early = (count // SLABS, rows, 128)
    x_own, panels, a, b = pl.pallas_call(
        load_kernel,
        out_shape=[f32((count, rows, cols)), f32((1, 8, 128)), f32(message), f32(message)],
        in_specs=[pl.BlockSpec(memory_space=pltpu.HBM)] * 6,
        out_specs=[VM] * 4,
        scratch_shapes=[pltpu.VMEM((2, 4, 128), jnp.int32), pltpu.SemaphoreType.DMA((6,))],
        compiler_params=pltpu.CompilerParams(vmem_limit_bytes=8 << 20),
    )(
        *[
            pltpu.with_memory_space_constraint(x, pltpu.HBM)
            for x in (
                right_side, horiz_coef, vert_coef,
                panel_owner.reshape(4, -1), panel_cell.reshape(4, -1), panel_pressure.reshape(4, -1),
            )
        ]
    )
    near = lax.ppermute(panels, "tile", [(i, i ^ 1) for i in range(tiles)])
    a = neighbour_swap(a, "tile", 0, "sub")
    b = neighbour_swap(b, "tile", 1, "sub")
    sub_own, strip_own = call(own_columns_kernel, [early, early], [], x_own)
    sub_own = neighbour_swap(sub_own, y_axes, 0, "group")
    strip_own = neighbour_swap(strip_own, y_axes, 1, "group")
    panels = jnp.concatenate([panels, near], 0)
    step = 2
    while step < tiles:
        swap = [(i, i ^ step) for i in range(tiles)]
        panels = jnp.concatenate([panels, lax.ppermute(panels, "tile", swap)], 0)
        step *= 2

    slabs = (count // SLABS + 1, 2 * HX, 128)
    ext, sub, strip = call(
        forcing_kernel, [(count, span, cols), slabs, slabs], [],
        x_own, a, b, panels,
    )
    sub = neighbour_swap(sub, y_axes, 0, "group")
    strip = neighbour_swap(strip, y_axes, 1, "group")

    lanes, half = cols + 128, cols // 2
    small = span - 16
    span1 = (span + 8) // 2
    span2 = span1 // 2

    def down_scratch(width, width1):
        return (
            [(2, span, width)] * 3 + [(depth + 2, span, width)] * 2 + [(count, width // 128, span + 8, 128)]
            + [(2, span1, width1)] * 3 + [(depth + 2, span1, width1)] * 2 + [(count, width1 // 128, span1, 128)]
        )

    u_in, b1_in, u1_in, c_in = call(
        inner_kernel,
        [(depth, small, cols), (count, span1, half), (depth, span1, half), (count, span2, half)],
        down_scratch(cols, half),
        ext, c1_inner, c2_inner,
    )
    (base,) = call(base_kernel, [(count, span, 128)], [], ext, sub_own, strip_own)
    message2 = (count + (count + 7) // 8, 8, half)
    edge, u_edge, b1_edge, u1_edge, c_own, a2, b2 = call(
        edge_kernel,
        [
            (count, span, 128), (depth, small, 128), (count, span1, 128), (depth, span1, 128),
            (count, span2, half), message2, message2,
        ],
        down_scratch(128, 128),
        base, sub, strip, c_in, c1_edge, c2_edge,
        aliases={0: 0},
    )
    a2 = neighbour_swap(a2, "tile", 0, "sub")
    b2 = neighbour_swap(b2, "tile", 1, "sub")

    pair0, field = (2, small, lanes), (depth, small, lanes)
    pair1, field1 = (2, span1, cols), (depth, span1, cols)
    state = call(
        join_kernel,
        [pair0, field, field, pair0, pair0, field1, field1, pair1, pair1],
        [pair0, pair1],
        ext, edge, u_in, u_edge, b1_in, b1_edge, u1_in, u1_edge,
    )

    wide2 = 32
    field2 = (depth + 2, wide2, half)
    own = right_side.shape
    potential, residual = pl.pallas_call(
        up_kernel,
        out_shape=[f32(own), f32(own)],
        in_specs=[VM] * (6 + len(state)),
        out_specs=[pl.BlockSpec(memory_space=pltpu.HBM)] * 2,
        scratch_shapes=[
            pltpu.VMEM(shape, jnp.float32)
            for shape in (
                (count, wide2, half), (2, wide2, half), (2, wide2, half), (2, wide2, half), (depth, wide2, half),
                field2, field2, (depth + 2, span1, cols), (depth + 2, span1, cols),
                (depth + 2, small, lanes), (depth + 2, small, lanes),
                (depth, cols // 128, span1, 128), (depth, lanes // 128, small, 128), own, own,
            )
        ]
        + [pltpu.SemaphoreType.DMA((5,))],
        compiler_params=pltpu.CompilerParams(vmem_limit_bytes=24 << 20),
    )(c_own, a2, b2, ext, *state, p1, p2)
    return potential, residual


def solution(mesh):
    return jax.shard_map(
        body,
        mesh=mesh,
        in_specs=(
            jax.P("group", "tile", ("strip", "sub")),
            jax.P(("group", "tile"), ("strip", "sub")),
            jax.P(("group", "tile"), ("strip", "sub")),
            jax.P(("group", "tile", "strip", "sub"), None),
            jax.P(("group", "tile", "strip", "sub")),
            jax.P(("group", "tile", "strip", "sub")),
        ),
        out_specs=(
            jax.P("group", "tile", ("strip", "sub")),
            jax.P("group", "tile", ("strip", "sub")),
        ),
        check_vma=False,
    )
```

```python
import jax
import jax.numpy as jnp
import numpy as np
from jax import lax
from jax.experimental import pallas as pl
from jax.experimental.pallas import tpu as pltpu

COARSE = 8
OMEGA = 0.8

HX = 12
HX2 = 9
HY = 42
LIMIT = 512
SLABS = 3
EDGE = 16


def neighbour_swap(x, axis, odd, spare):
    axis = axis if isinstance(axis, tuple) else (axis,)
    count = lax.axis_size(axis)
    twins = lax.axis_size(spare)
    leading = spare == "group"
    place = lambda i, twin: twin * count + i if leading else i * twins + twin
    pairs = []
    for twin in range(twins):
        for i in range(count):
            j, other = (i + 1 if i % 2 == odd else i - 1), twin
            if not 0 <= j < count:
                j, other = i, twin ^ 1
            pairs.append((place(i, twin), place(j, other)))
    return lax.ppermute(x, (spare,) + axis if leading else axis + (spare,), pairs)


def lane_maps(cols):
    half, quarter, h1, h2 = cols // 2, cols // 4, HY // 2, HY // 4
    wide1 = -np.ones(cols + 128, np.int64)
    wide1[:cols] = np.arange(cols) // 2
    wide1[cols : cols + HY] = half + np.arange(HY) // 2
    wide1[cols + 128 - HY :] = 2 * half - h1 + np.arange(HY) // 2
    wide2 = -np.ones(2 * half, np.int64)
    wide2[:half] = np.arange(half) // 2
    wide2[half : half + 2 * h2] = quarter + np.arange(2 * h2) // 2
    wide2[2 * half - 2 * h2 :] = 2 * quarter - h2 + np.arange(2 * h2) // 2
    inner2 = -np.ones(half, np.int64)
    inner2[4 : half - 4] = np.arange(4, half - 4) // 2
    edge1 = -np.ones(128, np.int64)
    edge1[: 2 * HY + EDGE] = np.arange(2 * HY + EDGE) // 2
    edge1[128 - EDGE :] = 128 - EDGE // 2 + np.arange(EDGE) // 2
    edge2 = -np.ones(128, np.int64)
    edge2[: 2 * h2] = quarter + np.arange(2 * h2) // 2
    edge2[2 * h1 - 2 * h2 : 2 * h1] = 2 * quarter - h2 + np.arange(2 * h2) // 2
    edge2[2 * h1 : 2 * h1 + 4] = np.arange(4) // 2
    edge2[124:] = quarter - 2 + np.arange(4) // 2
    return wide1, wide2, inner2, edge1, edge2


def selection(lanes, width):
    return (lanes[:, None] == np.arange(width)[None, :]).astype(np.float32)


def split(x, parts):
    out = []
    for _ in range(parts):
        out.append(x.astype(jnp.bfloat16))
        x = x - out[-1].astype(jnp.float32)
    return out


def exact_dot(left, right):
    return jnp.dot(jnp.concatenate(split(left, 2), 1), jnp.concatenate([right, right], 0), preferred_element_type=jnp.float32)


def neighbours(u):
    rows, lanes = u.shape
    return (
        pltpu.roll(u, 1, 0)
        + pltpu.roll(u, rows - 1, 0)
        + pltpu.roll(u, 1, 1)
        + pltpu.roll(u, lanes - 1, 1)
    )


def weights(kh, kv, scale, inside, w_ref, a_ref, b_ref):
    for i, layers in enumerate((1.0, 2.0)):
        diag = 4.0 * scale * kh + layers * kv
        w = jnp.where(inside, OMEGA / jnp.where(inside, diag, 1.0), 0.0)
        if w_ref is not None:
            w_ref[i] = w
        a_ref[i] = w * (scale * kh)
        b_ref[i] = w * kv


def loop(depth, fn, vregs):
    lax.fori_loop(0, depth, fn, 0, unroll=max(1, min(depth, LIMIT // vregs)))


def sweep(src, dst, wb, a_ref, b_ref, depth):
    def layer(z, c):
        i = jnp.minimum(z, 1)
        u = src[z + 1]
        dst[z + 1] = (
            (1.0 - OMEGA) * u
            + wb[z]
            + a_ref[i] * neighbours(u)
            + b_ref[i] * (src[z] + src[z + 2])
        )
        return c

    loop(depth, layer, src.shape[1] * src.shape[2] // 1024)


def residual_of(src, z, b, kh, kv, scale, lanes=None):
    layers = jnp.where(z == 0, 1.0, 2.0)
    u = src[z + 1]
    around = neighbours(u)[:, :lanes]
    u = u[:, :lanes]
    return b + (scale * kh) * (around - 4.0 * u) + kv * (src[z, :, :lanes] + src[z + 2, :, :lanes] - layers * u)


def blocks_out(ref, l, x):
    for j in range(ref.shape[1]):
        ref[l, j, 0 : x.shape[0], :] = x[:, 128 * j : 128 * (j + 1)]


def blocks_in(ref, l):
    return jnp.concatenate([ref[l, j] for j in range(ref.shape[1])], 1)


def rows_doubled(ref, l, part):
    n = part.shape[0]
    for j in range(ref.shape[1]):
        for s in (0, 1):
            ref[l, j, pl.ds(s, n, stride=2), :] = part[:, 128 * j : 128 * (j + 1)]


def slab_of(layers, at_right):
    shape = layers[0].shape
    lane = lax.broadcasted_iota(jnp.int32, shape, 1)
    out = jnp.zeros(shape, jnp.float32)
    for k, x in enumerate(layers):
        shift = (HY * (k + 1) if at_right else HY * k) % 128
        x = pltpu.roll(x, shift, 1) if shift else x
        out = jnp.where((lane >= HY * k) & (lane < HY * (k + 1)), x, out)
    return out


def load_kernel(rs, kh, kv, owner, cell, pressure, x, panels, a_out, b_out, ints, sems):
    depth, rows, cols = rs.shape
    count = depth + 2
    half = count // 2
    even = lax.axis_index("tile") % 2 == 0
    copies = [
        pltpu.make_async_copy(src, dst, sems.at[i])
        for i, (src, dst) in enumerate(
            (
                (owner, ints.at[0]),
                (cell, ints.at[1]),
                (pressure, panels.at[0, pl.ds(4, 4)]),
                (rs, x.at[pl.ds(0, depth)]),
                (kh, x.at[depth]),
                (kv, x.at[depth + 1]),
            )
        )
    ]
    for copy in copies:
        copy.start()
    for copy in copies:
        copy.wait()
    panels[0, 0:4, :] = (ints[0] * (rows * cols) + ints[1]).astype(jnp.float32)

    def first(out):
        for l in range(count):
            out[l] = x[l, 0:8, :]
            out[count + l % half, 4 * (l // half) : 4 * (l // half) + 4, :] = x[l, 8:HX, :]

    def last(out):
        for l in range(count):
            out[l] = x[l, rows - 8 : rows, :]
            out[count + l % half, 4 * (l // half) : 4 * (l // half) + 4, :] = x[l, rows - HX : rows - 8, :]

    @pl.when(even)
    def _():
        last(a_out)
        first(b_out)

    @pl.when(jnp.logical_not(even))
    def _():
        first(a_out)
        last(b_out)


def own_columns_kernel(x, sub_out, strip_out):
    count, _, cols = x.shape
    _, _, y_even = y_sides()
    for g in range(count // SLABS):
        layers = range(SLABS * g, SLABS * g + SLABS)
        to_right = slab_of([x[l, :, cols - 128 : cols] for l in layers], True)
        to_left = slab_of([x[l, :, 0:128] for l in layers], False)
        sub_out[g] = jnp.where(y_even, to_right, to_left)
        strip_out[g] = jnp.where(y_even, to_left, to_right)


def forcing_kernel(x_own, xa, xb, panels, ext, sub_out, strip_out):
    count, rows, cols = x_own.shape
    depth = count - 2
    half = count // 2
    tile = lax.axis_index("tile")
    even = tile % 2 == 0
    high = rows + HX

    def upper(x):
        for l in range(count):
            ext[l, 0:4, :] = x[count + l % half, 4 * (l // half) : 4 * (l // half) + 4, :]
            ext[l, 4:HX, :] = x[l]

    def lower(x):
        for l in range(count):
            ext[l, high : high + 8, :] = x[l]
            ext[l, high + 8 : high + HX, :] = x[count + l % half, 4 * (l // half) : 4 * (l // half) + 4, :]

    @pl.when(even)
    def _():
        lower(xa)
        upper(xb)

    @pl.when(jnp.logical_not(even))
    def _():
        upper(xa)
        lower(xb)

    for l in range(count):
        ext[l, HX:high, :] = x_own[l]

    span = rows + 2 * HX
    left, right = [], []
    for g in range(panels.shape[0]):
        group = panels[g]
        for k in range(4):
            code = group[k : k + 1].astype(jnp.int32)
            value = group[4 + k : 5 + k]
            row = code // cols - (tile * rows - HX)
            col = code % cols
            hit = row == lax.broadcasted_iota(jnp.int32, (span, 128), 0)
            left.append(jnp.where(hit, value, 0.0))
            right.append(
                jnp.where(col == lax.broadcasted_iota(jnp.int32, (cols, 128), 0), 1.0, 0.0).astype(jnp.bfloat16)
            )
    left = jnp.concatenate(left, 1)
    right = jnp.concatenate(right, 1)
    parts = lax.dot_general(
        jnp.concatenate(split(left, 3), 0), right, (((1,), (1,)), ((), ())), preferred_element_type=jnp.float32
    )
    total = parts[0:span] + parts[span : 2 * span] + parts[2 * span :]
    ext[depth - 1] = ext[depth - 1] + total

    _, _, y_even = y_sides()
    slabs = count // SLABS

    def send(g, to_right, to_left):
        sub_out[g] = jnp.where(y_even, to_right, to_left)
        strip_out[g] = jnp.where(y_even, to_left, to_right)

    def corners(l, first):
        return jnp.concatenate(
            [ext[l, 0:HX, first : first + 128], ext[l, high : high + HX, first : first + 128]], 0
        )

    for g in range(slabs):
        layers = range(SLABS * g, SLABS * g + SLABS)
        send(g, slab_of([corners(l, cols - 128) for l in layers], True), slab_of([corners(l, 0) for l in layers], False))
    pad = jnp.zeros((2 * HX - rows // 2, 128), jnp.float32)
    halves = [total[HX : HX + rows // 2], total[HX + rows // 2 : high]]
    send(
        slabs,
        jnp.concatenate([slab_of([x[:, cols - 128 :] for x in halves], True), pad], 0),
        jnp.concatenate([slab_of([x[:, :128] for x in halves], False), pad], 0),
    )


def rolled(x, shift):
    return pltpu.roll(x, shift % 128, 1) if shift % 128 else x


def base_kernel(ext, ysub, ystrip, base):
    count, span, cols = ext.shape
    high = span - HX
    _, _, y_even = y_sides()
    lane = lax.broadcasted_iota(jnp.int32, (span, 128), 1)
    lane_own = lane[HX:high]
    for g in range(count // SLABS):
        from_right = jnp.where(y_even, ysub[g], ystrip[g])
        from_left = jnp.where(y_even, ystrip[g], ysub[g])
        for k in range(SLABS):
            l = SLABS * g + k
            x = jnp.where(lane >= 128 - EDGE, ext[l, :, cols - 128 : cols], 0.0)
            x = jnp.where((lane >= 2 * HY) & (lane < 2 * HY + EDGE), rolled(ext[l, :, 0:128], 2 * HY), x)
            base[l] = x
            outer = jnp.where(lane_own < HY, rolled(from_right, -HY * k), rolled(from_left, HY - HY * k))
            base[l, HX:high, :] = jnp.where(lane_own < 2 * HY, outer, x[HX:high])


def row_inside(shape, rows, above):
    row = lax.axis_index("tile") * rows - above + lax.broadcasted_iota(jnp.int32, shape, 0)
    return (row >= 0) & (row < lax.axis_size("tile") * rows)


def y_sides():
    y = lax.axis_index("strip") * lax.axis_size("sub") + lax.axis_index("sub")
    return y > 0, y < lax.axis_size("strip") * lax.axis_size("sub") - 1, y % 2 == 0


def wide_inside(shape, rows, above, own, halo):
    has_left, has_right, _ = y_sides()
    column = lax.broadcasted_iota(jnp.int32, shape, 1)
    right = (column >= own) & (column < own + halo) & has_right
    left = (column >= shape[1] - halo) & has_left
    return row_inside(shape, rows, above) & ((column < own) | right | left)


def edge_inside(shape, rows, above, halo, edge):
    has_left, has_right, _ = y_sides()
    column = lax.broadcasted_iota(jnp.int32, shape, 1)
    right = (column < halo) & has_right
    left = (column >= halo) & (column < 2 * halo) & has_left
    own = ((column >= 2 * halo) & (column < 2 * halo + edge)) | (column >= 128 - edge)
    return row_inside(shape, rows, above) & (own | right | left)


def zero_ends(*refs):
    for ref in refs:
        ref[0] = jnp.zeros(ref.shape[1:], jnp.float32)
        ref[ref.shape[0] - 1] = jnp.zeros(ref.shape[1:], jnp.float32)


def presmooth(source, kh, kv, scale, inside, w, al, be, u, un, depth):
    weights(kh, kv, scale, inside, w, al, be)
    zero_ends(u, un)

    def first(z, c):
        u[z + 1] = w[jnp.minimum(z, 1)] * source[z]
        return c

    loop(depth, first, u.shape[1] * u.shape[2] // 1024)
    sweep(u, un, u.at[pl.ds(1, depth)], al, be, depth)


def restrict(source, un, scale, r, depth, parts):
    kh, kv = source[depth], source[depth + 1]
    rows = kh.shape[0]
    for l in range(depth + 2):
        for j in range(r.shape[1]):
            if r.shape[2] > rows:
                r[l, j, rows:, :] = jnp.zeros((r.shape[2] - rows, 128), jnp.float32)
    blocks_out(r, depth, kh)
    blocks_out(r, depth + 1, kv)

    def rest(z, c):
        blocks_out(r, z, residual_of(un, z, source[z], source[depth], source[depth + 1], scale))
        return c

    loop(depth, rest, rows * kh.shape[1] // 1024)
    n = r.shape[2] // 2
    pairs = jnp.concatenate(
        [
            jnp.concatenate(
                [r[l, j, pl.ds(0, n, stride=2), :] + r[l, j, pl.ds(1, n, stride=2), :] for j in range(r.shape[1])], 1
            )
            for l in range(depth + 2)
        ],
        0,
    )
    return exact_dot(pairs, parts).reshape(depth + 2, n, parts.shape[1])


def inner_kernel(
    ext, c1, c2, u_out, b1_out, u1_out, c_out,
    w0, al0, be0, u0, u0n, r0, w1, al1, be1, u1, u1n, r1,
):
    depth, span, cols = ext.shape[0] - 2, ext.shape[1], ext.shape[2]
    rows = span - 2 * HX
    presmooth(
        ext, ext[depth], ext[depth + 1], 1.0, row_inside((span, cols), rows, HX), w0, al0, be0, u0, u0n, depth
    )
    for z in range(depth):
        u_out[z] = u0n[z + 1, 8 : span - 8, :]
    b1_out[...] = restrict(ext, u0n, 1.0, r0, depth, c1[...])
    span1, half = b1_out.shape[1], b1_out.shape[2]
    presmooth(
        b1_out, b1_out[depth], b1_out[depth + 1], 0.25, row_inside((span1, half), rows // 2, HX // 2),
        w1, al1, be1, u1, u1n, depth,
    )
    u1_out[...] = u1n[pl.ds(1, depth)]
    c_out[...] = restrict(b1_out, u1n, 0.25, r1, depth, c2[...])


def edge_kernel(
    base, ysub, ystrip, c_inner, c1, c2,
    b_out, u_out, b1_out, u1_out, c_out, a_msg, b_msg,
    w0, al0, be0, u0, u0n, r0, w1, al1, be1, u1, u1n, r1,
):
    count, span = base.shape[:2]
    depth = count - 2
    rows = span - 2 * HX
    high = span - HX
    even = lax.axis_index("tile") % 2 == 0
    _, _, y_even = y_sides()
    slabs = count // SLABS
    lane = lax.broadcasted_iota(jnp.int32, (2 * HX, 128), 1)
    for g in range(slabs):
        from_right = jnp.where(y_even, ysub[g], ystrip[g])
        from_left = jnp.where(y_even, ystrip[g], ysub[g])
        for k in range(SLABS):
            l = SLABS * g + k
            outer = jnp.where(lane < HY, rolled(from_right, -HY * k), rolled(from_left, HY - HY * k))
            b_out[l, 0:HX, :] = jnp.where(lane[:HX] < 2 * HY, outer[:HX], base[l, 0:HX, :])
            b_out[l, high:span, :] = jnp.where(lane[HX:] < 2 * HY, outer[HX:], base[l, high:span, :])
    half = rows // 2
    lane = lane[:half]
    from_right = jnp.where(y_even, ysub[slabs, :half], ystrip[slabs, :half])
    from_left = jnp.where(y_even, ystrip[slabs, :half], ysub[slabs, :half])
    for k in (0, 1):
        force = jnp.where(lane < HY, rolled(from_right, -HY * k), rolled(from_left, HY - HY * k))
        part = pl.ds(HX + half * k, half)
        b_out[depth - 1, part, :] = base[depth - 1, part, :] + jnp.where(lane < 2 * HY, force, 0.0)
    presmooth(
        b_out, b_out[depth], b_out[depth + 1], 1.0, edge_inside((span, 128), rows, HX, HY, EDGE),
        w0, al0, be0, u0, u0n, depth,
    )
    for z in range(depth):
        u_out[z] = u0n[z + 1, 8 : span - 8, :]
    b1_out[...] = restrict(b_out, u0n, 1.0, r0, depth, c1[...])
    span1 = b1_out.shape[1]
    presmooth(
        b1_out, b1_out[depth], b1_out[depth + 1], 0.25,
        edge_inside((span1, 128), rows // 2, HX // 2, HY // 2, EDGE // 2),
        w1, al1, be1, u1, u1n, depth,
    )
    u1_out[...] = u1n[pl.ds(1, depth)]
    c_out[...] = c_inner[...] + restrict(b1_out, u1n, 0.25, r1, depth, c2[...])
    own2 = HX // 4

    def send(out, start):
        for l in range(count):
            out[count + l // 8, l % 8 : l % 8 + 1, :] = c_out[l, start : start + 1, :]
            out[l] = c_out[l, start + 1 : start + HX2, :]

    @pl.when(even)
    def _():
        send(a_msg, own2 - 1)
        send(b_msg, own2)

    @pl.when(jnp.logical_not(even))
    def _():
        send(a_msg, own2)
        send(b_msg, own2 - 1)


def join_kernel(
    ext, edge, u_in, u_edge, b1_in, b1_edge, u1_in, u1_edge,
    k0, u0, wb0, al0, be0, u1, wb1, al1, be1, w0, w1,
):
    depth, small, cols = u_in.shape
    span = ext.shape[1]
    rows = span - 2 * HX

    def joined(inner, strip, halo, edge, patch):
        own = inner.shape[1]
        lane = lax.broadcasted_iota(jnp.int32, strip.shape, 1)
        turned = pltpu.roll(strip, 128 - 2 * halo, 1)
        outer = jnp.where(lane < halo, strip, jnp.where(lane >= 128 - halo, turned, 0.0))
        blocks = [inner[:, 128 * j : 128 * (j + 1)] for j in range(own // 128)]
        blocks[0] = jnp.where(lane < patch, turned, blocks[0])
        blocks[-1] = jnp.where(lane >= 128 - patch, strip, blocks[-1])
        return jnp.concatenate(blocks + [outer], 1)

    part0 = lambda inner, strip: joined(inner, strip, HY, EDGE, EDGE // 2)
    part1 = lambda inner, strip: joined(inner, strip, HY // 2, EDGE // 2, EDGE // 4)
    low, top = 8, span - 8
    lanes = cols + 128
    for i in (0, 1):
        k0[i] = part0(ext[depth + i, low:top, :], edge[depth + i, low:top, :])
    weights(
        k0[0], k0[1], 1.0, wide_inside((small, lanes), rows, HX - low, cols, HY), w0, al0, be0,
    )
    span1, half = b1_in.shape[1], b1_in.shape[2]
    kh1, kv1 = (part1(b1_in[depth + i], b1_edge[depth + i]) for i in (0, 1))
    weights(
        kh1, kv1, 0.25, wide_inside((span1, 2 * half), rows // 2, HX // 2, half, HY // 2), w1, al1, be1,
    )
    for z in range(depth):
        i = min(z, 1)
        u0[z] = part0(u_in[z], u_edge[z])
        wb0[z] = w0[i] * part0(ext[z, low:top, :], edge[z, low:top, :])
        u1[z] = part1(u1_in[z], u1_edge[z])
        wb1[z] = w1[i] * part1(b1_in[z], b1_edge[z])


def up_kernel(
    c_in, xa, xb, ext, k0, u0, wb0, al0, be0, u1, wb1, al1, be1, p1, p2,
    potential, residual,
    b2, w2, al2, be2, wb2, u2, u2n, f1, f1n, f0, f0n, e1, e0, pot, res, sems,
):
    count = c_in.shape[0]
    depth = count - 2
    rows, cols = potential.shape[1:]
    rows2 = rows // 4
    even = lax.axis_index("tile") % 2 == 0
    own2 = HX // 4
    span2 = b2.shape[1]
    end2 = rows2 + 2 * HX2

    def put(x, start):
        for l in range(count):
            b2[l, start : start + 1, :] = x[count + l // 8, l % 8 : l % 8 + 1, :]
            b2[l, start + 1 : start + HX2, :] = x[l]

    @pl.when(even)
    def _():
        put(xa, HX2 + rows2)
        put(xb, 0)

    @pl.when(jnp.logical_not(even))
    def _():
        put(xa, 0)
        put(xb, HX2 + rows2)

    lanes2 = b2.shape[2]
    for l in range(count):
        b2[l, HX2 : HX2 + rows2, :] = c_in[l, own2 : own2 + rows2, :]
        b2[l, end2:span2, :] = jnp.zeros((span2 - end2, lanes2), jnp.float32)
    row = lax.broadcasted_iota(jnp.int32, (span2, lanes2), 0)
    inside2 = wide_inside((span2, lanes2), rows2, HX2, cols // 4, HY // 4)
    weights(b2[depth], b2[depth + 1], 0.0625, inside2 & (row < end2), w2, al2, be2)
    zero_ends(u2, u2n, f1, f1n, f0, f0n)

    def first2(z, c):
        v = w2[jnp.minimum(z, 1)] * b2[z]
        wb2[z] = v
        u2[z + 1] = v
        return c

    loop(depth, first2, 4)
    src, dst = u2, u2n
    for _ in range(COARSE - 1):
        sweep(src, dst, wb2, al2, be2, depth)
        src, dst = dst, src

    span1, lanes1 = u1.shape[1], u1.shape[2]
    off2 = HX2 - own2
    coarse = jnp.concatenate([src[z + 1][off2 : off2 + span1 // 2] for z in range(depth)], 0)
    fine = exact_dot(coarse, p2[...])
    for z in range(depth):
        rows_doubled(e1, z, fine[z * (span1 // 2) : (z + 1) * (span1 // 2)])

    def first1(z, c):
        f1[z + 1] = u1[z] + blocks_in(e1, z)
        return c

    loop(depth, first1, 8)
    sweep(f1, f1n, wb1, al1, be1, depth)
    sweep(f1n, f1, wb1, al1, be1, depth)

    span0, lanes0 = u0.shape[1], u0.shape[2]
    above = (span0 - rows) // 2
    off1 = (HX - above) // 2
    end1 = off1 + span0 // 2
    fine = exact_dot(jnp.concatenate([f1[z + 1, 0:end1, :] for z in range(depth)], 0), p1[...])
    for z in range(depth):
        rows_doubled(e0, z, fine[z * end1 + off1 : (z + 1) * end1])

    def first0(z, c):
        f0[z + 1] = u0[z] + blocks_in(e0, z)[:span0]
        return c

    loop(depth, first0, 15)
    sweep(f0, f0n, wb0, al0, be0, depth)
    sweep(f0n, f0, wb0, al0, be0, depth)

    copies = []

    def ship(src, dst, first, n):
        copy = pltpu.make_async_copy(src.at[pl.ds(first, n)], dst.at[pl.ds(first, n)], sems.at[len(copies)])
        copy.start()
        copies.append(copy)

    for z in range(depth):
        pot[z] = f0[z + 1, above : above + rows, 0:cols]
    ship(pot, potential, 0, depth)
    chunk = depth // 4
    for z in range(depth):
        b = ext[z, HX - above : HX - above + span0, :]
        r = residual_of(f0, z, b, k0[0, :, 0:cols], k0[1, :, 0:cols], 1.0, cols)
        res[z] = r[above : above + rows]
        if z % chunk == chunk - 1:
            ship(res, residual, z + 1 - chunk, chunk)
    for copy in copies:
        copy.wait()


VM = pl.BlockSpec(memory_space=pltpu.VMEM)


def call(kernel, outs, scratch, *args, aliases={}):
    f32 = lambda shape: jax.ShapeDtypeStruct(shape, jnp.float32)
    return pl.pallas_call(
        kernel,
        out_shape=[f32(s) for s in outs],
        in_specs=[VM] * len(args),
        out_specs=[VM] * len(outs),
        scratch_shapes=[pltpu.VMEM(s, jnp.float32) for s in scratch],
        input_output_aliases=aliases,
        compiler_params=pltpu.CompilerParams(vmem_limit_bytes=24 << 20),
    )(*args)


def body(right_side, horiz_coef, vert_coef, panel_owner, panel_cell, panel_pressure):
    depth, rows, cols = right_side.shape
    tiles = lax.axis_size("tile")
    y_axes = ("strip", "sub")
    y_count = lax.axis_size("strip") * lax.axis_size("sub")
    count = depth + 2
    span = rows + 2 * HX
    wide1, wide2, inner2, edge1, edge2 = lane_maps(cols)
    mean = lambda lanes, width: jnp.asarray(0.25 * selection(lanes, width), jnp.bfloat16)
    spread = lambda lanes, width: jnp.asarray(selection(lanes, width).T, jnp.bfloat16)
    c1_inner, c2_inner = mean(wide1[:cols], cols // 2), mean(inner2, cols // 2)
    c1_edge, c2_edge = mean(edge1, 128), mean(edge2, cols // 2)
    p1, p2 = spread(wide1, cols), spread(wide2, cols // 2)

    message = (count + count // 2, 8, cols)
    f32 = lambda shape: jax.ShapeDtypeStruct(shape, jnp.float32)
    early = (count // SLABS, rows, 128)
    x_own, panels, a, b = pl.pallas_call(
        load_kernel,
        out_shape=[f32((count, rows, cols)), f32((1, 8, 128)), f32(message), f32(message)],
        in_specs=[pl.BlockSpec(memory_space=pltpu.HBM)] * 6,
        out_specs=[VM] * 4,
        scratch_shapes=[pltpu.VMEM((2, 4, 128), jnp.int32), pltpu.SemaphoreType.DMA((6,))],
        compiler_params=pltpu.CompilerParams(vmem_limit_bytes=8 << 20),
    )(
        *[
            pltpu.with_memory_space_constraint(x, pltpu.HBM)
            for x in (
                right_side, horiz_coef, vert_coef,
                panel_owner.reshape(4, -1), panel_cell.reshape(4, -1), panel_pressure.reshape(4, -1),
            )
        ]
    )
    near = lax.ppermute(panels, "tile", [(i, i ^ 1) for i in range(tiles)])
    a = neighbour_swap(a, "tile", 0, "sub")
    b = neighbour_swap(b, "tile", 1, "sub")
    sub_own, strip_own = call(own_columns_kernel, [early, early], [], x_own)
    sub_own = neighbour_swap(sub_own, y_axes, 0, "group")
    strip_own = neighbour_swap(strip_own, y_axes, 1, "group")
    panels = jnp.concatenate([panels, near], 0)
    step = 2
    while step < tiles:
        swap = [(i, i ^ step) for i in range(tiles)]
        panels = jnp.concatenate([panels, lax.ppermute(panels, "tile", swap)], 0)
        step *= 2

    slabs = (count // SLABS + 1, 2 * HX, 128)
    ext, sub, strip = call(
        forcing_kernel, [(count, span, cols), slabs, slabs], [],
        x_own, a, b, panels,
    )
    sub = neighbour_swap(sub, y_axes, 0, "group")
    strip = neighbour_swap(strip, y_axes, 1, "group")

    lanes, half = cols + 128, cols // 2
    small = span - 16
    span1 = (span + 8) // 2
    span2 = span1 // 2

    def down_scratch(width, width1):
        return (
            [(2, span, width)] * 3 + [(depth + 2, span, width)] * 2 + [(count, width // 128, span + 8, 128)]
            + [(2, span1, width1)] * 3 + [(depth + 2, span1, width1)] * 2 + [(count, width1 // 128, span1, 128)]
        )

    u_in, b1_in, u1_in, c_in = call(
        inner_kernel,
        [(depth, small, cols), (count, span1, half), (depth, span1, half), (count, span2, half)],
        down_scratch(cols, half),
        ext, c1_inner, c2_inner,
    )
    (base,) = call(base_kernel, [(count, span, 128)], [], ext, sub_own, strip_own)
    message2 = (count + (count + 7) // 8, 8, half)
    edge, u_edge, b1_edge, u1_edge, c_own, a2, b2 = call(
        edge_kernel,
        [
            (count, span, 128), (depth, small, 128), (count, span1, 128), (depth, span1, 128),
            (count, span2, half), message2, message2,
        ],
        down_scratch(128, 128),
        base, sub, strip, c_in, c1_edge, c2_edge,
        aliases={0: 0},
    )
    a2 = neighbour_swap(a2, "tile", 0, "sub")
    b2 = neighbour_swap(b2, "tile", 1, "sub")

    pair0, field = (2, small, lanes), (depth, small, lanes)
    pair1, field1 = (2, span1, cols), (depth, span1, cols)
    state = call(
        join_kernel,
        [pair0, field, field, pair0, pair0, field1, field1, pair1, pair1],
        [pair0, pair1],
        ext, edge, u_in, u_edge, b1_in, b1_edge, u1_in, u1_edge,
    )

    wide2 = 32
    field2 = (depth + 2, wide2, half)
    own = right_side.shape
    potential, residual = pl.pallas_call(
        up_kernel,
        out_shape=[f32(own), f32(own)],
        in_specs=[VM] * (6 + len(state)),
        out_specs=[pl.BlockSpec(memory_space=pltpu.HBM)] * 2,
        scratch_shapes=[
            pltpu.VMEM(shape, jnp.float32)
            for shape in (
                (count, wide2, half), (2, wide2, half), (2, wide2, half), (2, wide2, half), (depth, wide2, half),
                field2, field2, (depth + 2, span1, cols), (depth + 2, span1, cols),
                (depth + 2, small, lanes), (depth + 2, small, lanes),
                (depth, cols // 128, span1, 128), (depth, lanes // 128, small + 8, 128), own, own,
            )
        ]
        + [pltpu.SemaphoreType.DMA((5,))],
        compiler_params=pltpu.CompilerParams(vmem_limit_bytes=24 << 20),
    )(c_own, a2, b2, ext, *state, p1, p2)
    return potential, residual


def solution(mesh):
    return jax.shard_map(
        body,
        mesh=mesh,
        in_specs=(
            jax.P("group", "tile", ("strip", "sub")),
            jax.P(("group", "tile"), ("strip", "sub")),
            jax.P(("group", "tile"), ("strip", "sub")),
            jax.P(("group", "tile", "strip", "sub"), None),
            jax.P(("group", "tile", "strip", "sub")),
            jax.P(("group", "tile", "strip", "sub")),
        ),
        out_specs=(
            jax.P("group", "tile", ("strip", "sub")),
            jax.P("group", "tile", ("strip", "sub")),
        ),
        check_vma=False,
    )
```

```python
import jax
import jax.numpy as jnp
import numpy as np
from jax import lax
from jax.experimental import pallas as pl
from jax.experimental.pallas import tpu as pltpu

COARSE = 8
OMEGA = 0.8

HX = 12
HX2 = 9
HY = 42
LIMIT = 512
SLABS = 3
EDGE = 16


def neighbour_swap(x, axis, odd, spare):
    axis = axis if isinstance(axis, tuple) else (axis,)
    count = lax.axis_size(axis)
    twins = lax.axis_size(spare)
    leading = spare == "group"
    place = lambda i, twin: twin * count + i if leading else i * twins + twin
    pairs = []
    for twin in range(twins):
        for i in range(count):
            j, other = (i + 1 if i % 2 == odd else i - 1), twin
            if not 0 <= j < count:
                j, other = i, twin ^ 1
            pairs.append((place(i, twin), place(j, other)))
    return lax.ppermute(x, (spare,) + axis if leading else axis + (spare,), pairs)


def lane_maps(cols):
    half, quarter, h1, h2 = cols // 2, cols // 4, HY // 2, HY // 4
    wide1 = -np.ones(cols + 128, np.int64)
    wide1[:cols] = np.arange(cols) // 2
    wide1[cols : cols + HY] = half + np.arange(HY) // 2
    wide1[cols + 128 - HY :] = 2 * half - h1 + np.arange(HY) // 2
    wide2 = -np.ones(2 * half, np.int64)
    wide2[:half] = np.arange(half) // 2
    wide2[half : half + 2 * h2] = quarter + np.arange(2 * h2) // 2
    wide2[2 * half - 2 * h2 :] = 2 * quarter - h2 + np.arange(2 * h2) // 2
    inner2 = -np.ones(half, np.int64)
    inner2[4 : half - 4] = np.arange(4, half - 4) // 2
    edge1 = -np.ones(128, np.int64)
    edge1[: 2 * HY + EDGE] = np.arange(2 * HY + EDGE) // 2
    edge1[128 - EDGE :] = 128 - EDGE // 2 + np.arange(EDGE) // 2
    edge2 = -np.ones(128, np.int64)
    edge2[: 2 * h2] = quarter + np.arange(2 * h2) // 2
    edge2[2 * h1 - 2 * h2 : 2 * h1] = 2 * quarter - h2 + np.arange(2 * h2) // 2
    edge2[2 * h1 : 2 * h1 + 4] = np.arange(4) // 2
    edge2[124:] = quarter - 2 + np.arange(4) // 2
    return wide1, wide2, inner2, edge1, edge2


def selection(lanes, width):
    return (lanes[:, None] == np.arange(width)[None, :]).astype(np.float32)


def split(x, parts):
    out = []
    for _ in range(parts):
        out.append(x.astype(jnp.bfloat16))
        x = x - out[-1].astype(jnp.float32)
    return out


def exact_dot(left, right):
    return jnp.dot(jnp.concatenate(split(left, 2), 1), jnp.concatenate([right, right], 0), preferred_element_type=jnp.float32)


def neighbours(u):
    rows, lanes = u.shape
    return (
        pltpu.roll(u, 1, 0)
        + pltpu.roll(u, rows - 1, 0)
        + pltpu.roll(u, 1, 1)
        + pltpu.roll(u, lanes - 1, 1)
    )


def weights(kh, kv, scale, inside, w_ref, a_ref, b_ref):
    for i, layers in enumerate((1.0, 2.0)):
        diag = 4.0 * scale * kh + layers * kv
        w = jnp.where(inside, OMEGA / jnp.where(inside, diag, 1.0), 0.0)
        if w_ref is not None:
            w_ref[i] = w
        a_ref[i] = w * (scale * kh)
        b_ref[i] = w * kv


def loop(depth, fn, vregs):
    lax.fori_loop(0, depth, fn, 0, unroll=max(1, min(depth, LIMIT // vregs)))


def sweep(src, dst, wb, a_ref, b_ref, depth):
    def layer(z, c):
        i = jnp.minimum(z, 1)
        u = src[z + 1]
        dst[z + 1] = (
            (1.0 - OMEGA) * u
            + wb[z]
            + a_ref[i] * neighbours(u)
            + b_ref[i] * (src[z] + src[z + 2])
        )
        return c

    loop(depth, layer, src.shape[1] * src.shape[2] // 1024)


def residual_of(src, z, b, kh, kv, scale, lanes=None):
    layers = jnp.where(z == 0, 1.0, 2.0)
    u = src[z + 1]
    around = neighbours(u)[:, :lanes]
    u = u[:, :lanes]
    return b + (scale * kh) * (around - 4.0 * u) + kv * (src[z, :, :lanes] + src[z + 2, :, :lanes] - layers * u)


def blocks_out(ref, l, x):
    for j in range(ref.shape[1]):
        ref[l, j, 0 : x.shape[0], :] = x[:, 128 * j : 128 * (j + 1)]


def blocks_in(ref, l):
    return jnp.concatenate([ref[l, j] for j in range(ref.shape[1])], 1)


def rows_doubled(ref, l, part):
    n = part.shape[0]
    for j in range(ref.shape[1]):
        for s in (0, 1):
            ref[l, j, pl.ds(s, n, stride=2), :] = part[:, 128 * j : 128 * (j + 1)]


def slab_of(layers, at_right):
    shape = layers[0].shape
    lane = lax.broadcasted_iota(jnp.int32, shape, 1)
    out = jnp.zeros(shape, jnp.float32)
    for k, x in enumerate(layers):
        shift = (HY * (k + 1) if at_right else HY * k) % 128
        x = pltpu.roll(x, shift, 1) if shift else x
        out = jnp.where((lane >= HY * k) & (lane < HY * (k + 1)), x, out)
    return out


def load_kernel(rs, kh, kv, owner, cell, pressure, x, panels, a_out, b_out, ints, sems):
    depth, rows, cols = rs.shape
    count = depth + 2
    half = count // 2
    even = lax.axis_index("tile") % 2 == 0
    copies = [
        pltpu.make_async_copy(src, dst, sems.at[i])
        for i, (src, dst) in enumerate(
            (
                (owner, ints.at[0]),
                (cell, ints.at[1]),
                (pressure, panels.at[0, pl.ds(4, 4)]),
                (rs, x.at[pl.ds(0, depth)]),
                (kh, x.at[depth]),
                (kv, x.at[depth + 1]),
            )
        )
    ]
    for copy in copies:
        copy.start()
    for copy in copies:
        copy.wait()
    panels[0, 0:4, :] = (ints[0] * (rows * cols) + ints[1]).astype(jnp.float32)

    def first(out):
        for l in range(count):
            out[l] = x[l, 0:8, :]
            out[count + l % half, 4 * (l // half) : 4 * (l // half) + 4, :] = x[l, 8:HX, :]

    def last(out):
        for l in range(count):
            out[l] = x[l, rows - 8 : rows, :]
            out[count + l % half, 4 * (l // half) : 4 * (l // half) + 4, :] = x[l, rows - HX : rows - 8, :]

    @pl.when(even)
    def _():
        last(a_out)
        first(b_out)

    @pl.when(jnp.logical_not(even))
    def _():
        first(a_out)
        last(b_out)


def own_columns_kernel(x, ext, sub_out, strip_out):
    count, rows, cols = x.shape
    for l in range(count):
        ext[l, HX : HX + rows, :] = x[l]
    _, _, y_even = y_sides()
    for g in range(count // SLABS):
        layers = range(SLABS * g, SLABS * g + SLABS)
        to_right = slab_of([x[l, :, cols - 128 : cols] for l in layers], True)
        to_left = slab_of([x[l, :, 0:128] for l in layers], False)
        sub_out[g] = jnp.where(y_even, to_right, to_left)
        strip_out[g] = jnp.where(y_even, to_left, to_right)


def forcing_kernel(ext_in, xa, xb, panels, ext, sub_out, strip_out):
    count, span, cols = ext.shape
    rows = span - 2 * HX
    depth = count - 2
    half = count // 2
    tile = lax.axis_index("tile")
    even = tile % 2 == 0
    high = rows + HX

    def upper(x):
        for l in range(count):
            ext[l, 0:4, :] = x[count + l % half, 4 * (l // half) : 4 * (l // half) + 4, :]
            ext[l, 4:HX, :] = x[l]

    def lower(x):
        for l in range(count):
            ext[l, high : high + 8, :] = x[l]
            ext[l, high + 8 : high + HX, :] = x[count + l % half, 4 * (l // half) : 4 * (l // half) + 4, :]

    @pl.when(even)
    def _():
        lower(xa)
        upper(xb)

    @pl.when(jnp.logical_not(even))
    def _():
        upper(xa)
        lower(xb)


    span = rows + 2 * HX
    left, right = [], []
    for g in range(panels.shape[0]):
        group = panels[g]
        for k in range(4):
            code = group[k : k + 1].astype(jnp.int32)
            value = group[4 + k : 5 + k]
            row = code // cols - (tile * rows - HX)
            col = code % cols
            hit = row == lax.broadcasted_iota(jnp.int32, (span, 128), 0)
            left.append(jnp.where(hit, value, 0.0))
            right.append(
                jnp.where(col == lax.broadcasted_iota(jnp.int32, (cols, 128), 0), 1.0, 0.0).astype(jnp.bfloat16)
            )
    left = jnp.concatenate(left, 1)
    right = jnp.concatenate(right, 1)
    parts = lax.dot_general(
        jnp.concatenate(split(left, 3), 0), right, (((1,), (1,)), ((), ())), preferred_element_type=jnp.float32
    )
    total = parts[0:span] + parts[span : 2 * span] + parts[2 * span :]
    ext[depth - 1] = ext[depth - 1] + total

    _, _, y_even = y_sides()
    slabs = count // SLABS

    def send(g, to_right, to_left):
        sub_out[g] = jnp.where(y_even, to_right, to_left)
        strip_out[g] = jnp.where(y_even, to_left, to_right)

    def corners(l, first):
        return jnp.concatenate(
            [ext[l, 0:HX, first : first + 128], ext[l, high : high + HX, first : first + 128]], 0
        )

    for g in range(slabs):
        layers = range(SLABS * g, SLABS * g + SLABS)
        send(g, slab_of([corners(l, cols - 128) for l in layers], True), slab_of([corners(l, 0) for l in layers], False))
    pad = jnp.zeros((2 * HX - rows // 2, 128), jnp.float32)
    halves = [total[HX : HX + rows // 2], total[HX + rows // 2 : high]]
    send(
        slabs,
        jnp.concatenate([slab_of([x[:, cols - 128 :] for x in halves], True), pad], 0),
        jnp.concatenate([slab_of([x[:, :128] for x in halves], False), pad], 0),
    )


def rolled(x, shift):
    return pltpu.roll(x, shift % 128, 1) if shift % 128 else x


def base_kernel(ext, ysub, ystrip, base):
    count, span, cols = ext.shape
    high = span - HX
    _, _, y_even = y_sides()
    lane = lax.broadcasted_iota(jnp.int32, (span, 128), 1)
    lane_own = lane[HX:high]
    for g in range(count // SLABS):
        from_right = jnp.where(y_even, ysub[g], ystrip[g])
        from_left = jnp.where(y_even, ystrip[g], ysub[g])
        for k in range(SLABS):
            l = SLABS * g + k
            x = jnp.where(lane >= 128 - EDGE, ext[l, :, cols - 128 : cols], 0.0)
            x = jnp.where((lane >= 2 * HY) & (lane < 2 * HY + EDGE), rolled(ext[l, :, 0:128], 2 * HY), x)
            base[l] = x
            outer = jnp.where(lane_own < HY, rolled(from_right, -HY * k), rolled(from_left, HY - HY * k))
            base[l, HX:high, :] = jnp.where(lane_own < 2 * HY, outer, x[HX:high])


def row_inside(shape, rows, above):
    row = lax.axis_index("tile") * rows - above + lax.broadcasted_iota(jnp.int32, shape, 0)
    return (row >= 0) & (row < lax.axis_size("tile") * rows)


def y_sides():
    y = lax.axis_index("strip") * lax.axis_size("sub") + lax.axis_index("sub")
    return y > 0, y < lax.axis_size("strip") * lax.axis_size("sub") - 1, y % 2 == 0


def wide_inside(shape, rows, above, own, halo):
    has_left, has_right, _ = y_sides()
    column = lax.broadcasted_iota(jnp.int32, shape, 1)
    right = (column >= own) & (column < own + halo) & has_right
    left = (column >= shape[1] - halo) & has_left
    return row_inside(shape, rows, above) & ((column < own) | right | left)


def edge_inside(shape, rows, above, halo, edge):
    has_left, has_right, _ = y_sides()
    column = lax.broadcasted_iota(jnp.int32, shape, 1)
    right = (column < halo) & has_right
    left = (column >= halo) & (column < 2 * halo) & has_left
    own = ((column >= 2 * halo) & (column < 2 * halo + edge)) | (column >= 128 - edge)
    return row_inside(shape, rows, above) & (own | right | left)


def zero_ends(*refs):
    for ref in refs:
        ref[0] = jnp.zeros(ref.shape[1:], jnp.float32)
        ref[ref.shape[0] - 1] = jnp.zeros(ref.shape[1:], jnp.float32)


def presmooth(source, kh, kv, scale, inside, w, al, be, u, un, depth):
    weights(kh, kv, scale, inside, w, al, be)
    zero_ends(u, un)

    def first(z, c):
        u[z + 1] = w[jnp.minimum(z, 1)] * source[z]
        return c

    loop(depth, first, u.shape[1] * u.shape[2] // 1024)
    sweep(u, un, u.at[pl.ds(1, depth)], al, be, depth)


def restrict(source, un, scale, r, depth, parts):
    kh, kv = source[depth], source[depth + 1]
    rows = kh.shape[0]
    for l in range(depth + 2):
        for j in range(r.shape[1]):
            if r.shape[2] > rows:
                r[l, j, rows:, :] = jnp.zeros((r.shape[2] - rows, 128), jnp.float32)
    blocks_out(r, depth, kh)
    blocks_out(r, depth + 1, kv)

    def rest(z, c):
        blocks_out(r, z, residual_of(un, z, source[z], source[depth], source[depth + 1], scale))
        return c

    loop(depth, rest, rows * kh.shape[1] // 1024)
    n = r.shape[2] // 2
    pairs = jnp.concatenate(
        [
            jnp.concatenate(
                [r[l, j, pl.ds(0, n, stride=2), :] + r[l, j, pl.ds(1, n, stride=2), :] for j in range(r.shape[1])], 1
            )
            for l in range(depth + 2)
        ],
        0,
    )
    return exact_dot(pairs, parts).reshape(depth + 2, n, parts.shape[1])


def inner_kernel(
    ext, c1, c2, u_out, b1_out, u1_out, c_out,
    w0, al0, be0, u0, u0n, r0, w1, al1, be1, u1, u1n, r1,
):
    depth, span, cols = ext.shape[0] - 2, ext.shape[1], ext.shape[2]
    rows = span - 2 * HX
    presmooth(
        ext, ext[depth], ext[depth + 1], 1.0, row_inside((span, cols), rows, HX), w0, al0, be0, u0, u0n, depth
    )
    for z in range(depth):
        u_out[z] = u0n[z + 1, 8 : span - 8, :]
    b1_out[...] = restrict(ext, u0n, 1.0, r0, depth, c1[...])
    span1, half = b1_out.shape[1], b1_out.shape[2]
    presmooth(
        b1_out, b1_out[depth], b1_out[depth + 1], 0.25, row_inside((span1, half), rows // 2, HX // 2),
        w1, al1, be1, u1, u1n, depth,
    )
    u1_out[...] = u1n[pl.ds(1, depth)]
    c_out[...] = restrict(b1_out, u1n, 0.25, r1, depth, c2[...])


def edge_kernel(
    base, ysub, ystrip, c_inner, c1, c2,
    b_out, u_out, b1_out, u1_out, c_out, a_msg, b_msg,
    w0, al0, be0, u0, u0n, r0, w1, al1, be1, u1, u1n, r1,
):
    count, span = base.shape[:2]
    depth = count - 2
    rows = span - 2 * HX
    high = span - HX
    even = lax.axis_index("tile") % 2 == 0
    _, _, y_even = y_sides()
    slabs = count // SLABS
    lane = lax.broadcasted_iota(jnp.int32, (2 * HX, 128), 1)
    for g in range(slabs):
        from_right = jnp.where(y_even, ysub[g], ystrip[g])
        from_left = jnp.where(y_even, ystrip[g], ysub[g])
        for k in range(SLABS):
            l = SLABS * g + k
            outer = jnp.where(lane < HY, rolled(from_right, -HY * k), rolled(from_left, HY - HY * k))
            b_out[l, 0:HX, :] = jnp.where(lane[:HX] < 2 * HY, outer[:HX], base[l, 0:HX, :])
            b_out[l, high:span, :] = jnp.where(lane[HX:] < 2 * HY, outer[HX:], base[l, high:span, :])
    half = rows // 2
    lane = lane[:half]
    from_right = jnp.where(y_even, ysub[slabs, :half], ystrip[slabs, :half])
    from_left = jnp.where(y_even, ystrip[slabs, :half], ysub[slabs, :half])
    for k in (0, 1):
        force = jnp.where(lane < HY, rolled(from_right, -HY * k), rolled(from_left, HY - HY * k))
        part = pl.ds(HX + half * k, half)
        b_out[depth - 1, part, :] = base[depth - 1, part, :] + jnp.where(lane < 2 * HY, force, 0.0)
    presmooth(
        b_out, b_out[depth], b_out[depth + 1], 1.0, edge_inside((span, 128), rows, HX, HY, EDGE),
        w0, al0, be0, u0, u0n, depth,
    )
    for z in range(depth):
        u_out[z] = u0n[z + 1, 8 : span - 8, :]
    b1_out[...] = restrict(b_out, u0n, 1.0, r0, depth, c1[...])
    span1 = b1_out.shape[1]
    presmooth(
        b1_out, b1_out[depth], b1_out[depth + 1], 0.25,
        edge_inside((span1, 128), rows // 2, HX // 2, HY // 2, EDGE // 2),
        w1, al1, be1, u1, u1n, depth,
    )
    u1_out[...] = u1n[pl.ds(1, depth)]
    c_out[...] = c_inner[...] + restrict(b1_out, u1n, 0.25, r1, depth, c2[...])
    own2 = HX // 4

    def send(out, start):
        for l in range(count):
            out[count + l // 8, l % 8 : l % 8 + 1, :] = c_out[l, start : start + 1, :]
            out[l] = c_out[l, start + 1 : start + HX2, :]

    @pl.when(even)
    def _():
        send(a_msg, own2 - 1)
        send(b_msg, own2)

    @pl.when(jnp.logical_not(even))
    def _():
        send(a_msg, own2)
        send(b_msg, own2 - 1)


def join_kernel(
    ext, edge, u_in, u_edge, b1_in, b1_edge, u1_in, u1_edge,
    k0, u0, wb0, al0, be0, u1, wb1, al1, be1, w0, w1,
):
    depth, small, cols = u_in.shape
    span = ext.shape[1]
    rows = span - 2 * HX

    def joined(inner, strip, halo, edge, patch):
        own = inner.shape[1]
        lane = lax.broadcasted_iota(jnp.int32, strip.shape, 1)
        turned = pltpu.roll(strip, 128 - 2 * halo, 1)
        outer = jnp.where(lane < halo, strip, jnp.where(lane >= 128 - halo, turned, 0.0))
        blocks = [inner[:, 128 * j : 128 * (j + 1)] for j in range(own // 128)]
        blocks[0] = jnp.where(lane < patch, turned, blocks[0])
        blocks[-1] = jnp.where(lane >= 128 - patch, strip, blocks[-1])
        return jnp.concatenate(blocks + [outer], 1)

    part0 = lambda inner, strip: joined(inner, strip, HY, EDGE, EDGE // 2)
    part1 = lambda inner, strip: joined(inner, strip, HY // 2, EDGE // 2, EDGE // 4)
    low, top = 8, span - 8
    lanes = cols + 128
    for i in (0, 1):
        k0[i] = part0(ext[depth + i, low:top, :], edge[depth + i, low:top, :])
    weights(
        k0[0], k0[1], 1.0, wide_inside((small, lanes), rows, HX - low, cols, HY), w0, al0, be0,
    )
    span1, half = b1_in.shape[1], b1_in.shape[2]
    kh1, kv1 = (part1(b1_in[depth + i], b1_edge[depth + i]) for i in (0, 1))
    weights(
        kh1, kv1, 0.25, wide_inside((span1, 2 * half), rows // 2, HX // 2, half, HY // 2), w1, al1, be1,
    )
    for z in range(depth):
        i = min(z, 1)
        u0[z] = part0(u_in[z], u_edge[z])
        wb0[z] = w0[i] * part0(ext[z, low:top, :], edge[z, low:top, :])
        u1[z] = part1(u1_in[z], u1_edge[z])
        wb1[z] = w1[i] * part1(b1_in[z], b1_edge[z])


def up_kernel(
    c_in, xa, xb, ext, k0, u0, wb0, al0, be0, u1, wb1, al1, be1, p1, p2,
    potential, residual,
    b2, w2, al2, be2, wb2, u2, u2n, f1, f1n, f0, f0n, e1, e0, pot, res, sems,
):
    count = c_in.shape[0]
    depth = count - 2
    rows, cols = potential.shape[1:]
    rows2 = rows // 4
    even = lax.axis_index("tile") % 2 == 0
    own2 = HX // 4
    span2 = b2.shape[1]
    end2 = rows2 + 2 * HX2

    def put(x, start):
        for l in range(count):
            b2[l, start : start + 1, :] = x[count + l // 8, l % 8 : l % 8 + 1, :]
            b2[l, start + 1 : start + HX2, :] = x[l]

    @pl.when(even)
    def _():
        put(xa, HX2 + rows2)
        put(xb, 0)

    @pl.when(jnp.logical_not(even))
    def _():
        put(xa, 0)
        put(xb, HX2 + rows2)

    lanes2 = b2.shape[2]
    for l in range(count):
        b2[l, HX2 : HX2 + rows2, :] = c_in[l, own2 : own2 + rows2, :]
        b2[l, end2:span2, :] = jnp.zeros((span2 - end2, lanes2), jnp.float32)
    row = lax.broadcasted_iota(jnp.int32, (span2, lanes2), 0)
    inside2 = wide_inside((span2, lanes2), rows2, HX2, cols // 4, HY // 4)
    weights(b2[depth], b2[depth + 1], 0.0625, inside2 & (row < end2), w2, al2, be2)
    zero_ends(u2, u2n, f1, f1n, f0, f0n)

    def first2(z, c):
        v = w2[jnp.minimum(z, 1)] * b2[z]
        wb2[z] = v
        u2[z + 1] = v
        return c

    loop(depth, first2, 4)
    src, dst = u2, u2n
    for _ in range(COARSE - 1):
        sweep(src, dst, wb2, al2, be2, depth)
        src, dst = dst, src

    span1, lanes1 = u1.shape[1], u1.shape[2]
    off2 = HX2 - own2
    coarse = jnp.concatenate([src[z + 1][off2 : off2 + span1 // 2] for z in range(depth)], 0)
    fine = exact_dot(coarse, p2[...])
    for z in range(depth):
        rows_doubled(e1, z, fine[z * (span1 // 2) : (z + 1) * (span1 // 2)])

    def first1(z, c):
        f1[z + 1] = u1[z] + blocks_in(e1, z)
        return c

    loop(depth, first1, 8)
    sweep(f1, f1n, wb1, al1, be1, depth)
    sweep(f1n, f1, wb1, al1, be1, depth)

    span0, lanes0 = u0.shape[1], u0.shape[2]
    above = (span0 - rows) // 2
    off1 = (HX - above) // 2
    end1 = off1 + span0 // 2
    fine = exact_dot(jnp.concatenate([f1[z + 1, 0:end1, :] for z in range(depth)], 0), p1[...])
    for z in range(depth):
        rows_doubled(e0, z, fine[z * end1 + off1 : (z + 1) * end1])

    def first0(z, c):
        f0[z + 1] = u0[z] + blocks_in(e0, z)[:span0]
        return c

    loop(depth, first0, 15)
    sweep(f0, f0n, wb0, al0, be0, depth)
    sweep(f0n, f0, wb0, al0, be0, depth)

    copies = []

    def ship(src, dst, first, n):
        copy = pltpu.make_async_copy(src.at[pl.ds(first, n)], dst.at[pl.ds(first, n)], sems.at[len(copies)])
        copy.start()
        copies.append(copy)

    for z in range(depth):
        pot[z] = f0[z + 1, above : above + rows, 0:cols]
    ship(pot, potential, 0, depth)
    chunk = depth // 4
    for z in range(depth):
        b = ext[z, HX - above : HX - above + span0, :]
        r = residual_of(f0, z, b, k0[0, :, 0:cols], k0[1, :, 0:cols], 1.0, cols)
        res[z] = r[above : above + rows]
        if z % chunk == chunk - 1:
            ship(res, residual, z + 1 - chunk, chunk)
    for copy in copies:
        copy.wait()


VM = pl.BlockSpec(memory_space=pltpu.VMEM)


def call(kernel, outs, scratch, *args, aliases={}):
    f32 = lambda shape: jax.ShapeDtypeStruct(shape, jnp.float32)
    return pl.pallas_call(
        kernel,
        out_shape=[f32(s) for s in outs],
        in_specs=[VM] * len(args),
        out_specs=[VM] * len(outs),
        scratch_shapes=[pltpu.VMEM(s, jnp.float32) for s in scratch],
        input_output_aliases=aliases,
        compiler_params=pltpu.CompilerParams(vmem_limit_bytes=24 << 20),
    )(*args)


def body(right_side, horiz_coef, vert_coef, panel_owner, panel_cell, panel_pressure):
    depth, rows, cols = right_side.shape
    tiles = lax.axis_size("tile")
    y_axes = ("strip", "sub")
    y_count = lax.axis_size("strip") * lax.axis_size("sub")
    count = depth + 2
    span = rows + 2 * HX
    wide1, wide2, inner2, edge1, edge2 = lane_maps(cols)
    mean = lambda lanes, width: jnp.asarray(0.25 * selection(lanes, width), jnp.bfloat16)
    spread = lambda lanes, width: jnp.asarray(selection(lanes, width).T, jnp.bfloat16)
    c1_inner, c2_inner = mean(wide1[:cols], cols // 2), mean(inner2, cols // 2)
    c1_edge, c2_edge = mean(edge1, 128), mean(edge2, cols // 2)
    p1, p2 = spread(wide1, cols), spread(wide2, cols // 2)

    message = (count + count // 2, 8, cols)
    f32 = lambda shape: jax.ShapeDtypeStruct(shape, jnp.float32)
    early = (count // SLABS, rows, 128)
    x_own, panels, a, b = pl.pallas_call(
        load_kernel,
        out_shape=[f32((count, rows, cols)), f32((1, 8, 128)), f32(message), f32(message)],
        in_specs=[pl.BlockSpec(memory_space=pltpu.HBM)] * 6,
        out_specs=[VM] * 4,
        scratch_shapes=[pltpu.VMEM((2, 4, 128), jnp.int32), pltpu.SemaphoreType.DMA((6,))],
        compiler_params=pltpu.CompilerParams(vmem_limit_bytes=8 << 20),
    )(
        *[
            pltpu.with_memory_space_constraint(x, pltpu.HBM)
            for x in (
                right_side, horiz_coef, vert_coef,
                panel_owner.reshape(4, -1), panel_cell.reshape(4, -1), panel_pressure.reshape(4, -1),
            )
        ]
    )
    near = lax.ppermute(panels, "tile", [(i, i ^ 1) for i in range(tiles)])
    a = neighbour_swap(a, "tile", 0, "sub")
    b = neighbour_swap(b, "tile", 1, "sub")
    ext, sub_own, strip_own = call(own_columns_kernel, [(count, span, cols), early, early], [], x_own)
    sub_own = neighbour_swap(sub_own, y_axes, 0, "group")
    strip_own = neighbour_swap(strip_own, y_axes, 1, "group")
    panels = jnp.concatenate([panels, near], 0)
    step = 2
    while step < tiles:
        swap = [(i, i ^ step) for i in range(tiles)]
        panels = jnp.concatenate([panels, lax.ppermute(panels, "tile", swap)], 0)
        step *= 2

    slabs = (count // SLABS + 1, 2 * HX, 128)
    ext, sub, strip = call(
        forcing_kernel, [(count, span, cols), slabs, slabs], [],
        ext, a, b, panels,
        aliases={0: 0},
    )
    sub = neighbour_swap(sub, y_axes, 0, "group")
    strip = neighbour_swap(strip, y_axes, 1, "group")

    lanes, half = cols + 128, cols // 2
    small = span - 16
    span1 = (span + 8) // 2
    span2 = span1 // 2

    def down_scratch(width, width1):
        return (
            [(2, span, width)] * 3 + [(depth + 2, span, width)] * 2 + [(count, width // 128, span + 8, 128)]
            + [(2, span1, width1)] * 3 + [(depth + 2, span1, width1)] * 2 + [(count, width1 // 128, span1, 128)]
        )

    u_in, b1_in, u1_in, c_in = call(
        inner_kernel,
        [(depth, small, cols), (count, span1, half), (depth, span1, half), (count, span2, half)],
        down_scratch(cols, half),
        ext, c1_inner, c2_inner,
    )
    (base,) = call(base_kernel, [(count, span, 128)], [], ext, sub_own, strip_own)
    message2 = (count + (count + 7) // 8, 8, half)
    edge, u_edge, b1_edge, u1_edge, c_own, a2, b2 = call(
        edge_kernel,
        [
            (count, span, 128), (depth, small, 128), (count, span1, 128), (depth, span1, 128),
            (count, span2, half), message2, message2,
        ],
        down_scratch(128, 128),
        base, sub, strip, c_in, c1_edge, c2_edge,
        aliases={0: 0},
    )
    a2 = neighbour_swap(a2, "tile", 0, "sub")
    b2 = neighbour_swap(b2, "tile", 1, "sub")

    pair0, field = (2, small, lanes), (depth, small, lanes)
    pair1, field1 = (2, span1, cols), (depth, span1, cols)
    state = call(
        join_kernel,
        [pair0, field, field, pair0, pair0, field1, field1, pair1, pair1],
        [pair0, pair1],
        ext, edge, u_in, u_edge, b1_in, b1_edge, u1_in, u1_edge,
    )

    wide2 = 32
    field2 = (depth + 2, wide2, half)
    own = right_side.shape
    potential, residual = pl.pallas_call(
        up_kernel,
        out_shape=[f32(own), f32(own)],
        in_specs=[VM] * (6 + len(state)),
        out_specs=[pl.BlockSpec(memory_space=pltpu.HBM)] * 2,
        scratch_shapes=[
            pltpu.VMEM(shape, jnp.float32)
            for shape in (
                (count, wide2, half), (2, wide2, half), (2, wide2, half), (2, wide2, half), (depth, wide2, half),
                field2, field2, (depth + 2, span1, cols), (depth + 2, span1, cols),
                (depth + 2, small, lanes), (depth + 2, small, lanes),
                (depth, cols // 128, span1, 128), (depth, lanes // 128, small + 8, 128), own, own,
            )
        ]
        + [pltpu.SemaphoreType.DMA((5,))],
        compiler_params=pltpu.CompilerParams(vmem_limit_bytes=24 << 20),
    )(c_own, a2, b2, ext, *state, p1, p2)
    return potential, residual


def solution(mesh):
    return jax.shard_map(
        body,
        mesh=mesh,
        in_specs=(
            jax.P("group", "tile", ("strip", "sub")),
            jax.P(("group", "tile"), ("strip", "sub")),
            jax.P(("group", "tile"), ("strip", "sub")),
            jax.P(("group", "tile", "strip", "sub"), None),
            jax.P(("group", "tile", "strip", "sub")),
            jax.P(("group", "tile", "strip", "sub")),
        ),
        out_specs=(
            jax.P("group", "tile", ("strip", "sub")),
            jax.P("group", "tile", ("strip", "sub")),
        ),
        check_vma=False,
    )
```

```python
import jax
import jax.numpy as jnp
import numpy as np
from jax import lax
from jax.experimental import pallas as pl
from jax.experimental.pallas import tpu as pltpu

COARSE = 8
OMEGA = 0.8

HX = 12
HX2 = 9
HY = 42
LIMIT = 512
SLABS = 3
EDGE = 16


def neighbour_swap(x, axis, odd, spare):
    axis = axis if isinstance(axis, tuple) else (axis,)
    count = lax.axis_size(axis)
    twins = lax.axis_size(spare)
    leading = spare == "group"
    place = lambda i, twin: twin * count + i if leading else i * twins + twin
    pairs = []
    for twin in range(twins):
        for i in range(count):
            j, other = (i + 1 if i % 2 == odd else i - 1), twin
            if not 0 <= j < count:
                j, other = i, twin ^ 1
            pairs.append((place(i, twin), place(j, other)))
    return lax.ppermute(x, (spare,) + axis if leading else axis + (spare,), pairs)


def lane_maps(cols):
    half, quarter, h1, h2 = cols // 2, cols // 4, HY // 2, HY // 4
    wide1 = -np.ones(cols + 128, np.int64)
    wide1[:cols] = np.arange(cols) // 2
    wide1[cols : cols + HY] = half + np.arange(HY) // 2
    wide1[cols + 128 - HY :] = 2 * half - h1 + np.arange(HY) // 2
    wide2 = -np.ones(2 * half, np.int64)
    wide2[:half] = np.arange(half) // 2
    wide2[half : half + 2 * h2] = quarter + np.arange(2 * h2) // 2
    wide2[2 * half - 2 * h2 :] = 2 * quarter - h2 + np.arange(2 * h2) // 2
    inner2 = -np.ones(half, np.int64)
    inner2[4 : half - 4] = np.arange(4, half - 4) // 2
    edge1 = -np.ones(128, np.int64)
    edge1[: 2 * HY + EDGE] = np.arange(2 * HY + EDGE) // 2
    edge1[128 - EDGE :] = 128 - EDGE // 2 + np.arange(EDGE) // 2
    edge2 = -np.ones(128, np.int64)
    edge2[: 2 * h2] = quarter + np.arange(2 * h2) // 2
    edge2[2 * h1 - 2 * h2 : 2 * h1] = 2 * quarter - h2 + np.arange(2 * h2) // 2
    edge2[2 * h1 : 2 * h1 + 4] = np.arange(4) // 2
    edge2[124:] = quarter - 2 + np.arange(4) // 2
    return wide1, wide2, inner2, edge1, edge2


def selection(lanes, width):
    return (lanes[:, None] == np.arange(width)[None, :]).astype(np.float32)


def split(x, parts):
    out = []
    for _ in range(parts):
        out.append(x.astype(jnp.bfloat16))
        x = x - out[-1].astype(jnp.float32)
    return out


def exact_dot(left, right):
    return jnp.dot(jnp.concatenate(split(left, 2), 1), jnp.concatenate([right, right], 0), preferred_element_type=jnp.float32)


def neighbours(u):
    rows, lanes = u.shape
    return (
        pltpu.roll(u, 1, 0)
        + pltpu.roll(u, rows - 1, 0)
        + pltpu.roll(u, 1, 1)
        + pltpu.roll(u, lanes - 1, 1)
    )


def weights(kh, kv, scale, inside, w_ref, a_ref, b_ref):
    for i, layers in enumerate((1.0, 2.0)):
        diag = 4.0 * scale * kh + layers * kv
        w = jnp.where(inside, OMEGA / jnp.where(inside, diag, 1.0), 0.0)
        if w_ref is not None:
            w_ref[i] = w
        a_ref[i] = w * (scale * kh)
        b_ref[i] = w * kv


def loop(depth, fn, vregs):
    lax.fori_loop(0, depth, fn, 0, unroll=max(1, min(depth, LIMIT // vregs)))


def sweep(src, dst, wb, a_ref, b_ref, depth):
    def layer(z, c):
        i = jnp.minimum(z, 1)
        u = src[z + 1]
        dst[z + 1] = (
            (1.0 - OMEGA) * u
            + wb[z]
            + a_ref[i] * neighbours(u)
            + b_ref[i] * (src[z] + src[z + 2])
        )
        return c

    loop(depth, layer, src.shape[1] * src.shape[2] // 1024)


def residual_of(src, z, b, kh, kv, scale, lanes=None):
    layers = jnp.where(z == 0, 1.0, 2.0)
    u = src[z + 1]
    around = neighbours(u)[:, :lanes]
    u = u[:, :lanes]
    return b + (scale * kh) * (around - 4.0 * u) + kv * (src[z, :, :lanes] + src[z + 2, :, :lanes] - layers * u)


def blocks_out(ref, l, x):
    for j in range(ref.shape[1]):
        ref[l, j, 0 : x.shape[0], :] = x[:, 128 * j : 128 * (j + 1)]


def blocks_in(ref, l):
    return jnp.concatenate([ref[l, j] for j in range(ref.shape[1])], 1)


def rows_doubled(ref, l, part):
    n = part.shape[0]
    for j in range(ref.shape[1]):
        for s in (0, 1):
            ref[l, j, pl.ds(s, n, stride=2), :] = part[:, 128 * j : 128 * (j + 1)]


def slab_of(layers, at_right):
    shape = layers[0].shape
    lane = lax.broadcasted_iota(jnp.int32, shape, 1)
    out = jnp.zeros(shape, jnp.float32)
    for k, x in enumerate(layers):
        shift = (HY * (k + 1) if at_right else HY * k) % 128
        x = pltpu.roll(x, shift, 1) if shift else x
        out = jnp.where((lane >= HY * k) & (lane < HY * (k + 1)), x, out)
    return out


def load_kernel(rs, kh, kv, owner, cell, pressure, x, panels, a_out, b_out, ints, sems):
    depth, rows, cols = rs.shape
    count = depth + 2
    half = count // 2
    even = lax.axis_index("tile") % 2 == 0
    copies = [
        pltpu.make_async_copy(src, dst, sems.at[i])
        for i, (src, dst) in enumerate(
            (
                (owner, ints.at[0]),
                (cell, ints.at[1]),
                (pressure, panels.at[0, pl.ds(4, 4)]),
                (rs, x.at[pl.ds(0, depth)]),
                (kh, x.at[depth]),
                (kv, x.at[depth + 1]),
            )
        )
    ]
    for copy in copies:
        copy.start()
    for copy in copies:
        copy.wait()
    panels[0, 0:4, :] = (ints[0] * (rows * cols) + ints[1]).astype(jnp.float32)

    def first(out):
        for l in range(count):
            out[l] = x[l, 0:8, :]
            out[count + l % half, 4 * (l // half) : 4 * (l // half) + 4, :] = x[l, 8:HX, :]

    def last(out):
        for l in range(count):
            out[l] = x[l, rows - 8 : rows, :]
            out[count + l % half, 4 * (l // half) : 4 * (l // half) + 4, :] = x[l, rows - HX : rows - 8, :]

    @pl.when(even)
    def _():
        last(a_out)
        first(b_out)

    @pl.when(jnp.logical_not(even))
    def _():
        first(a_out)
        last(b_out)


def own_columns_kernel(x, ext, sub_out, strip_out):
    count, rows, cols = x.shape
    for l in range(count):
        ext[l, HX : HX + rows, :] = x[l]
    _, _, y_even = y_sides()
    for g in range(count // SLABS):
        layers = range(SLABS * g, SLABS * g + SLABS)
        to_right = slab_of([x[l, :, cols - 128 : cols] for l in layers], True)
        to_left = slab_of([x[l, :, 0:128] for l in layers], False)
        sub_out[g] = jnp.where(y_even, to_right, to_left)
        strip_out[g] = jnp.where(y_even, to_left, to_right)


def forcing_kernel(ext_in, xa, xb, panels, ext, sub_out, strip_out):
    count, span, cols = ext.shape
    rows = span - 2 * HX
    depth = count - 2
    half = count // 2
    tile = lax.axis_index("tile")
    even = tile % 2 == 0
    high = rows + HX

    def upper(x):
        for l in range(count):
            ext[l, 0:4, :] = x[count + l % half, 4 * (l // half) : 4 * (l // half) + 4, :]
            ext[l, 4:HX, :] = x[l]

    def lower(x):
        for l in range(count):
            ext[l, high : high + 8, :] = x[l]
            ext[l, high + 8 : high + HX, :] = x[count + l % half, 4 * (l // half) : 4 * (l // half) + 4, :]

    @pl.when(even)
    def _():
        lower(xa)
        upper(xb)

    @pl.when(jnp.logical_not(even))
    def _():
        upper(xa)
        lower(xb)


    span = rows + 2 * HX
    left, right = [], []
    for g in range(panels.shape[0]):
        group = panels[g]
        for k in range(4):
            code = group[k : k + 1].astype(jnp.int32)
            value = group[4 + k : 5 + k]
            row = code // cols - (tile * rows - HX)
            col = code % cols
            hit = row == lax.broadcasted_iota(jnp.int32, (span, 128), 0)
            left.append(jnp.where(hit, value, 0.0))
            right.append(
                jnp.where(col == lax.broadcasted_iota(jnp.int32, (cols, 128), 0), 1.0, 0.0).astype(jnp.bfloat16)
            )
    left = jnp.concatenate(left, 1)
    right = jnp.concatenate(right, 1)
    parts = lax.dot_general(
        jnp.concatenate(split(left, 3), 0), right, (((1,), (1,)), ((), ())), preferred_element_type=jnp.float32
    )
    total = parts[0:span] + parts[span : 2 * span] + parts[2 * span :]
    ext[depth - 1] = ext[depth - 1] + total

    _, _, y_even = y_sides()
    slabs = count // SLABS

    def send(g, to_right, to_left):
        sub_out[g] = jnp.where(y_even, to_right, to_left)
        strip_out[g] = jnp.where(y_even, to_left, to_right)

    def corners(l, first):
        return jnp.concatenate(
            [ext[l, 0:HX, first : first + 128], ext[l, high : high + HX, first : first + 128]], 0
        )

    for g in range(slabs):
        layers = range(SLABS * g, SLABS * g + SLABS)
        send(g, slab_of([corners(l, cols - 128) for l in layers], True), slab_of([corners(l, 0) for l in layers], False))
    pad = jnp.zeros((2 * HX - rows // 2, 128), jnp.float32)
    halves = [total[HX : HX + rows // 2], total[HX + rows // 2 : high]]
    send(
        slabs,
        jnp.concatenate([slab_of([x[:, cols - 128 :] for x in halves], True), pad], 0),
        jnp.concatenate([slab_of([x[:, :128] for x in halves], False), pad], 0),
    )


def rolled(x, shift):
    return pltpu.roll(x, shift % 128, 1) if shift % 128 else x


def base_kernel(ext, ysub, ystrip, base):
    count, span, cols = ext.shape
    high = span - HX
    _, _, y_even = y_sides()
    lane = lax.broadcasted_iota(jnp.int32, (span, 128), 1)
    lane_own = lane[HX:high]
    for g in range(count // SLABS):
        from_right = jnp.where(y_even, ysub[g], ystrip[g])
        from_left = jnp.where(y_even, ystrip[g], ysub[g])
        for k in range(SLABS):
            l = SLABS * g + k
            x = jnp.where(lane >= 128 - EDGE, ext[l, :, cols - 128 : cols], 0.0)
            x = jnp.where((lane >= 2 * HY) & (lane < 2 * HY + EDGE), rolled(ext[l, :, 0:128], 2 * HY), x)
            base[l] = x
            outer = jnp.where(lane_own < HY, rolled(from_right, -HY * k), rolled(from_left, HY - HY * k))
            base[l, HX:high, :] = jnp.where(lane_own < 2 * HY, outer, x[HX:high])


def row_inside(shape, rows, above):
    row = lax.axis_index("tile") * rows - above + lax.broadcasted_iota(jnp.int32, shape, 0)
    return (row >= 0) & (row < lax.axis_size("tile") * rows)


def y_sides():
    y = lax.axis_index("strip") * lax.axis_size("sub") + lax.axis_index("sub")
    return y > 0, y < lax.axis_size("strip") * lax.axis_size("sub") - 1, y % 2 == 0


def wide_inside(shape, rows, above, own, halo):
    has_left, has_right, _ = y_sides()
    column = lax.broadcasted_iota(jnp.int32, shape, 1)
    right = (column >= own) & (column < own + halo) & has_right
    left = (column >= shape[1] - halo) & has_left
    return row_inside(shape, rows, above) & ((column < own) | right | left)


def edge_inside(shape, rows, above, halo, edge):
    has_left, has_right, _ = y_sides()
    column = lax.broadcasted_iota(jnp.int32, shape, 1)
    right = (column < halo) & has_right
    left = (column >= halo) & (column < 2 * halo) & has_left
    own = ((column >= 2 * halo) & (column < 2 * halo + edge)) | (column >= 128 - edge)
    return row_inside(shape, rows, above) & (own | right | left)


def zero_ends(*refs):
    for ref in refs:
        ref[0] = jnp.zeros(ref.shape[1:], jnp.float32)
        ref[ref.shape[0] - 1] = jnp.zeros(ref.shape[1:], jnp.float32)


def presmooth(source, kh, kv, scale, inside, w, al, be, u, un, depth):
    weights(kh, kv, scale, inside, w, al, be)
    zero_ends(u, un)

    def first(z, c):
        u[z + 1] = w[jnp.minimum(z, 1)] * source[z]
        return c

    loop(depth, first, u.shape[1] * u.shape[2] // 1024)
    sweep(u, un, u.at[pl.ds(1, depth)], al, be, depth)


def restrict(source, un, scale, r, depth, parts):
    kh, kv = source[depth], source[depth + 1]
    rows = kh.shape[0]
    for l in range(depth + 2):
        for j in range(r.shape[1]):
            if r.shape[2] > rows:
                r[l, j, rows:, :] = jnp.zeros((r.shape[2] - rows, 128), jnp.float32)
    blocks_out(r, depth, kh)
    blocks_out(r, depth + 1, kv)

    def rest(z, c):
        blocks_out(r, z, residual_of(un, z, source[z], source[depth], source[depth + 1], scale))
        return c

    loop(depth, rest, rows * kh.shape[1] // 1024)
    n = r.shape[2] // 2
    pairs = jnp.concatenate(
        [
            jnp.concatenate(
                [r[l, j, pl.ds(0, n, stride=2), :] + r[l, j, pl.ds(1, n, stride=2), :] for j in range(r.shape[1])], 1
            )
            for l in range(depth + 2)
        ],
        0,
    )
    return exact_dot(pairs, parts).reshape(depth + 2, n, parts.shape[1])


def inner_kernel(
    ext, c1, c2, u_out, b1_out, u1_out, c_out,
    w0, al0, be0, u0, u0n, r0, w1, al1, be1, u1, u1n, r1,
):
    depth, span, cols = ext.shape[0] - 2, ext.shape[1], ext.shape[2]
    rows = span - 2 * HX
    presmooth(
        ext, ext[depth], ext[depth + 1], 1.0, row_inside((span, cols), rows, HX), w0, al0, be0, u0, u0n, depth
    )
    for z in range(depth):
        u_out[z] = u0n[z + 1, 8 : span - 8, :]
    b1_out[...] = restrict(ext, u0n, 1.0, r0, depth, c1[...])
    span1, half = b1_out.shape[1], b1_out.shape[2]
    presmooth(
        b1_out, b1_out[depth], b1_out[depth + 1], 0.25, row_inside((span1, half), rows // 2, HX // 2),
        w1, al1, be1, u1, u1n, depth,
    )
    u1_out[...] = u1n[pl.ds(1, depth)]
    c_out[...] = restrict(b1_out, u1n, 0.25, r1, depth, c2[...])


def edge_kernel(
    base, ysub, ystrip, c_inner, c1, c2,
    b_out, u0n, b1_out, u1n, c_out, a_msg, b_msg,
    w0, al0, be0, u0, r0, w1, al1, be1, u1, r1,
):
    count, span = base.shape[:2]
    depth = count - 2
    rows = span - 2 * HX
    high = span - HX
    even = lax.axis_index("tile") % 2 == 0
    _, _, y_even = y_sides()
    slabs = count // SLABS
    lane = lax.broadcasted_iota(jnp.int32, (2 * HX, 128), 1)
    for g in range(slabs):
        from_right = jnp.where(y_even, ysub[g], ystrip[g])
        from_left = jnp.where(y_even, ystrip[g], ysub[g])
        for k in range(SLABS):
            l = SLABS * g + k
            outer = jnp.where(lane < HY, rolled(from_right, -HY * k), rolled(from_left, HY - HY * k))
            b_out[l, 0:HX, :] = jnp.where(lane[:HX] < 2 * HY, outer[:HX], base[l, 0:HX, :])
            b_out[l, high:span, :] = jnp.where(lane[HX:] < 2 * HY, outer[HX:], base[l, high:span, :])
    half = rows // 2
    lane = lane[:half]
    from_right = jnp.where(y_even, ysub[slabs, :half], ystrip[slabs, :half])
    from_left = jnp.where(y_even, ystrip[slabs, :half], ysub[slabs, :half])
    for k in (0, 1):
        force = jnp.where(lane < HY, rolled(from_right, -HY * k), rolled(from_left, HY - HY * k))
        part = pl.ds(HX + half * k, half)
        b_out[depth - 1, part, :] = base[depth - 1, part, :] + jnp.where(lane < 2 * HY, force, 0.0)
    presmooth(
        b_out, b_out[depth], b_out[depth + 1], 1.0, edge_inside((span, 128), rows, HX, HY, EDGE),
        w0, al0, be0, u0, u0n, depth,
    )
    b1_out[...] = restrict(b_out, u0n, 1.0, r0, depth, c1[...])
    span1 = b1_out.shape[1]
    presmooth(
        b1_out, b1_out[depth], b1_out[depth + 1], 0.25,
        edge_inside((span1, 128), rows // 2, HX // 2, HY // 2, EDGE // 2),
        w1, al1, be1, u1, u1n, depth,
    )
    c_out[...] = c_inner[...] + restrict(b1_out, u1n, 0.25, r1, depth, c2[...])
    own2 = HX // 4

    def send(out, start):
        for l in range(count):
            out[count + l // 8, l % 8 : l % 8 + 1, :] = c_out[l, start : start + 1, :]
            out[l] = c_out[l, start + 1 : start + HX2, :]

    @pl.when(even)
    def _():
        send(a_msg, own2 - 1)
        send(b_msg, own2)

    @pl.when(jnp.logical_not(even))
    def _():
        send(a_msg, own2)
        send(b_msg, own2 - 1)


def join_kernel(
    ext, edge, u_in, u_edge, b1_in, b1_edge, u1_in, u1_edge,
    k0, u0, wb0, al0, be0, u1, wb1, al1, be1, w0, w1,
):
    depth, small, cols = u_in.shape
    span = ext.shape[1]
    rows = span - 2 * HX

    def joined(inner, strip, halo, edge, patch):
        own = inner.shape[1]
        lane = lax.broadcasted_iota(jnp.int32, strip.shape, 1)
        turned = pltpu.roll(strip, 128 - 2 * halo, 1)
        outer = jnp.where(lane < halo, strip, jnp.where(lane >= 128 - halo, turned, 0.0))
        blocks = [inner[:, 128 * j : 128 * (j + 1)] for j in range(own // 128)]
        blocks[0] = jnp.where(lane < patch, turned, blocks[0])
        blocks[-1] = jnp.where(lane >= 128 - patch, strip, blocks[-1])
        return jnp.concatenate(blocks + [outer], 1)

    part0 = lambda inner, strip: joined(inner, strip, HY, EDGE, EDGE // 2)
    part1 = lambda inner, strip: joined(inner, strip, HY // 2, EDGE // 2, EDGE // 4)
    low, top = 8, span - 8
    lanes = cols + 128
    for i in (0, 1):
        k0[i] = part0(ext[depth + i, low:top, :], edge[depth + i, low:top, :])
    weights(
        k0[0], k0[1], 1.0, wide_inside((small, lanes), rows, HX - low, cols, HY), w0, al0, be0,
    )
    span1, half = b1_in.shape[1], b1_in.shape[2]
    kh1, kv1 = (part1(b1_in[depth + i], b1_edge[depth + i]) for i in (0, 1))
    weights(
        kh1, kv1, 0.25, wide_inside((span1, 2 * half), rows // 2, HX // 2, half, HY // 2), w1, al1, be1,
    )
    for z in range(depth):
        i = min(z, 1)
        u0[z] = part0(u_in[z], u_edge[z + 1, low:top, :])
        wb0[z] = w0[i] * part0(ext[z, low:top, :], edge[z, low:top, :])
        u1[z] = part1(u1_in[z], u1_edge[z + 1])
        wb1[z] = w1[i] * part1(b1_in[z], b1_edge[z])


def up_kernel(
    c_in, xa, xb, ext, k0, u0, wb0, al0, be0, u1, wb1, al1, be1, p1, p2,
    potential, residual,
    b2, w2, al2, be2, wb2, u2, u2n, f1, f1n, f0, f0n, e1, e0, pot, res, sems,
):
    count = c_in.shape[0]
    depth = count - 2
    rows, cols = potential.shape[1:]
    rows2 = rows // 4
    even = lax.axis_index("tile") % 2 == 0
    own2 = HX // 4
    span2 = b2.shape[1]
    end2 = rows2 + 2 * HX2

    def put(x, start):
        for l in range(count):
            b2[l, start : start + 1, :] = x[count + l // 8, l % 8 : l % 8 + 1, :]
            b2[l, start + 1 : start + HX2, :] = x[l]

    @pl.when(even)
    def _():
        put(xa, HX2 + rows2)
        put(xb, 0)

    @pl.when(jnp.logical_not(even))
    def _():
        put(xa, 0)
        put(xb, HX2 + rows2)

    lanes2 = b2.shape[2]
    for l in range(count):
        b2[l, HX2 : HX2 + rows2, :] = c_in[l, own2 : own2 + rows2, :]
        b2[l, end2:span2, :] = jnp.zeros((span2 - end2, lanes2), jnp.float32)
    row = lax.broadcasted_iota(jnp.int32, (span2, lanes2), 0)
    inside2 = wide_inside((span2, lanes2), rows2, HX2, cols // 4, HY // 4)
    weights(b2[depth], b2[depth + 1], 0.0625, inside2 & (row < end2), w2, al2, be2)
    zero_ends(u2, u2n, f1, f1n, f0, f0n)

    def first2(z, c):
        v = w2[jnp.minimum(z, 1)] * b2[z]
        wb2[z] = v
        u2[z + 1] = v
        return c

    loop(depth, first2, 4)
    src, dst = u2, u2n
    for _ in range(COARSE - 1):
        sweep(src, dst, wb2, al2, be2, depth)
        src, dst = dst, src

    span1, lanes1 = u1.shape[1], u1.shape[2]
    off2 = HX2 - own2
    coarse = jnp.concatenate([src[z + 1][off2 : off2 + span1 // 2] for z in range(depth)], 0)
    fine = exact_dot(coarse, p2[...])
    for z in range(depth):
        rows_doubled(e1, z, fine[z * (span1 // 2) : (z + 1) * (span1 // 2)])

    def first1(z, c):
        f1[z + 1] = u1[z] + blocks_in(e1, z)
        return c

    loop(depth, first1, 8)
    sweep(f1, f1n, wb1, al1, be1, depth)
    sweep(f1n, f1, wb1, al1, be1, depth)

    span0, lanes0 = u0.shape[1], u0.shape[2]
    above = (span0 - rows) // 2
    off1 = (HX - above) // 2
    end1 = off1 + span0 // 2
    fine = exact_dot(jnp.concatenate([f1[z + 1, 0:end1, :] for z in range(depth)], 0), p1[...])
    for z in range(depth):
        rows_doubled(e0, z, fine[z * end1 + off1 : (z + 1) * end1])

    def first0(z, c):
        f0[z + 1] = u0[z] + blocks_in(e0, z)[:span0]
        return c

    loop(depth, first0, 15)
    sweep(f0, f0n, wb0, al0, be0, depth)
    sweep(f0n, f0, wb0, al0, be0, depth)

    copies = []

    def ship(src, dst, first, n):
        copy = pltpu.make_async_copy(src.at[pl.ds(first, n)], dst.at[pl.ds(first, n)], sems.at[len(copies)])
        copy.start()
        copies.append(copy)

    for z in range(depth):
        pot[z] = f0[z + 1, above : above + rows, 0:cols]
    ship(pot, potential, 0, depth)
    chunk = depth // 4
    for z in range(depth):
        b = ext[z, HX - above : HX - above + span0, :]
        r = residual_of(f0, z, b, k0[0, :, 0:cols], k0[1, :, 0:cols], 1.0, cols)
        res[z] = r[above : above + rows]
        if z % chunk == chunk - 1:
            ship(res, residual, z + 1 - chunk, chunk)
    for copy in copies:
        copy.wait()


VM = pl.BlockSpec(memory_space=pltpu.VMEM)


def call(kernel, outs, scratch, *args, aliases={}):
    f32 = lambda shape: jax.ShapeDtypeStruct(shape, jnp.float32)
    return pl.pallas_call(
        kernel,
        out_shape=[f32(s) for s in outs],
        in_specs=[VM] * len(args),
        out_specs=[VM] * len(outs),
        scratch_shapes=[pltpu.VMEM(s, jnp.float32) for s in scratch],
        input_output_aliases=aliases,
        compiler_params=pltpu.CompilerParams(vmem_limit_bytes=24 << 20),
    )(*args)


def body(right_side, horiz_coef, vert_coef, panel_owner, panel_cell, panel_pressure):
    depth, rows, cols = right_side.shape
    tiles = lax.axis_size("tile")
    y_axes = ("strip", "sub")
    y_count = lax.axis_size("strip") * lax.axis_size("sub")
    count = depth + 2
    span = rows + 2 * HX
    wide1, wide2, inner2, edge1, edge2 = lane_maps(cols)
    mean = lambda lanes, width: jnp.asarray(0.25 * selection(lanes, width), jnp.bfloat16)
    spread = lambda lanes, width: jnp.asarray(selection(lanes, width).T, jnp.bfloat16)
    c1_inner, c2_inner = mean(wide1[:cols], cols // 2), mean(inner2, cols // 2)
    c1_edge, c2_edge = mean(edge1, 128), mean(edge2, cols // 2)
    p1, p2 = spread(wide1, cols), spread(wide2, cols // 2)

    message = (count + count // 2, 8, cols)
    f32 = lambda shape: jax.ShapeDtypeStruct(shape, jnp.float32)
    early = (count // SLABS, rows, 128)
    x_own, panels, a, b = pl.pallas_call(
        load_kernel,
        out_shape=[f32((count, rows, cols)), f32((1, 8, 128)), f32(message), f32(message)],
        in_specs=[pl.BlockSpec(memory_space=pltpu.HBM)] * 6,
        out_specs=[VM] * 4,
        scratch_shapes=[pltpu.VMEM((2, 4, 128), jnp.int32), pltpu.SemaphoreType.DMA((6,))],
        compiler_params=pltpu.CompilerParams(vmem_limit_bytes=8 << 20),
    )(
        *[
            pltpu.with_memory_space_constraint(x, pltpu.HBM)
            for x in (
                right_side, horiz_coef, vert_coef,
                panel_owner.reshape(4, -1), panel_cell.reshape(4, -1), panel_pressure.reshape(4, -1),
            )
        ]
    )
    near = lax.ppermute(panels, "tile", [(i, i ^ 1) for i in range(tiles)])
    a = neighbour_swap(a, "tile", 0, "sub")
    b = neighbour_swap(b, "tile", 1, "sub")
    ext, sub_own, strip_own = call(own_columns_kernel, [(count, span, cols), early, early], [], x_own)
    sub_own = neighbour_swap(sub_own, y_axes, 0, "group")
    strip_own = neighbour_swap(strip_own, y_axes, 1, "group")
    panels = jnp.concatenate([panels, near], 0)
    step = 2
    while step < tiles:
        swap = [(i, i ^ step) for i in range(tiles)]
        panels = jnp.concatenate([panels, lax.ppermute(panels, "tile", swap)], 0)
        step *= 2

    slabs = (count // SLABS + 1, 2 * HX, 128)
    ext, sub, strip = call(
        forcing_kernel, [(count, span, cols), slabs, slabs], [],
        ext, a, b, panels,
        aliases={0: 0},
    )
    sub = neighbour_swap(sub, y_axes, 0, "group")
    strip = neighbour_swap(strip, y_axes, 1, "group")

    lanes, half = cols + 128, cols // 2
    small = span - 16
    span1 = (span + 8) // 2
    span2 = span1 // 2

    def down_scratch(width, width1, fields=2):
        return (
            [(2, span, width)] * 3 + [(depth + 2, span, width)] * fields + [(count, width // 128, span + 8, 128)]
            + [(2, span1, width1)] * 3 + [(depth + 2, span1, width1)] * fields + [(count, width1 // 128, span1, 128)]
        )

    u_in, b1_in, u1_in, c_in = call(
        inner_kernel,
        [(depth, small, cols), (count, span1, half), (depth, span1, half), (count, span2, half)],
        down_scratch(cols, half),
        ext, c1_inner, c2_inner,
    )
    (base,) = call(base_kernel, [(count, span, 128)], [], ext, sub_own, strip_own)
    message2 = (count + (count + 7) // 8, 8, half)
    edge, u_edge, b1_edge, u1_edge, c_own, a2, b2 = call(
        edge_kernel,
        [
            (count, span, 128), (depth + 2, span, 128), (count, span1, 128), (depth + 2, span1, 128),
            (count, span2, half), message2, message2,
        ],
        down_scratch(128, 128, 1),
        base, sub, strip, c_in, c1_edge, c2_edge,
        aliases={0: 0},
    )
    a2 = neighbour_swap(a2, "tile", 0, "sub")
    b2 = neighbour_swap(b2, "tile", 1, "sub")

    pair0, field = (2, small, lanes), (depth, small, lanes)
    pair1, field1 = (2, span1, cols), (depth, span1, cols)
    state = call(
        join_kernel,
        [pair0, field, field, pair0, pair0, field1, field1, pair1, pair1],
        [pair0, pair1],
        ext, edge, u_in, u_edge, b1_in, b1_edge, u1_in, u1_edge,
    )

    wide2 = 32
    field2 = (depth + 2, wide2, half)
    own = right_side.shape
    potential, residual = pl.pallas_call(
        up_kernel,
        out_shape=[f32(own), f32(own)],
        in_specs=[VM] * (6 + len(state)),
        out_specs=[pl.BlockSpec(memory_space=pltpu.HBM)] * 2,
        scratch_shapes=[
            pltpu.VMEM(shape, jnp.float32)
            for shape in (
                (count, wide2, half), (2, wide2, half), (2, wide2, half), (2, wide2, half), (depth, wide2, half),
                field2, field2, (depth + 2, span1, cols), (depth + 2, span1, cols),
                (depth + 2, small, lanes), (depth + 2, small, lanes),
                (depth, cols // 128, span1, 128), (depth, lanes // 128, small + 8, 128), own, own,
            )
        ]
        + [pltpu.SemaphoreType.DMA((5,))],
        compiler_params=pltpu.CompilerParams(vmem_limit_bytes=24 << 20),
    )(c_own, a2, b2, ext, *state, p1, p2)
    return potential, residual


def solution(mesh):
    return jax.shard_map(
        body,
        mesh=mesh,
        in_specs=(
            jax.P("group", "tile", ("strip", "sub")),
            jax.P(("group", "tile"), ("strip", "sub")),
            jax.P(("group", "tile"), ("strip", "sub")),
            jax.P(("group", "tile", "strip", "sub"), None),
            jax.P(("group", "tile", "strip", "sub")),
            jax.P(("group", "tile", "strip", "sub")),
        ),
        out_specs=(
            jax.P("group", "tile", ("strip", "sub")),
            jax.P("group", "tile", ("strip", "sub")),
        ),
        check_vma=False,
    )
```
